32 devices in a mesh: gx: 8 (over z, core), gy: 4 (over y, x).
Axes of the slice: x: 2, y: 2, z: 4, core: 2. Of those that a mesh axis runs over, the one named last changes fastest.
Arguments:
- adjoint: float32 [3, 64, 32, 128], P(None, 'gx', 'gy'), may hold values from -6 to 6
- jacobian: bfloat16 [63, 64, 32, 128], P(None, 'gx', 'gy'), may hold values from -2.390625 to 2.390625
- active: int32 [64, 32, 128], P('gx', 'gy'), may hold values 0 or 1
- trans_x: float32 [64, 32, 128], P('gx', 'gy'), may hold values from 0.3 to 3
- trans_y: float32 [64, 32, 128], P('gx', 'gy'), may hold values from 0.3 to 3
- trans_z: float32 [64, 32, 128], P('gx', 'gy'), may hold values from 0.3 to 3
- pressure_diag: float32 [64, 32, 128], P('gx', 'gy'), may hold values from 0.05 to 0.5
- weights: float32 [3, 64, 32, 128], P(None, 'gx', 'gy'), may hold values from 0.3 to 3
- perf_cell: int32 [4096], P(('gx', 'gy')), may hold values from 0 to 8191
- perf_well: int32 [4096], P(('gx', 'gy')), may hold values from 0 to 31
- perf_seg: int32 [4096], P(('gx', 'gy')), may hold values from 0 to 15
- perf_in: float32 [3, 4096], P(None, ('gx', 'gy')), may hold values from -6 to 6
- perf_out: float32 [3, 4096], P(None, ('gx', 'gy')), may hold values from -6 to 6
- well_owner: int32 [4, 32], P('gy'), may hold values from 0 to 31, each once within a row
- well_rhs: float32 [16, 4, 32], P(None, 'gy', 'gx'), may hold values from -6 to 6
- seg_diag: float32 [16, 4, 32], P(None, 'gy', 'gx'), may hold values from 1.5 to 3
- seg_off: float32 [16, 4, 32], P(None, 'gy', 'gx'), may hold values from -1 to 1
- seg_parent: int32 [16, 4, 32], P(None, 'gy', 'gx'), may hold values from 0 to 14, as said below
Outputs:
- update: float32 [3, 64, 32, 128], P(None, 'gx', 'gy')
- well_adjoint: float32 [16, 4, 32], P(None, 'gy', 'gx')
The draws below stay inside these ranges and needn't reach their ends.
Inputs may be any that keep to these rules, and one draw needn't show every extreme that they name: seg_parent[s] is below s for every segment s of 1 or more, and 0 for segment 0.
All inputs are finite; a program needn't handle non-finite values. No bound on the sum of `active` on one device may be relied on, other than what follows from the above.
Results may differ from the reference program's by a relative error of at most 0.0003.
Values may be sent and summed in bfloat16 or wider, within the bound.
A program may use at most 64 MiB of HBM per device.

```python
import math
import jax
import jax.numpy as jnp
import numpy as np
from jax import lax

CX = 8
CY = 8
NZ = 128
PD = 128
NS = 16
ITERS = 4
NX = 64
NY = 32
WR = 32
N_GX = 8
N_GY = 4


def draw_seg_parent(key, part):
    levels = jnp.arange(NS, dtype=jnp.int32).reshape(NS, 1, 1)
    upper = jnp.maximum(levels, 1)
    return jax.random.randint(key, (NS, N_GY, WR), 0, upper).astype(jnp.int32)


def set_ends(values, own_key, smallest, high):
    longest = values.shape.index(max(values.shape))
    spots = []
    for shift in (0, 1):
        where = [jax.random.randint(jax.random.fold_in(own_key, axis), (), 0, length) for axis, length in enumerate(values.shape)]
        where[longest] = (where[longest] + shift) % values.shape[longest]
        spots.append(tuple(where))
    return values.at[spots[0]].set(smallest).at[spots[1]].set(high)


def steps_of(key, extent, split, smallest, top_value):
    def one(axis_at, blocks):
        heights = jax.random.uniform(jax.random.fold_in(jax.random.fold_in(key, 6), axis_at), (blocks,), jnp.float32, smallest / len(split), top_value / len(split))
        return jnp.repeat(jnp.exp(heights), extent[axis_at] // blocks).reshape((-1,) + (1,) * (len(extent) - axis_at - 1))

    loudness = one(*split[0])
    for cut in split[1:]:
        loudness = loudness * one(*cut)
    return loudness


def rank_table(number_of, skew):
    weights = [(1 << 20) // math.isqrt(rank ** skew) + 1 for rank in range(1, number_of + 1)]
    spread = 1 + sum(weights) // (1 << 30)
    return np.cumsum(np.array([max(1, weight // spread) for weight in weights]))


def ranked_ids(rng, dims, number_of, skew):
    grid = rank_table(number_of, skew)
    lot = jax.random.randint(jax.random.fold_in(rng, 1), dims, 0, int(grid[number_of - 1]))
    rank = jnp.searchsorted(jnp.asarray(grid, jnp.int32), lot, side="right")
    return jax.random.permutation(jax.random.fold_in(rng, 2), number_of)[rank].astype(jnp.int32)


def normal_values(stream_key, dims, deviation, reach, pieces=(), held_as=jnp.bfloat16):
    entries = jax.random.normal(stream_key, dims, jnp.float32) * deviation
    if len(pieces) > 0:
        entries = steps_of(stream_key, dims, pieces, -0.22, 0.18) * entries
    return jnp.clip(entries, min=-reach, max=reach).astype(held_as)


def setup_inputs(seed: int = 0) -> dict:
    key_of = jax.random.split(jax.random.key(seed), 19)
    adjoint = normal_values(key_of[0], (3, NX, NY, NZ), 1.0, 6.0, ((1, 8), (2, 4)), jnp.float32)
    jacobian = normal_values(key_of[1], (63, NX, NY, NZ), 0.4, 2.390625, ((1, 8), (2, 4)))
    active = set_ends((jax.random.randint(key_of[2], (NX, NY, NZ), 0, 10) < 9).astype(jnp.int32), jax.random.fold_in(key_of[2], 1), 0, 1)
    trans_x = jnp.clip(jnp.exp(math.log(3.0) - 2.3025851 * jax.random.uniform(key_of[3], (NX, NY, NZ), jnp.float32) ** steps_of(key_of[3], (NX, NY, NZ), ((0, 8), (1, 4)), -0.2, 0.2)), 0.3, 3.0)
    trans_y = jnp.clip(jnp.exp(math.log(3.0) - 2.3025851 * jax.random.uniform(key_of[4], (NX, NY, NZ), jnp.float32) ** steps_of(key_of[4], (NX, NY, NZ), ((0, 8), (1, 4)), -0.2, 0.2)), 0.3, 3.0)
    trans_z = jnp.clip(jnp.exp(math.log(3.0) - 2.3025851 * jax.random.uniform(key_of[5], (NX, NY, NZ), jnp.float32) ** steps_of(key_of[5], (NX, NY, NZ), ((0, 8), (1, 4)), -0.2, 0.2)), 0.3, 3.0)
    pressure_diag = jnp.clip(jnp.exp(math.log(0.5) - 2.3025851 * jax.random.uniform(key_of[6], (NX, NY, NZ), jnp.float32) ** steps_of(key_of[6], (NX, NY, NZ), ((0, 8), (1, 4)), -0.2, 0.2)), 0.05, 0.5)
    weights = jnp.clip(jnp.exp(math.log(3.0) - 2.3025851 * jax.random.uniform(key_of[7], (3, NX, NY, NZ), jnp.float32) ** steps_of(key_of[7], (3, NX, NY, NZ), ((1, 8), (2, 4)), -0.2, 0.2)), 0.3, 3.0)
    perf_cell = set_ends(jax.random.randint(key_of[8], (N_GX * N_GY * PD,), 0, CX * CY * NZ), jax.random.fold_in(key_of[8], 1), 0, (CX * CY * NZ) - 1).astype(jnp.int32)
    perf_well = set_ends(ranked_ids(key_of[9], (N_GX * N_GY * PD,), WR, 2), jax.random.fold_in(key_of[9], 3), 0, WR - 1).astype(jnp.int32)
    perf_seg = set_ends(jax.random.randint(key_of[10], (N_GX * N_GY * PD,), 0, NS), jax.random.fold_in(key_of[10], 1), 0, NS - 1).astype(jnp.int32)
    perf_in = normal_values(key_of[11], (3, N_GX * N_GY * PD), 1.0, 6.0, ((1, 32),), jnp.float32)
    perf_out = normal_values(key_of[12], (3, N_GX * N_GY * PD), 1.0, 6.0, ((1, 32),), jnp.float32)
    well_owner = jax.vmap(lambda own: jax.random.permutation(own, WR))(jax.random.split(key_of[13], N_GY)).reshape((N_GY, WR)).astype(jnp.int32)
    well_rhs = normal_values(key_of[14], (NS, N_GY, WR), 1.0, 6.0, ((1, 4), (2, 8)), jnp.float32)
    seg_diag = jnp.clip(1.5 + 1.5 * jax.random.uniform(key_of[15], (NS, N_GY, WR), jnp.float32) ** steps_of(key_of[15], (NS, N_GY, WR), ((1, 4), (2, 8)), -0.2, 0.2), 1.5, 3.0)
    seg_off = jnp.clip(jax.random.uniform(key_of[16], (NS, N_GY, WR), jnp.float32, -1.0, 1.0) * steps_of(key_of[16], (NS, N_GY, WR), ((1, 4), (2, 8)), -0.4, 0.0), -1.0, 1.0)
    seg_parent = draw_seg_parent(jax.random.fold_in(key_of[18], 71), 0)
    return {"adjoint": adjoint, "jacobian": jacobian, "active": active, "trans_x": trans_x, "trans_y": trans_y, "trans_z": trans_z, "pressure_diag": pressure_diag, "weights": weights, "perf_cell": perf_cell, "perf_well": perf_well, "perf_seg": perf_seg, "perf_in": perf_in, "perf_out": perf_out, "well_owner": well_owner, "well_rhs": well_rhs, "seg_diag": seg_diag, "seg_off": seg_off, "seg_parent": seg_parent}


def shifted(values, axis_no, offset):
    widths = [(0, 0)] * values.ndim
    length = values.shape[axis_no]
    if offset > 0:
        widths[axis_no] = (1, 0)
        padded = jnp.pad(values, widths)
        return lax.slice_in_dim(padded, 0, length, axis=axis_no)
    widths[axis_no] = (0, 1)
    padded = jnp.pad(values, widths)
    return lax.slice_in_dim(padded, 1, length + 1, axis=axis_no)


def transposed_block(blocks, vector):
    mats = blocks.astype(jnp.float32).reshape((3, 3) + blocks.shape[1:])
    return mats[0] * vector[0] + mats[1] * vector[1] + mats[2] * vector[2]


def solve_segments(seg_load, seg_diag, seg_off, seg_parent):
    count = seg_load.shape[0]
    levels = jnp.arange(count, dtype=jnp.int32).reshape((count,) + (1,) * (seg_load.ndim - 1))
    answers = [None] * count
    for seg_no in range(count - 1, 0, -1):
        value = seg_load[seg_no] / seg_diag[seg_no]
        answers[seg_no] = value
        hit = (levels == seg_parent[seg_no][None]).astype(jnp.float32)
        seg_load = seg_load + (seg_off[seg_no] * value)[None] * hit
    answers[0] = seg_load[0] / seg_diag[0]
    return jnp.stack(answers)


def reference(adjoint, jacobian, active, trans_x, trans_y, trans_z, pressure_diag, weights, perf_cell, perf_well, perf_seg, perf_in, perf_out, well_owner, well_rhs, seg_diag, seg_off, seg_parent):
    prods = [transposed_block(jacobian[9 * block_no:9 * block_no + 9], adjoint) for block_no in range(7)]
    cell_res = prods[0] + shifted(prods[1], 1, 1) + shifted(prods[2], 1, -1)
    cell_res = cell_res + shifted(prods[3], 2, 1) + shifted(prods[4], 2, -1)
    cell_res = cell_res + shifted(prods[5], 3, 1) + shifted(prods[6], 3, -1)
    total_perf = N_GX * N_GY * PD
    device_of = jnp.arange(total_perf, dtype=jnp.int32) // PD
    col_dev = device_of // N_GY
    row_dev = device_of % N_GY
    cell_x = perf_cell // (CY * NZ)
    cell_y = (perf_cell // NZ) % CY
    cell_z = perf_cell % NZ
    glob_x = col_dev * CX + cell_x
    glob_y = row_dev * CY + cell_y
    picked = adjoint[:, glob_x, glob_y, cell_z]
    perf_flux = jnp.sum(perf_in * picked, axis=0)
    position = well_owner[row_dev, perf_well]
    summed = jnp.zeros((NS, N_GY, WR), jnp.float32).at[perf_seg, row_dev, position].add(perf_flux)
    seg_load = summed + well_rhs
    well_adjoint = solve_segments(seg_load, seg_diag, seg_off, seg_parent)
    well_vals = well_adjoint[perf_seg, row_dev, position]
    cell_res = cell_res.at[:, glob_x, glob_y, cell_z].add(perf_out * well_vals[None])
    residual = cell_res * active.astype(jnp.float32)[None]
    rhs = weights[0] * residual[0] + weights[1] * residual[1] + weights[2] * residual[2]
    trans_xm = shifted(trans_x, 0, 1)
    trans_ym = shifted(trans_y, 1, 1)
    trans_zm = shifted(trans_z, 2, 1)
    diag_sum = pressure_diag + trans_x + trans_xm + trans_y + trans_ym + trans_z + trans_zm

    def operate(field):
        result = diag_sum * field - trans_x * shifted(field, 0, -1) - trans_xm * shifted(field, 0, 1)
        result = result - trans_y * shifted(field, 1, -1) - trans_ym * shifted(field, 1, 1)
        return result - trans_z * shifted(field, 2, -1) - trans_zm * shifted(field, 2, 1)

    pressure = jnp.zeros_like(rhs)
    cg_res = rhs
    direction = rhs
    norm_now = jnp.sum(cg_res * cg_res)
    for iteration in range(ITERS):
        image = operate(direction)
        alpha = norm_now / jnp.sum(direction * image)
        pressure = pressure + alpha * direction
        cg_res = cg_res - alpha * image
        norm_next = jnp.sum(cg_res * cg_res)
        direction = cg_res + (norm_next / norm_now) * direction
        norm_now = norm_next
    update = residual + weights * pressure[None]
    return update, well_adjoint
```

```python
import functools
import math

import jax
import jax.numpy as jnp
from jax import lax
from jax.experimental import pallas as pl
from jax.experimental.pallas import tpu as pltpu
from jax.sharding import PartitionSpec as P

ITERS = 4
MESH = pl.DeviceIdType.MESH
HIGH = lax.Precision.HIGHEST
PAIRS = [(i, j) for i in range(ITERS) for j in range(i, ITERS + 1)]


def iota(shape, dim):
    return lax.broadcasted_iota(jnp.int32, shape, dim)


def dot(a, b, dims, precision=HIGH):
    return lax.dot_general(
        a, b, (dims, ((), ())), precision=precision, preferred_element_type=jnp.float32
    )


def dot_exact(a, pick, dims):
    high = a.astype(jnp.bfloat16)
    rest = a - high.astype(jnp.float32)
    mid = rest.astype(jnp.bfloat16)
    low = (rest - mid.astype(jnp.float32)).astype(jnp.bfloat16)
    parts = [dot(part, pick, dims, None) for part in (high, mid, low)]
    return parts[0] + (parts[1] + parts[2])


def tree(values):
    values = list(values)
    while len(values) > 1:
        pairs = [a + b for a, b in zip(values[::2], values[1::2])]
        values = pairs + values[len(pairs) * 2 :]
    return values[0]


def krylov_coefficients(gram, shift):
    size = ITERS + 1

    def apply(v):
        out = [None] * size

        def put(k, value):
            out[k] = value if out[k] is None else out[k] + value

        for k, value in enumerate(v):
            if value is None:
                continue
            scaled = value * shift
            put(k, scaled)
            if k == 0:
                put(1, scaled)
            else:
                put(k + 1, scaled * 0.5)
                put(k - 1, scaled * 0.5)
        return out

    def inner(a, b):
        total = []
        for j in range(size):
            if b[j] is None:
                continue
            part = [a[i] * gram(i, j) for i in range(size) if a[i] is not None]
            total.append(tree(part) * b[j])
        return tree(total)

    def axpy(a, scale, b):
        out = []
        for p, q in zip(a, b):
            if q is None:
                out.append(p)
            else:
                out.append(scale * q if p is None else p + scale * q)
        return out

    one = jnp.ones_like(shift)
    residual = [one] + [None] * ITERS
    direction = list(residual)
    answer = [None] * size
    norm = gram(0, 0)
    for iteration in range(ITERS):
        image = apply(direction)
        bottom = inner(direction, image)
        alpha = jnp.where(bottom > 0, norm / bottom, 0.0)
        answer = axpy(answer, alpha, direction)
        if iteration == ITERS - 1:
            break
        residual = axpy(residual, -alpha, image)
        new = inner(residual, residual)
        beta = jnp.where(norm > 0, new / norm, 0.0)
        direction = axpy(residual, beta, direction)
        norm = new
    return answer[:ITERS]


DEPTH = ITERS
SENDS = [(1, 0), (-1, 0), (0, 1), (0, -1), (1, 1), (-1, 1), (1, -1), (-1, -1)]
FACES = [(1, 0), (-1, 0), (0, 1), (0, -1)]
HELD = 16


def kernel(n_x, n_y, *refs):
    inputs, (upd, wout) = refs[:18], refs[18:20]
    held, scratch = refs[20 : 20 + HELD], refs[20 + HELD :]
    adj, jac, active, weights, pcell, pwell, pseg, pin, pout, owner = held[:10]
    wrhs, sdiag, soff, spar, ext, pext = held[10:]
    (cres, coef, ctab, ctabg, ftab, gtab, gtabg, cpack, crecv, ppack, precv) = scratch[:11]
    ustage, uhalo, ruler, in_sem, sent_sem, got_sem = scratch[11:]
    c_sem, cg_sem, f_sem, g_sem, gg_sem, t_sem, u_sem, v_sem = [got_sem.at[i] for i in range(8)]

    ix = lax.axis_index("gx")
    iy = lax.axis_index("gy")
    size_x, size_y, size_z = adj.shape[1:]
    planes = range(size_x)
    wide_x = size_x + 2 * DEPTH
    own = slice(DEPTH, DEPTH + size_x)
    half = size_y // 2
    tiles = size_x // 2
    edge = DEPTH // 2
    perfs = pcell.shape[1]
    slots, segs = wrhs.shape
    wells = owner.shape[1]
    wide = -(-wells // 128) * 128
    columns = size_x * size_y

    places = [
        adj, jac, active, ext.at[1, own], ext.at[2, own], ext.at[3, own], ext.at[0, own],
        weights, pcell, pwell, pseg, pin, pout, owner, wrhs, sdiag, soff, spar,
    ]
    loads_in = [
        pltpu.make_async_copy(src, dst, in_sem.at[i])
        for i, (src, dst) in enumerate(zip(inputs, places))
    ]
    for i in (8, 9, 10, 11, 13, 0, 14, 15, 16, 17, 3, 4, 5, 6, 1, 12, 2, 7):
        loads_in[i].start()

    def exists(sx, sy):
        fine = None
        for step, at, count in ((sx, ix, n_x), (sy, iy, n_y)):
            if step:
                one = at < count - 1 if step > 0 else at > 0
                fine = one if fine is None else jnp.logical_and(fine, one)
        return fine

    barrier = pltpu.get_barrier_semaphore()
    everyone = n_x * n_y
    direct = gtab.shape[0] == everyone
    flat = ix * n_y + iy
    if direct:
        for off in range(1, everyone):
            peer = lax.rem(flat + off, everyone)
            pl.semaphore_signal(
                barrier,
                inc=1,
                device_id=(lax.div(peer, n_y), lax.rem(peer, n_y)),
                device_id_type=MESH,
            )
    else:
        for off in range(1, n_x):
            pl.semaphore_signal(
                barrier, inc=1, device_id=(lax.rem(ix + off, n_x), iy), device_id_type=MESH
            )
        for off in range(1, n_y):
            pl.semaphore_signal(
                barrier, inc=1, device_id=(ix, lax.rem(iy + off, n_y)), device_id_type=MESH
            )
        for sx, sy in SENDS[4:]:

            @pl.when(exists(sx, sy))
            def _(sx=sx, sy=sy):
                pl.semaphore_signal(barrier, inc=1, device_id=(ix + sx, iy + sy), device_id_type=MESH)

    def spot(sx, sy):
        if sy == 0:
            if sx > 0:
                return slice(size_x, size_x + DEPTH), slice(0, DEPTH)
            return slice(DEPTH, 2 * DEPTH), slice(DEPTH + size_x, wide_x)
        if sx == 0:
            return slice(0, tiles), slice(edge, edge + tiles)
        if sx > 0:
            return slice(tiles - edge, tiles), slice(0, edge)
        return slice(0, edge), slice(edge + tiles, tiles + 2 * edge)

    def halo_refs(sx, sy, coefs):
        src, dst = spot(sx, sy)
        if sy == 0:
            if coefs:
                return ext.at[:, src], ext.at[:, dst]
            return pext.at[0, 0, src], pext.at[0, 0, dst]
        side = 0 if sy > 0 else 1
        if coefs:
            return cpack.at[side, :, src], crecv.at[side, :, dst]
        return ppack.at[side, src], precv.at[side, dst]

    for d, (sx, sy) in enumerate(SENDS):

        @pl.when(jnp.logical_not(exists(-sx, -sy)))
        def _(d=d, sx=sx, sy=sy):
            for coefs in (True, False):
                ref = halo_refs(sx, sy, coefs)[1]
                ref[...] = jnp.zeros(ref.shape, jnp.float32)
            if d < 4:
                uhalo[d] = jnp.zeros(uhalo.shape[1:], jnp.float32)

    def message(sx, sy, src, dst, rsem):
        def copy():
            return pltpu.make_async_remote_copy(
                src_ref=src,
                dst_ref=dst,
                send_sem=sent_sem.at[0],
                recv_sem=rsem,
                device_id=(ix + sx, iy + sy),
                device_id_type=MESH,
            )

        def start():
            @pl.when(exists(sx, sy))
            def _():
                copy().start()

        return start

    sides_x = (ix > 0).astype(jnp.int32) + (ix < n_x - 1).astype(jnp.int32)
    sides_y = (iy > 0).astype(jnp.int32) + (iy < n_y - 1).astype(jnp.int32)

    def rows_of(ref):
        return math.prod(ref.shape) // 128

    def wait_rows(count, sem):
        part = ruler.at[pl.ds(0, count)]
        pltpu.make_async_copy(part, part, sem).wait()

    def wait_sides(refs, sem):
        along_x, along_y = rows_of(refs[0]), rows_of(refs[2])
        corner = rows_of(refs[4]) if len(refs) > 4 else 0
        for a in (1, 2):
            for b in (1, 2):

                @pl.when(jnp.logical_and(sides_x == a, sides_y == b))
                def _(count=a * along_x + b * along_y + a * b * corner):
                    wait_rows(count, sem)

    def gather(table, rsem, axis):
        me, count = ((ix, n_x), (iy, n_y), (flat, everyone))[axis]

        def copy(off):
            peer = lax.rem(me + off, count)
            return pltpu.make_async_remote_copy(
                src_ref=table.at[me],
                dst_ref=table.at[me],
                send_sem=sent_sem.at[0],
                recv_sem=rsem,
                device_id=(
                    (peer, iy),
                    (ix, peer),
                    (lax.div(peer, n_y), lax.rem(peer, n_y)),
                )[axis],
                device_id_type=MESH,
            )

        def start():
            for off in range(1, count):
                copy(off).start()

        def wait():
            wait_rows((count - 1) * rows_of(table.at[0]), rsem)

        return start, wait

    t_refs = [halo_refs(sx, sy, True)[1] for sx, sy in SENDS]
    v_refs = [halo_refs(sx, sy, False)[1] for sx, sy in SENDS]
    u_refs = [uhalo.at[d] for d in range(4)]
    c_ops = gather(ctab, c_sem, 0)
    cg_ops = gather(ctabg, cg_sem, 1)
    f_ops = gather(ftab, f_sem, 0)
    g_ops = gather(gtab, g_sem, 2 if direct else 0)
    gg_ops = gather(gtabg, gg_sem, 1)
    t_ops = [
        message(sx, sy, *halo_refs(sx, sy, True), t_sem)
        for d, (sx, sy) in enumerate(SENDS)
    ]
    v_ops = [
        message(sx, sy, *halo_refs(sx, sy, False), v_sem)
        for d, (sx, sy) in enumerate(SENDS)
    ]
    u_ops = [
        message(sx, sy, ustage.at[d], uhalo.at[d], u_sem)
        for d, (sx, sy) in enumerate(FACES)
    ]
    rows = iota((size_y, size_z), 0)
    lanes = iota((size_y, size_z), 1)
    low = rows < half

    for i in (8, 9, 10, 11, 13, 0, 14):
        loads_in[i].wait()
    cell = pcell[...]
    cell_col = lax.shift_right_logical(cell, size_z.bit_length() - 1)
    cell_z = cell & (size_z - 1)
    one_z = (iota((size_z, perfs), 0) == cell_z).astype(jnp.bfloat16)
    one_col = (iota((columns, perfs), 0) == cell_col).astype(jnp.float32)
    one_seg = (iota((segs, perfs), 0) == pseg[...]).astype(jnp.float32)
    one_well = (iota((wells, perfs), 0) == pwell[...]).astype(jnp.bfloat16)
    moves = (iota((wide, wells), 0) == owner[...]).astype(jnp.bfloat16)
    one_slot = dot(moves, one_well, ((1,), (0,)), None).astype(jnp.bfloat16)
    picked = dot_exact(adj[...].reshape(3 * columns, size_z), one_z, ((1,), (0,)))
    flux = None
    for m in range(3):
        part = jnp.sum(picked[m * columns : (m + 1) * columns] * one_col, axis=0, keepdims=True)
        part = part * pin[m : m + 1, :]
        flux = part if flux is None else flux + part
    loads = dot_exact(one_seg * flux, one_slot, ((1,), (1,)))
    slot_no = iota((slots, wide), 0) + ix * slots
    mine = (iota((slots, wide), 1) == slot_no).astype(jnp.float32)
    loads = loads + dot(wrhs[...], mine, ((0,), (0,)))
    folded = ftab.shape[1] < segs
    if folded:
        loads = loads[: segs // 2] + pltpu.roll(loads[segs // 2 :], 64, 1)
    ftab[ix] = loads

    for i in (15, 16, 17, 3, 4, 5, 6):
        loads_in[i].wait()
    packed = ctab.shape[2]
    lane_no = iota((slots, packed), 1)
    first = iota((slots, packed), 0) + ix * slots
    table = None
    for no, ref in enumerate((sdiag, soff, spar)):
        here = (lane_no == first + no * wells).astype(jnp.float32)
        part = dot(ref[...].astype(jnp.float32), here, ((0,), (0,)))
        table = part if table is None else table + part
    share = tree(
        ext[0, x + DEPTH] + 2.0 * (ext[1, x + DEPTH] + ext[2, x + DEPTH] + ext[3, x + DEPTH])
        for x in planes
    )
    share = jnp.sum(jnp.sum(share, axis=0, keepdims=True), axis=1, keepdims=True)
    table = jnp.where(iota((segs, packed), 1) == 3 * wells, share, table)
    ctab[ix] = table

    def pack(read, write):
        for i in range(tiles):
            even, odd = read(2 * i), read(2 * i + 1)
            write(0, i, jnp.where(low, pltpu.roll(even, half, 0), odd))
            write(1, i, jnp.where(low, even, pltpu.roll(odd, half, 0)))

    def unpack(north, south):
        north_r, south_r = pltpu.roll(north, half, 0), pltpu.roll(south, half, 0)
        return jnp.where(low, north, south_r), jnp.where(low, north_r, south)

    if direct:
        pl.semaphore_wait(barrier, everyone - 1)
    else:
        diagonals = [exists(sx, sy).astype(jnp.int32) for sx, sy in SENDS[4:]]
        pl.semaphore_wait(barrier, n_x - 1 + n_y - 1 + sum(diagonals[1:], diagonals[0]))
    f_ops[0]()
    c_ops[0]()

    loads_in[1].wait()

    def product(k, x):
        vector = [adj[m, x] for m in range(3)]
        return [
            tree(jac[9 * k + 3 * m + n, x].astype(jnp.float32) * vector[m] for m in range(3))
            for n in range(3)
        ]

    for n, value in enumerate(product(1, size_x - 1)):
        ustage[0, n] = value
    u_ops[0]()
    for n, value in enumerate(product(2, 0)):
        ustage[1, n] = value
    u_ops[1]()
    for x in planes:
        for n, value in enumerate(product(3, x)):
            ustage[2, n, x : x + 1, :] = value[size_y - 1 : size_y]
            cres[n, x] = jnp.where(rows == 0, 0.0, pltpu.roll(value, 1, 0))
    u_ops[2]()
    for x in planes:
        for n, value in enumerate(product(4, x)):
            ustage[3, n, x : x + 1, :] = value[0:1]
            cres[n, x] += jnp.where(rows == size_y - 1, 0.0, pltpu.roll(value, size_y - 1, 0))
    u_ops[3]()

    for f in range(4):

        def put(side, i, value, f=f):
            cpack[side, f, i] = value

        pack(lambda x, f=f: ext[f, x + DEPTH], put)
    for op in t_ops:
        op()

    for x in planes:
        groups = [product(0, x)]
        if x > 0:
            groups.append(product(1, x - 1))
        if x < size_x - 1:
            groups.append(product(2, x + 1))
        above = product(5, x)
        groups.append([jnp.where(lanes == 0, 0.0, pltpu.roll(v, 1, 1)) for v in above])
        below = product(6, x)
        groups.append(
            [jnp.where(lanes == size_z - 1, 0.0, pltpu.roll(v, size_z - 1, 1)) for v in below]
        )
        for n in range(3):
            cres[n, x] += tree(group[n] for group in groups)

    c_ops[1]()
    total = tree(ctab[i] for i in range(n_x))
    base = (3 * wells) // 128 * 128
    ctabg[iy] = total[0:1, base : base + 128]
    cg_ops[0]()

    def constant(no):
        if wells % 128 == 0:
            return total[:, no * wells : (no + 1) * wells]
        return total if no == 0 else pltpu.roll(total, 128 - no * wells, 1)

    used = iota((segs, wide), 1) < wells
    diag = jnp.where(used, constant(0), 1.0)
    ratio = jnp.where(used, constant(1), 0.0) / diag
    parent = jnp.where(used, constant(2), 0.0)
    levels = iota((segs, wide), 0).astype(jnp.float32)
    steps = [
        jnp.where(levels == parent[s : s + 1], ratio[s : s + 1], 0.0) for s in range(1, segs)
    ]
    for i in (12, 2, 7):
        loads_in[i].wait()

    f_ops[1]()
    load = tree(ftab[i] for i in range(n_x))
    if folded:
        load = jnp.concatenate([load, pltpu.roll(load, 64, 1)], axis=0)
    for s in range(segs - 1, 0, -1):
        load = load + load[s : s + 1] * steps[s - 1]
    answers = load / diag
    values = dot_exact(answers, one_slot, ((1,), (0,)))
    values = jnp.sum(values * one_seg, axis=0, keepdims=True)
    spread = jnp.concatenate([one_col * (pout[n : n + 1, :] * values) for n in range(3)], axis=0)
    added = dot_exact(spread, one_z, ((1,), (1,)))

    wait_sides(u_refs, u_sem)
    for x in planes:
        live = active[x].astype(jnp.float32)
        rhs = None
        for n in range(3):
            row = n * columns + x * size_y
            value = cres[n, x] + added[row : row + size_y]
            if x == 0:
                value = value + uhalo[0, n]
            if x == size_x - 1:
                value = value + uhalo[1, n]
            value = value + jnp.where(rows == 0, uhalo[2, n, x : x + 1, :], 0.0)
            value = value + jnp.where(rows == size_y - 1, uhalo[3, n, x : x + 1, :], 0.0)
            value = value * live
            upd[n, x] = value
            part = weights[n, x] * value
            rhs = part if rhs is None else rhs + part
        pext[0, 0, x + DEPTH] = rhs

    def put_p(side, i, value):
        ppack[side, i] = value

    pack(lambda x: pext[0, 0, x + DEPTH], put_p)
    for op in v_ops:
        op()

    wout[...] = dot(mine, answers, ((1,), (1,)))
    cg_ops[1]()
    mean = tree(ctabg[i] for i in range(n_y))
    mean = jnp.where(iota((1, 128), 1) == 3 * wells - base, mean, 0.0)
    mean = jnp.sum(mean, axis=1, keepdims=True)
    shift = jnp.broadcast_to(mean * (0.75 / (n_x * n_y * columns * size_z)), (1, size_z))
    inverse = 1.0 / shift
    wait_sides(t_refs, t_sem)
    last_x = (ix == n_x - 1).astype(jnp.int32)
    last_y = (iy == n_y - 1).astype(jnp.int32)
    last_row = rows == jnp.where(last_y == 1, size_y - 1, size_y)
    keep_x = 1.0 - last_x.astype(jnp.float32)

    def following(a, b):
        a, b = pltpu.roll(a, size_y - 1, 0), pltpu.roll(b, size_y - 1, 0)
        return jnp.where(rows == size_y - 1, b, a), jnp.where(rows == size_y - 1, a, b)

    def preceding(a, b):
        a, b = pltpu.roll(a, 1, 0), pltpu.roll(b, 1, 0)
        return jnp.where(rows == 0, b, a), jnp.where(rows == 0, a, b)

    raw_x = None
    for i in range(wide_x // 2):
        both = [unpack(crecv[1, f, i], crecv[0, f, i]) for f in range(4)]
        for odd in range(2):
            j = 2 * i + odd
            parts = [(ext[f, j], both[f][odd]) for f in range(4)]
            south_raw = preceding(*parts[2])
            north = (jnp.where(last_row, 0.0, parts[2][0]), parts[2][1])
            south = preceding(*north)
            for h in range(2):
                here_x = parts[1][h]
                inside = jnp.where(lanes == size_z - 1, 0.0, parts[3][h])
                under = pltpu.roll(inside, 1, 1)
                if j > 0:
                    full = tree(
                        [
                            parts[0][h] + here_x,
                            raw_x[h] + parts[2][h],
                            south_raw[h] + parts[3][h],
                            under,
                        ]
                    )
                    coef[0, h, j] = full * inverse - 1.0
                east = here_x * inverse
                coef[1, h, j] = east * keep_x if j == DEPTH + size_x - 1 else east
                coef[2, h, j] = north[h] * inverse
                coef[3, h, j] = south[h] * inverse
                coef[4, h, j] = inside * inverse
                coef[5, h, j] = under * inverse
            raw_x = (parts[1][0], parts[1][1])

    wait_sides(v_refs, v_sem)
    for i in range(wide_x // 2):
        pair = unpack(precv[1, i], precv[0, i])
        pext[0, 1, 2 * i] = pair[0]
        pext[0, 1, 2 * i + 1] = pair[1]

    for k in range(ITERS):
        final = k == ITERS - 1
        for j in range(k + 1, wide_x - k - 1):
            here = (pext[k, 0, j], pext[k, 1, j])
            up = following(*here)
            down = preceding(*here)
            for h in range(1 if final else 2):
                image = coef[0, h, j] * here[h] - tree(
                    [
                        coef[1, h, j] * pext[k, h, j + 1],
                        coef[1, h, j - 1] * pext[k, h, j - 1],
                        coef[2, h, j] * up[h],
                        coef[3, h, j] * down[h],
                        coef[4, h, j] * pltpu.roll(here[h], size_z - 1, 1),
                        coef[5, h, j] * pltpu.roll(here[h], 1, 1),
                    ]
                )
                pext[k + 1, h, j] = image if k == 0 else 2.0 * image - pext[k - 1, h, j]

    def mine_of(k, x):
        return pext[k, 0, x + DEPTH]

    count = 16
    grams = [
        jnp.sum(tree(mine_of(i, x) * mine_of(j, x) for x in planes), axis=0, keepdims=True)
        for i, j in PAIRS
    ]
    grams += [jnp.zeros((1, size_z), jnp.float32)] * (count - len(PAIRS))
    column = jnp.sum(jnp.concatenate(grams, axis=0), axis=1, keepdims=True)
    on_lane = iota((count, 128), 0) == iota((count, 128), 1)
    entries = jnp.sum(jnp.where(on_lane, column, 0.0), axis=0, keepdims=True)
    gtab[flat if direct else ix] = entries
    g_ops[0]()
    g_ops[1]()
    sums = tree(gtab[i] for i in range(gtab.shape[0]))
    if not direct:
        gtabg[iy] = sums
        gg_ops[0]()
        gg_ops[1]()
        sums = tree(gtabg[i] for i in range(n_y))
    sums = jnp.sum(jnp.where(on_lane, sums, 0.0), axis=1, keepdims=True)
    sums = jnp.broadcast_to(sums, (count, size_z))

    def gram(i, j):
        row = PAIRS.index((min(i, j), max(i, j)))
        return sums[row : row + 1]

    answer = krylov_coefficients(gram, shift)
    for x in planes:
        pressure = tree(answer[k] * mine_of(k, x) for k in range(ITERS))
        for n in range(3):
            upd[n, x] += weights[n, x] * pressure

    sent_rows = sum(
        (count - 1) * rows_of(table.at[0])
        for table, count in (
            (ctab, n_x), (ctabg, n_y), (ftab, n_x), (gtab, gtab.shape[0]), (gtabg, 1 if direct else n_y),
        )
    )
    shapes = [[t, v] + ([u_refs[d]] if d < 4 else []) for d, (t, v) in enumerate(zip(t_refs, v_refs))]
    along_x, along_y, corner = [sum(rows_of(r) for r in shapes[d]) for d in (0, 2, 4)]
    for a in (1, 2):
        for b in (1, 2):

            @pl.when(jnp.logical_and(sides_x == a, sides_y == b))
            def _(count=a * along_x + b * along_y + a * b * corner + sent_rows):
                wait_rows(count, sent_sem.at[0])


def shards(n_x, n_y, *args):
    args = list(args)
    size_x, size_y, size_z = args[0].shape[1:]
    for k in (8, 9, 10):
        args[k] = args[k][None]
    for k in (14, 15, 16, 17):
        args[k] = args[k][:, 0, :].T
    slots, segs = args[14].shape
    wells = args[13].shape[1]
    wide = -(-wells // 128) * 128
    packed = -(-(3 * wells + 1) // 128) * 128
    folded = segs // 2 if wells <= 64 and segs == 16 else segs
    joined = n_x * n_y if n_x * n_y <= 32 else n_x
    plane = (size_y, size_z)
    wide_x = size_x + 2 * DEPTH
    dma = pltpu.SemaphoreType.DMA

    def f32(*shape):
        return pltpu.VMEM(shape, jnp.float32)

    held = [pltpu.VMEM(args[k].shape, args[k].dtype) for k in (0, 1, 2, 7) + tuple(range(8, 18))]
    held += [f32(4, wide_x, *plane), f32(ITERS + 1, 2, wide_x, *plane)]
    tiles = size_x // 2
    along = DEPTH * size_y
    ruler = 2 * (2 * 5 * along + 2 * 3 * size_y) + 4 * 5 * along // 2
    ruler += n_x * segs * (packed + wide) // 128 + 2 * n_y + joined
    scratch = [
        f32(3, size_x, *plane),
        f32(6, 2, wide_x, *plane),
        f32(n_x, segs, packed),
        f32(n_y, 1, 128),
        f32(n_x, folded, wide),
        f32(joined, 1, 128),
        f32(n_y, 1, 128),
        f32(2, 4, tiles, *plane),
        f32(2, 4, wide_x // 2, *plane),
        f32(2, tiles, *plane),
        f32(2, wide_x // 2, *plane),
        f32(4, 3, *plane),
        f32(4, 3, *plane),
        f32(ruler, 1, 128),
        dma((18,)),
        dma((1,)),
        dma((8,)),
    ]
    vmem = pl.BlockSpec(memory_space=pltpu.VMEM)
    update, answers = pl.pallas_call(
        functools.partial(kernel, n_x, n_y),
        out_shape=(
            pltpu.VMEM(args[0].shape, jnp.float32),
            pltpu.VMEM((slots, segs), jnp.float32),
        ),
        in_specs=[pl.BlockSpec(memory_space=pl.ANY)] * 18,
        out_specs=(vmem, vmem),
        scratch_shapes=held + scratch,
        compiler_params=pltpu.CompilerParams(collective_id=0, has_side_effects=True),
    )(*args)
    return update, answers.T[:, None, :]


def solution(mesh):
    body = functools.partial(shards, mesh.shape["gx"], mesh.shape["gy"])
    cells = P("gx", "gy", None)
    stacked = P(None, "gx", "gy", None)
    perf = P(("gx", "gy"))
    perf_3 = P(None, ("gx", "gy"))
    segment = P(None, "gy", "gx")
    return jax.shard_map(
        body,
        mesh=mesh,
        in_specs=(stacked, stacked)
        + (cells,) * 5
        + (stacked,)
        + (perf,) * 3
        + (perf_3,) * 2
        + (P("gy", None),)
        + (segment,) * 4,
        out_specs=(stacked, segment),
        check_vma=False,
    )
```

```python
import functools
import math

import jax
import jax.numpy as jnp
from jax import lax
from jax.experimental import pallas as pl
from jax.experimental.pallas import tpu as pltpu
from jax.sharding import PartitionSpec as P

ITERS = 4
MESH = pl.DeviceIdType.MESH
HIGH = lax.Precision.HIGHEST
PAIRS = [(i, j) for i in range(ITERS) for j in range(i, ITERS + 1)]


def iota(shape, dim):
    return lax.broadcasted_iota(jnp.int32, shape, dim)


def dot(a, b, dims, precision=HIGH):
    return lax.dot_general(
        a, b, (dims, ((), ())), precision=precision, preferred_element_type=jnp.float32
    )


def dot_exact(a, pick, dims):
    high = a.astype(jnp.bfloat16)
    rest = a - high.astype(jnp.float32)
    mid = rest.astype(jnp.bfloat16)
    low = (rest - mid.astype(jnp.float32)).astype(jnp.bfloat16)
    parts = [dot(part, pick, dims, None) for part in (high, mid, low)]
    return parts[0] + (parts[1] + parts[2])


def tree(values):
    values = list(values)
    while len(values) > 1:
        pairs = [a + b for a, b in zip(values[::2], values[1::2])]
        values = pairs + values[len(pairs) * 2 :]
    return values[0]


def krylov_coefficients(gram, shift):
    size = ITERS + 1

    def apply(v):
        out = [None] * size

        def put(k, value):
            out[k] = value if out[k] is None else out[k] + value

        for k, value in enumerate(v):
            if value is None:
                continue
            scaled = value * shift
            put(k, scaled)
            if k == 0:
                put(1, scaled)
            else:
                put(k + 1, scaled * 0.5)
                put(k - 1, scaled * 0.5)
        return out

    def inner(a, b):
        total = []
        for j in range(size):
            if b[j] is None:
                continue
            part = [a[i] * gram(i, j) for i in range(size) if a[i] is not None]
            total.append(tree(part) * b[j])
        return tree(total)

    def axpy(a, scale, b):
        out = []
        for p, q in zip(a, b):
            if q is None:
                out.append(p)
            else:
                out.append(scale * q if p is None else p + scale * q)
        return out

    one = jnp.ones_like(shift)
    residual = [one] + [None] * ITERS
    direction = list(residual)
    answer = [None] * size
    norm = gram(0, 0)
    for iteration in range(ITERS):
        image = apply(direction)
        bottom = inner(direction, image)
        alpha = jnp.where(bottom > 0, norm / bottom, 0.0)
        answer = axpy(answer, alpha, direction)
        if iteration == ITERS - 1:
            break
        residual = axpy(residual, -alpha, image)
        new = inner(residual, residual)
        beta = jnp.where(norm > 0, new / norm, 0.0)
        direction = axpy(residual, beta, direction)
        norm = new
    return answer[:ITERS]


DEPTH = ITERS
SENDS = [(1, 0), (-1, 0), (0, 1), (0, -1), (1, 1), (-1, 1), (1, -1), (-1, -1)]
FACES = [(1, 0), (-1, 0), (0, 1), (0, -1)]
HELD = 16


def kernel(n_x, n_y, *refs):
    inputs, (upd, wout) = refs[:18], refs[18:20]
    held, scratch = refs[20 : 20 + HELD], refs[20 + HELD :]
    adj, jac, active, weights, pcell, pwell, pseg, pin, pout, owner = held[:10]
    wrhs, sdiag, soff, spar, ext, pext = held[10:]
    (cres, coef, ctab, ctabg, ftab, gtab, gtabg, cpack, crecv, ppack, precv) = scratch[:11]
    ustage, uhalo, ruler, in_sem, sent_sem, got_sem = scratch[11:]
    c_sem, cg_sem, f_sem, g_sem, gg_sem, t_sem, u_sem, v_sem = [got_sem.at[i] for i in range(8)]

    ix = lax.axis_index("gx")
    iy = lax.axis_index("gy")
    size_x, size_y, size_z = adj.shape[1:]
    planes = range(size_x)
    wide_x = size_x + 2 * DEPTH
    own = slice(DEPTH, DEPTH + size_x)
    half = size_y // 2
    tiles = size_x // 2
    edge = DEPTH // 2
    perfs = pcell.shape[1]
    slots, segs = wrhs.shape
    wells = owner.shape[1]
    wide = -(-wells // 128) * 128
    columns = size_x * size_y

    places = [
        adj, jac, active, ext.at[1, own], ext.at[2, own], ext.at[3, own], ext.at[0, own],
        weights, pcell, pwell, pseg, pin, pout, owner, wrhs, sdiag, soff, spar,
    ]
    loads_in = [
        pltpu.make_async_copy(src, dst, in_sem.at[i])
        for i, (src, dst) in enumerate(zip(inputs, places))
    ]
    for i in (8, 9, 10, 11, 13, 0, 14, 15, 16, 17, 3, 4, 5, 6, 1, 12, 2, 7):
        loads_in[i].start()

    def exists(sx, sy):
        fine = None
        for step, at, count in ((sx, ix, n_x), (sy, iy, n_y)):
            if step:
                one = at < count - 1 if step > 0 else at > 0
                fine = one if fine is None else jnp.logical_and(fine, one)
        return fine

    barrier = pltpu.get_barrier_semaphore()
    everyone = n_x * n_y
    direct = gtab.shape[0] == everyone
    flat = ix * n_y + iy
    for off in range(1, n_x):
        pl.semaphore_signal(
            barrier, inc=1, device_id=(lax.rem(ix + off, n_x), iy), device_id_type=MESH
        )
    for off in range(1, n_y):
        pl.semaphore_signal(
            barrier, inc=1, device_id=(ix, lax.rem(iy + off, n_y)), device_id_type=MESH
        )
    for sx, sy in SENDS[4:]:

        @pl.when(exists(sx, sy))
        def _(sx=sx, sy=sy):
            pl.semaphore_signal(barrier, inc=1, device_id=(ix + sx, iy + sy), device_id_type=MESH)

    def spot(sx, sy):
        if sy == 0:
            if sx > 0:
                return slice(size_x, size_x + DEPTH), slice(0, DEPTH)
            return slice(DEPTH, 2 * DEPTH), slice(DEPTH + size_x, wide_x)
        if sx == 0:
            return slice(0, tiles), slice(edge, edge + tiles)
        if sx > 0:
            return slice(tiles - edge, tiles), slice(0, edge)
        return slice(0, edge), slice(edge + tiles, tiles + 2 * edge)

    def halo_refs(sx, sy, coefs):
        src, dst = spot(sx, sy)
        if sy == 0:
            if coefs:
                return ext.at[:, src], ext.at[:, dst]
            return pext.at[0, 0, src], pext.at[0, 0, dst]
        side = 0 if sy > 0 else 1
        if coefs:
            return cpack.at[side, :, src], crecv.at[side, :, dst]
        return ppack.at[side, src], precv.at[side, dst]

    for d, (sx, sy) in enumerate(SENDS):

        @pl.when(jnp.logical_not(exists(-sx, -sy)))
        def _(d=d, sx=sx, sy=sy):
            for coefs in (True, False):
                ref = halo_refs(sx, sy, coefs)[1]
                ref[...] = jnp.zeros(ref.shape, jnp.float32)
            if d < 4:
                uhalo[d] = jnp.zeros(uhalo.shape[1:], jnp.float32)

    def message(sx, sy, src, dst, rsem):
        def copy():
            return pltpu.make_async_remote_copy(
                src_ref=src,
                dst_ref=dst,
                send_sem=sent_sem.at[0],
                recv_sem=rsem,
                device_id=(ix + sx, iy + sy),
                device_id_type=MESH,
            )

        def start():
            @pl.when(exists(sx, sy))
            def _():
                copy().start()

        return start

    sides_x = (ix > 0).astype(jnp.int32) + (ix < n_x - 1).astype(jnp.int32)
    sides_y = (iy > 0).astype(jnp.int32) + (iy < n_y - 1).astype(jnp.int32)

    def rows_of(ref):
        return math.prod(ref.shape) // 128

    def wait_rows(count, sem):
        part = ruler.at[pl.ds(0, count)]
        pltpu.make_async_copy(part, part, sem).wait()

    def wait_sides(refs, sem):
        along_x, along_y = rows_of(refs[0]), rows_of(refs[2])
        corner = rows_of(refs[4]) if len(refs) > 4 else 0
        for a in (1, 2):
            for b in (1, 2):

                @pl.when(jnp.logical_and(sides_x == a, sides_y == b))
                def _(count=a * along_x + b * along_y + a * b * corner):
                    wait_rows(count, sem)

    def gather(table, rsem, axis):
        me, count = ((ix, n_x), (iy, n_y), (flat, everyone))[axis]

        def copy(off):
            if axis == 2:
                peer = off - 1 + (off > me).astype(jnp.int32)
            else:
                peer = lax.rem(me + jnp.where(me < count // 2, count - off, off), count)
            return pltpu.make_async_remote_copy(
                src_ref=table.at[me],
                dst_ref=table.at[me],
                send_sem=sent_sem.at[0],
                recv_sem=rsem,
                device_id=(
                    (peer, iy),
                    (ix, peer),
                    (lax.div(peer, n_y), lax.rem(peer, n_y)),
                )[axis],
                device_id_type=MESH,
            )

        def start():
            for off in range(1, count):
                copy(off).start()

        def wait():
            wait_rows((count - 1) * rows_of(table.at[0]), rsem)

        return start, wait

    t_refs = [halo_refs(sx, sy, True)[1] for sx, sy in SENDS]
    v_refs = [halo_refs(sx, sy, False)[1] for sx, sy in SENDS]
    u_refs = [uhalo.at[d] for d in range(4)]
    c_ops = gather(ctab, c_sem, 0)
    cg_ops = gather(ctabg, cg_sem, 1)
    f_ops = gather(ftab, f_sem, 0)
    g_ops = gather(gtab, g_sem, 2 if direct else 0)
    gg_ops = gather(gtabg, gg_sem, 1)
    t_ops = [
        message(sx, sy, *halo_refs(sx, sy, True), t_sem)
        for d, (sx, sy) in enumerate(SENDS)
    ]
    v_ops = [
        message(sx, sy, *halo_refs(sx, sy, False), v_sem)
        for d, (sx, sy) in enumerate(SENDS)
    ]
    u_ops = [
        message(sx, sy, ustage.at[d], uhalo.at[d], u_sem)
        for d, (sx, sy) in enumerate(FACES)
    ]
    rows = iota((size_y, size_z), 0)
    lanes = iota((size_y, size_z), 1)
    low = rows < half

    for i in (8, 9, 10, 11, 13, 0, 14):
        loads_in[i].wait()
    cell = pcell[...]
    cell_col = lax.shift_right_logical(cell, size_z.bit_length() - 1)
    cell_z = cell & (size_z - 1)
    one_z = (iota((size_z, perfs), 0) == cell_z).astype(jnp.bfloat16)
    one_col = (iota((columns, perfs), 0) == cell_col).astype(jnp.float32)
    one_seg = (iota((segs, perfs), 0) == pseg[...]).astype(jnp.float32)
    one_well = (iota((wells, perfs), 0) == pwell[...]).astype(jnp.bfloat16)
    moves = (iota((wide, wells), 0) == owner[...]).astype(jnp.bfloat16)
    one_slot = dot(moves, one_well, ((1,), (0,)), None).astype(jnp.bfloat16)
    picked = dot_exact(adj[...].reshape(3 * columns, size_z), one_z, ((1,), (0,)))
    flux = None
    for m in range(3):
        part = jnp.sum(picked[m * columns : (m + 1) * columns] * one_col, axis=0, keepdims=True)
        part = part * pin[m : m + 1, :]
        flux = part if flux is None else flux + part
    loads = dot_exact(one_seg * flux, one_slot, ((1,), (1,)))
    slot_no = iota((slots, wide), 0) + ix * slots
    mine = (iota((slots, wide), 1) == slot_no).astype(jnp.float32)
    loads = loads + dot(wrhs[...], mine, ((0,), (0,)))
    folded = ftab.shape[1] < segs
    if folded:
        loads = loads[: segs // 2] + pltpu.roll(loads[segs // 2 :], 64, 1)
    ftab[ix] = loads

    for i in (15, 16, 17, 3, 4, 5, 6):
        loads_in[i].wait()
    packed = ctab.shape[2]
    lane_no = iota((slots, packed), 1)
    first = iota((slots, packed), 0) + ix * slots
    table = None
    for no, ref in enumerate((sdiag, soff, spar)):
        here = (lane_no == first + no * wells).astype(jnp.float32)
        part = dot(ref[...].astype(jnp.float32), here, ((0,), (0,)))
        table = part if table is None else table + part
    share = tree(
        ext[0, x + DEPTH] + 2.0 * (ext[1, x + DEPTH] + ext[2, x + DEPTH] + ext[3, x + DEPTH])
        for x in planes
    )
    share = jnp.sum(jnp.sum(share, axis=0, keepdims=True), axis=1, keepdims=True)
    table = jnp.where(iota((segs, packed), 1) == 3 * wells, share, table)
    ctab[ix] = table

    def pack(read, write):
        for i in range(tiles):
            even, odd = read(2 * i), read(2 * i + 1)
            write(0, i, jnp.where(low, pltpu.roll(even, half, 0), odd))
            write(1, i, jnp.where(low, even, pltpu.roll(odd, half, 0)))

    def unpack(north, south):
        north_r, south_r = pltpu.roll(north, half, 0), pltpu.roll(south, half, 0)
        return jnp.where(low, north, south_r), jnp.where(low, north_r, south)

    diagonals = [exists(sx, sy).astype(jnp.int32) for sx, sy in SENDS[4:]]
    pl.semaphore_wait(barrier, n_x - 1 + n_y - 1 + sum(diagonals[1:], diagonals[0]))
    f_ops[0]()
    c_ops[0]()

    loads_in[1].wait()

    def product(k, x):
        vector = [adj[m, x] for m in range(3)]
        return [
            tree(jac[9 * k + 3 * m + n, x].astype(jnp.float32) * vector[m] for m in range(3))
            for n in range(3)
        ]

    for n, value in enumerate(product(1, size_x - 1)):
        ustage[0, n] = value
    u_ops[0]()
    for n, value in enumerate(product(2, 0)):
        ustage[1, n] = value
    u_ops[1]()
    for x in planes:
        for n, value in enumerate(product(3, x)):
            ustage[2, n, x : x + 1, :] = value[size_y - 1 : size_y]
            cres[n, x] = jnp.where(rows == 0, 0.0, pltpu.roll(value, 1, 0))
    u_ops[2]()
    for x in planes:
        for n, value in enumerate(product(4, x)):
            ustage[3, n, x : x + 1, :] = value[0:1]
            cres[n, x] += jnp.where(rows == size_y - 1, 0.0, pltpu.roll(value, size_y - 1, 0))
    u_ops[3]()

    for f in range(4):

        def put(side, i, value, f=f):
            cpack[side, f, i] = value

        pack(lambda x, f=f: ext[f, x + DEPTH], put)
    for op in t_ops:
        op()

    for x in planes:
        groups = [product(0, x)]
        if x > 0:
            groups.append(product(1, x - 1))
        if x < size_x - 1:
            groups.append(product(2, x + 1))
        above = product(5, x)
        groups.append([jnp.where(lanes == 0, 0.0, pltpu.roll(v, 1, 1)) for v in above])
        below = product(6, x)
        groups.append(
            [jnp.where(lanes == size_z - 1, 0.0, pltpu.roll(v, size_z - 1, 1)) for v in below]
        )
        for n in range(3):
            cres[n, x] += tree(group[n] for group in groups)

    c_ops[1]()
    total = tree(ctab[i] for i in range(n_x))
    base = (3 * wells) // 128 * 128
    ctabg[iy] = total[0:1, base : base + 128]
    cg_ops[0]()

    def constant(no):
        if wells % 128 == 0:
            return total[:, no * wells : (no + 1) * wells]
        return total if no == 0 else pltpu.roll(total, 128 - no * wells, 1)

    used = iota((segs, wide), 1) < wells
    diag = jnp.where(used, constant(0), 1.0)
    ratio = jnp.where(used, constant(1), 0.0) / diag
    parent = jnp.where(used, constant(2), 0.0)
    levels = iota((segs, wide), 0).astype(jnp.float32)
    steps = [
        jnp.where(levels == parent[s : s + 1], ratio[s : s + 1], 0.0) for s in range(1, segs)
    ]
    for i in (12, 2, 7):
        loads_in[i].wait()

    f_ops[1]()
    load = tree(ftab[i] for i in range(n_x))
    if folded:
        load = jnp.concatenate([load, pltpu.roll(load, 64, 1)], axis=0)
    for s in range(segs - 1, 0, -1):
        load = load + load[s : s + 1] * steps[s - 1]
    answers = load / diag
    values = dot_exact(answers, one_slot, ((1,), (0,)))
    values = jnp.sum(values * one_seg, axis=0, keepdims=True)
    spread = jnp.concatenate([one_col * (pout[n : n + 1, :] * values) for n in range(3)], axis=0)
    added = dot_exact(spread, one_z, ((1,), (1,)))

    wait_sides(u_refs, u_sem)
    for x in planes:
        live = active[x].astype(jnp.float32)
        rhs = None
        for n in range(3):
            row = n * columns + x * size_y
            value = cres[n, x] + added[row : row + size_y]
            if x == 0:
                value = value + uhalo[0, n]
            if x == size_x - 1:
                value = value + uhalo[1, n]
            value = value + jnp.where(rows == 0, uhalo[2, n, x : x + 1, :], 0.0)
            value = value + jnp.where(rows == size_y - 1, uhalo[3, n, x : x + 1, :], 0.0)
            value = value * live
            upd[n, x] = value
            part = weights[n, x] * value
            rhs = part if rhs is None else rhs + part
        pext[0, 0, x + DEPTH] = rhs

    def put_p(side, i, value):
        ppack[side, i] = value

    pack(lambda x: pext[0, 0, x + DEPTH], put_p)
    for op in v_ops:
        op()

    wout[...] = dot(mine, answers, ((1,), (1,)))
    cg_ops[1]()
    mean = tree(ctabg[i] for i in range(n_y))
    mean = jnp.where(iota((1, 128), 1) == 3 * wells - base, mean, 0.0)
    mean = jnp.sum(mean, axis=1, keepdims=True)
    shift = jnp.broadcast_to(mean * (0.75 / (n_x * n_y * columns * size_z)), (1, size_z))
    inverse = 1.0 / shift
    wait_sides(t_refs, t_sem)
    last_x = (ix == n_x - 1).astype(jnp.int32)
    last_y = (iy == n_y - 1).astype(jnp.int32)
    last_row = rows == jnp.where(last_y == 1, size_y - 1, size_y)
    keep_x = 1.0 - last_x.astype(jnp.float32)

    def following(a, b):
        a, b = pltpu.roll(a, size_y - 1, 0), pltpu.roll(b, size_y - 1, 0)
        return jnp.where(rows == size_y - 1, b, a), jnp.where(rows == size_y - 1, a, b)

    def preceding(a, b):
        a, b = pltpu.roll(a, 1, 0), pltpu.roll(b, 1, 0)
        return jnp.where(rows == 0, b, a), jnp.where(rows == 0, a, b)

    raw_x = None
    for i in range(wide_x // 2):
        both = [unpack(crecv[1, f, i], crecv[0, f, i]) for f in range(4)]
        for odd in range(2):
            j = 2 * i + odd
            parts = [(ext[f, j], both[f][odd]) for f in range(4)]
            south_raw = preceding(*parts[2])
            north = (jnp.where(last_row, 0.0, parts[2][0]), parts[2][1])
            south = preceding(*north)
            for h in range(2):
                here_x = parts[1][h]
                inside = jnp.where(lanes == size_z - 1, 0.0, parts[3][h])
                under = pltpu.roll(inside, 1, 1)
                if j > 0:
                    full = tree(
                        [
                            parts[0][h] + here_x,
                            raw_x[h] + parts[2][h],
                            south_raw[h] + parts[3][h],
                            under,
                        ]
                    )
                    coef[0, h, j] = full * inverse - 1.0
                east = here_x * inverse
                coef[1, h, j] = east * keep_x if j == DEPTH + size_x - 1 else east
                coef[2, h, j] = north[h] * inverse
                coef[3, h, j] = south[h] * inverse
                coef[4, h, j] = inside * inverse
                coef[5, h, j] = under * inverse
            raw_x = (parts[1][0], parts[1][1])

    wait_sides(v_refs, v_sem)
    for i in range(wide_x // 2):
        pair = unpack(precv[1, i], precv[0, i])
        pext[0, 1, 2 * i] = pair[0]
        pext[0, 1, 2 * i + 1] = pair[1]

    for k in range(ITERS):
        final = k == ITERS - 1
        for j in range(k + 1, wide_x - k - 1):
            here = (pext[k, 0, j], pext[k, 1, j])
            up = following(*here)
            down = preceding(*here)
            for h in range(1 if final else 2):
                image = coef[0, h, j] * here[h] - tree(
                    [
                        coef[1, h, j] * pext[k, h, j + 1],
                        coef[1, h, j - 1] * pext[k, h, j - 1],
                        coef[2, h, j] * up[h],
                        coef[3, h, j] * down[h],
                        coef[4, h, j] * pltpu.roll(here[h], size_z - 1, 1),
                        coef[5, h, j] * pltpu.roll(here[h], 1, 1),
                    ]
                )
                pext[k + 1, h, j] = image if k == 0 else 2.0 * image - pext[k - 1, h, j]

    def mine_of(k, x):
        return pext[k, 0, x + DEPTH]

    count = 16
    grams = [
        jnp.sum(tree(mine_of(i, x) * mine_of(j, x) for x in planes), axis=0, keepdims=True)
        for i, j in PAIRS
    ]
    grams += [jnp.zeros((1, size_z), jnp.float32)] * (count - len(PAIRS))
    column = jnp.sum(jnp.concatenate(grams, axis=0), axis=1, keepdims=True)
    on_lane = iota((count, 128), 0) == iota((count, 128), 1)
    entries = jnp.sum(jnp.where(on_lane, column, 0.0), axis=0, keepdims=True)
    gtab[flat if direct else ix] = entries
    g_ops[0]()
    g_ops[1]()
    sums = tree(gtab[i] for i in range(gtab.shape[0]))
    if not direct:
        gtabg[iy] = sums
        gg_ops[0]()
        gg_ops[1]()
        sums = tree(gtabg[i] for i in range(n_y))
    sums = jnp.sum(jnp.where(on_lane, sums, 0.0), axis=1, keepdims=True)
    sums = jnp.broadcast_to(sums, (count, size_z))

    def gram(i, j):
        row = PAIRS.index((min(i, j), max(i, j)))
        return sums[row : row + 1]

    answer = krylov_coefficients(gram, shift)
    for x in planes:
        pressure = tree(answer[k] * mine_of(k, x) for k in range(ITERS))
        for n in range(3):
            upd[n, x] += weights[n, x] * pressure

    sent_rows = sum(
        (count - 1) * rows_of(table.at[0])
        for table, count in (
            (ctab, n_x), (ctabg, n_y), (ftab, n_x), (gtab, gtab.shape[0]), (gtabg, 1 if direct else n_y),
        )
    )
    shapes = [[t, v] + ([u_refs[d]] if d < 4 else []) for d, (t, v) in enumerate(zip(t_refs, v_refs))]
    along_x, along_y, corner = [sum(rows_of(r) for r in shapes[d]) for d in (0, 2, 4)]
    for a in (1, 2):
        for b in (1, 2):

            @pl.when(jnp.logical_and(sides_x == a, sides_y == b))
            def _(count=a * along_x + b * along_y + a * b * corner + sent_rows):
                wait_rows(count, sent_sem.at[0])


def hand_over(update, answers, update_out, answers_out, sems):
    copies = [
        pltpu.make_async_copy(update, update_out, sems.at[0]),
        pltpu.make_async_copy(answers, answers_out, sems.at[1]),
    ]
    for copy in copies:
        copy.start()
    for copy in copies:
        copy.wait()


def shards(n_x, n_y, *args):
    args = list(args)
    size_x, size_y, size_z = args[0].shape[1:]
    for k in (8, 9, 10):
        args[k] = args[k][None]
    for k in (14, 15, 16, 17):
        args[k] = args[k][:, 0, :].T
    slots, segs = args[14].shape
    wells = args[13].shape[1]
    wide = -(-wells // 128) * 128
    packed = -(-(3 * wells + 1) // 128) * 128
    folded = segs // 2 if wells <= 64 and segs == 16 else segs
    joined = n_x * n_y if n_x * n_y <= 32 else n_x
    plane = (size_y, size_z)
    wide_x = size_x + 2 * DEPTH
    dma = pltpu.SemaphoreType.DMA

    def f32(*shape):
        return pltpu.VMEM(shape, jnp.float32)

    held = [pltpu.VMEM(args[k].shape, args[k].dtype) for k in (0, 1, 2, 7) + tuple(range(8, 18))]
    held += [f32(4, wide_x, *plane), f32(ITERS + 1, 2, wide_x, *plane)]
    tiles = size_x // 2
    along = DEPTH * size_y
    ruler = 2 * (2 * 5 * along + 2 * 3 * size_y) + 4 * 5 * along // 2
    ruler += n_x * segs * (packed + wide) // 128 + 2 * n_y + joined
    scratch = [
        f32(3, size_x, *plane),
        f32(6, 2, wide_x, *plane),
        f32(n_x, segs, packed),
        f32(n_y, 1, 128),
        f32(n_x, folded, wide),
        f32(joined, 1, 128),
        f32(n_y, 1, 128),
        f32(2, 4, tiles, *plane),
        f32(2, 4, wide_x // 2, *plane),
        f32(2, tiles, *plane),
        f32(2, wide_x // 2, *plane),
        f32(4, 3, *plane),
        f32(4, 3, *plane),
        f32(ruler, 1, 128),
        dma((18,)),
        dma((1,)),
        dma((8,)),
    ]
    vmem = pl.BlockSpec(memory_space=pltpu.VMEM)
    update, answers = pl.pallas_call(
        functools.partial(kernel, n_x, n_y),
        out_shape=(
            pltpu.VMEM(args[0].shape, jnp.float32),
            pltpu.VMEM((slots, segs), jnp.float32),
        ),
        in_specs=[pl.BlockSpec(memory_space=pl.ANY)] * 18,
        out_specs=(vmem, vmem),
        scratch_shapes=held + scratch,
        compiler_params=pltpu.CompilerParams(collective_id=0, has_side_effects=True),
    )(*args)
    update = pltpu.with_memory_space_constraint(update, pltpu.VMEM)
    answers = pltpu.with_memory_space_constraint(answers, pltpu.VMEM)
    any_space = pl.BlockSpec(memory_space=pl.ANY)
    update, answers = pl.pallas_call(
        hand_over,
        out_shape=(
            jax.ShapeDtypeStruct(update.shape, jnp.float32),
            jax.ShapeDtypeStruct(answers.shape, jnp.float32),
        ),
        in_specs=[vmem, vmem],
        out_specs=(any_space, any_space),
        scratch_shapes=[dma((2,))],
    )(update, answers)
    return update, answers.T[:, None, :]


def solution(mesh):
    body = functools.partial(shards, mesh.shape["gx"], mesh.shape["gy"])
    cells = P("gx", "gy", None)
    stacked = P(None, "gx", "gy", None)
    perf = P(("gx", "gy"))
    perf_3 = P(None, ("gx", "gy"))
    segment = P(None, "gy", "gx")
    return jax.shard_map(
        body,
        mesh=mesh,
        in_specs=(stacked, stacked)
        + (cells,) * 5
        + (stacked,)
        + (perf,) * 3
        + (perf_3,) * 2
        + (P("gy", None),)
        + (segment,) * 4,
        out_specs=(stacked, segment),
        check_vma=False,
    )
```

```python
import functools
import math

import jax
import jax.numpy as jnp
from jax import lax
from jax.experimental import pallas as pl
from jax.experimental.pallas import tpu as pltpu
from jax.sharding import PartitionSpec as P

ITERS = 4
MESH = pl.DeviceIdType.MESH
HIGH = lax.Precision.HIGHEST
PAIRS = [(i, j) for i in range(ITERS) for j in range(i, ITERS + 1)]


def iota(shape, dim):
    return lax.broadcasted_iota(jnp.int32, shape, dim)


def dot(a, b, dims, precision=HIGH):
    return lax.dot_general(
        a, b, (dims, ((), ())), precision=precision, preferred_element_type=jnp.float32
    )


def dot_exact(a, pick, dims):
    high = a.astype(jnp.bfloat16)
    rest = a - high.astype(jnp.float32)
    mid = rest.astype(jnp.bfloat16)
    low = (rest - mid.astype(jnp.float32)).astype(jnp.bfloat16)
    parts = [dot(part, pick, dims, None) for part in (high, mid, low)]
    return parts[0] + (parts[1] + parts[2])


def tree(values):
    values = list(values)
    while len(values) > 1:
        pairs = [a + b for a, b in zip(values[::2], values[1::2])]
        values = pairs + values[len(pairs) * 2 :]
    return values[0]


def krylov_coefficients(gram, shift):
    size = ITERS + 1

    def apply(v):
        out = [None] * size

        def put(k, value):
            out[k] = value if out[k] is None else out[k] + value

        for k, value in enumerate(v):
            if value is None:
                continue
            scaled = value * shift
            put(k, scaled)
            if k == 0:
                put(1, scaled)
            else:
                put(k + 1, scaled * 0.5)
                put(k - 1, scaled * 0.5)
        return out

    def inner(a, b):
        total = []
        for j in range(size):
            if b[j] is None:
                continue
            part = [a[i] * gram(i, j) for i in range(size) if a[i] is not None]
            total.append(tree(part) * b[j])
        return tree(total)

    def axpy(a, scale, b):
        out = []
        for p, q in zip(a, b):
            if q is None:
                out.append(p)
            else:
                out.append(scale * q if p is None else p + scale * q)
        return out

    one = jnp.ones_like(shift)
    residual = [one] + [None] * ITERS
    direction = list(residual)
    answer = [None] * size
    norm = gram(0, 0)
    for iteration in range(ITERS):
        image = apply(direction)
        bottom = inner(direction, image)
        alpha = jnp.where(bottom > 0, norm / bottom, 0.0)
        answer = axpy(answer, alpha, direction)
        if iteration == ITERS - 1:
            break
        residual = axpy(residual, -alpha, image)
        new = inner(residual, residual)
        beta = jnp.where(norm > 0, new / norm, 0.0)
        direction = axpy(residual, beta, direction)
        norm = new
    return answer[:ITERS]


DEPTH = ITERS
ORDER = (0, 3, 1, 2)
SENDS = [(1, 0), (-1, 0), (0, 1), (0, -1), (1, 1), (-1, 1), (1, -1), (-1, -1)]
FACES = [(1, 0), (-1, 0), (0, 1), (0, -1)]
HELD = 16


def kernel(n_x, n_y, *refs):
    inputs, (upd, wout) = refs[:18], refs[18:20]
    held, scratch = refs[20 : 20 + HELD], refs[20 + HELD :]
    adj, jac, active, weights, pcell, pwell, pseg, pin, pout, owner = held[:10]
    wrhs, sdiag, soff, spar, ext, pext = held[10:]
    (cres, coef, ctab, ctabg, ftab, gtab, gtabg, cpack, crecv, ppack, precv) = scratch[:11]
    ustage, uhalo, ruler, in_sem, sent_sem, got_sem = scratch[11:]
    c_sem, cg_sem, f_sem, g_sem, gg_sem, t_sem, u_sem, v_sem = [got_sem.at[i] for i in range(8)]

    ix = lax.axis_index("gx")
    iy = lax.axis_index("gy")
    size_x, size_y, size_z = adj.shape[1:]
    planes = range(size_x)
    wide_x = size_x + 2 * DEPTH
    own = slice(DEPTH, DEPTH + size_x)
    half = size_y // 2
    tiles = size_x // 2
    edge = DEPTH // 2
    perfs = pcell.shape[1]
    slots, segs = wrhs.shape
    wells = owner.shape[1]
    wide = -(-wells // 128) * 128
    columns = size_x * size_y

    places = [
        adj, jac, active, ext.at[1, own], ext.at[2, own], ext.at[3, own], ext.at[0, own],
        weights, pcell, pwell, pseg, pin, pout, owner, wrhs, sdiag, soff, spar,
    ]
    loads_in = [
        pltpu.make_async_copy(src, dst, in_sem.at[i])
        for i, (src, dst) in enumerate(zip(inputs, places))
    ]
    for i in (8, 9, 10, 11, 13, 0, 14, 15, 16, 17, 3, 4, 5, 6, 1, 12, 2, 7):
        loads_in[i].start()

    def exists(sx, sy):
        fine = None
        for step, at, count in ((sx, ix, n_x), (sy, iy, n_y)):
            if step:
                one = at < count - 1 if step > 0 else at > 0
                fine = one if fine is None else jnp.logical_and(fine, one)
        return fine

    barrier = pltpu.get_barrier_semaphore()
    everyone = n_x * n_y
    direct = gtab.shape[0] == everyone
    flat = ix * n_y + iy
    for off in range(1, n_x):
        pl.semaphore_signal(
            barrier, inc=1, device_id=(lax.rem(ix + off, n_x), iy), device_id_type=MESH
        )
    for off in range(1, n_y):
        pl.semaphore_signal(
            barrier, inc=1, device_id=(ix, lax.rem(iy + off, n_y)), device_id_type=MESH
        )
    for sx, sy in SENDS[4:]:

        @pl.when(exists(sx, sy))
        def _(sx=sx, sy=sy):
            pl.semaphore_signal(barrier, inc=1, device_id=(ix + sx, iy + sy), device_id_type=MESH)

    def spot(sx, sy):
        if sy == 0:
            if sx > 0:
                return slice(size_x, size_x + DEPTH), slice(0, DEPTH)
            return slice(DEPTH, 2 * DEPTH), slice(DEPTH + size_x, wide_x)
        if sx == 0:
            return slice(0, tiles), slice(edge, edge + tiles)
        if sx > 0:
            return slice(tiles - edge, tiles), slice(0, edge)
        return slice(0, edge), slice(edge + tiles, tiles + 2 * edge)

    def halo_refs(sx, sy, coefs):
        src, dst = spot(sx, sy)
        if sy == 0:
            if coefs:
                return ext.at[:, src], ext.at[:, dst]
            return pext.at[0, 0, src], pext.at[0, 0, dst]
        side = 0 if sy > 0 else 1
        if coefs:
            if sx == 0:
                src, dst = slice(0, 4 * tiles), slice(4 * edge, 4 * (edge + tiles))
            elif sx > 0:
                src, dst = slice(4 * tiles - 5, 4 * tiles), slice(4 * edge - 5, 4 * edge)
            else:
                src, dst = slice(0, 5), slice(4 * (edge + tiles), 4 * (edge + tiles) + 5)
            return cpack.at[side, src], crecv.at[side, dst]
        return ppack.at[side, src], precv.at[side, dst]

    for d, (sx, sy) in enumerate(SENDS):

        @pl.when(jnp.logical_not(exists(-sx, -sy)))
        def _(d=d, sx=sx, sy=sy):
            for coefs in (True, False):
                ref = halo_refs(sx, sy, coefs)[1]
                ref[...] = jnp.zeros(ref.shape, jnp.float32)
            if d < 4:
                uhalo[d] = jnp.zeros(uhalo.shape[1:], jnp.float32)

    def message(sx, sy, src, dst, rsem):
        def copy():
            return pltpu.make_async_remote_copy(
                src_ref=src,
                dst_ref=dst,
                send_sem=sent_sem.at[0],
                recv_sem=rsem,
                device_id=(ix + sx, iy + sy),
                device_id_type=MESH,
            )

        def start():
            @pl.when(exists(sx, sy))
            def _():
                copy().start()

        return start

    sides_x = (ix > 0).astype(jnp.int32) + (ix < n_x - 1).astype(jnp.int32)
    sides_y = (iy > 0).astype(jnp.int32) + (iy < n_y - 1).astype(jnp.int32)

    def rows_of(ref):
        return math.prod(ref.shape) // 128

    def wait_rows(count, sem):
        part = ruler.at[pl.ds(0, count)]
        pltpu.make_async_copy(part, part, sem).wait()

    def wait_sides(refs, sem):
        along_x, along_y = rows_of(refs[0]), rows_of(refs[2])
        corner = rows_of(refs[4]) if len(refs) > 4 else 0
        for a in (1, 2):
            for b in (1, 2):

                @pl.when(jnp.logical_and(sides_x == a, sides_y == b))
                def _(count=a * along_x + b * along_y + a * b * corner):
                    wait_rows(count, sem)

    def gather(table, rsem, axis):
        me, count = ((ix, n_x), (iy, n_y), (flat, everyone))[axis]

        def copy(off):
            if axis == 2:
                peer = off - 1 + (off > me).astype(jnp.int32)
            else:
                peer = lax.rem(me + jnp.where(me < count // 2, count - off, off), count)
            return pltpu.make_async_remote_copy(
                src_ref=table.at[me],
                dst_ref=table.at[me],
                send_sem=sent_sem.at[0],
                recv_sem=rsem,
                device_id=(
                    (peer, iy),
                    (ix, peer),
                    (lax.div(peer, n_y), lax.rem(peer, n_y)),
                )[axis],
                device_id_type=MESH,
            )

        def start():
            for off in range(1, count):
                copy(off).start()

        def wait():
            wait_rows((count - 1) * rows_of(table.at[0]), rsem)

        return start, wait

    t_refs = [halo_refs(sx, sy, True)[1] for sx, sy in SENDS]
    v_refs = [halo_refs(sx, sy, False)[1] for sx, sy in SENDS]
    u_refs = [uhalo.at[d] for d in range(4)]
    c_ops = gather(ctab, c_sem, 0)
    cg_ops = gather(ctabg, cg_sem, 1)
    f_ops = gather(ftab, f_sem, 0)
    g_ops = gather(gtab, g_sem, 2 if direct else 0)
    gg_ops = gather(gtabg, gg_sem, 1)
    t_ops = [
        message(sx, sy, *halo_refs(sx, sy, True), t_sem)
        for d, (sx, sy) in enumerate(SENDS)
    ]
    v_ops = [
        message(sx, sy, *halo_refs(sx, sy, False), v_sem)
        for d, (sx, sy) in enumerate(SENDS)
    ]
    u_ops = [
        message(sx, sy, ustage.at[d], uhalo.at[d], u_sem)
        for d, (sx, sy) in enumerate(FACES)
    ]
    rows = iota((size_y, size_z), 0)
    lanes = iota((size_y, size_z), 1)
    low = rows < half

    for i in (8, 9, 10, 11, 13, 0, 14):
        loads_in[i].wait()
    cell = pcell[...]
    cell_col = lax.shift_right_logical(cell, size_z.bit_length() - 1)
    cell_z = cell & (size_z - 1)
    one_z = (iota((size_z, perfs), 0) == cell_z).astype(jnp.bfloat16)
    one_col = (iota((columns, perfs), 0) == cell_col).astype(jnp.float32)
    one_seg = (iota((segs, perfs), 0) == pseg[...]).astype(jnp.float32)
    one_well = (iota((wells, perfs), 0) == pwell[...]).astype(jnp.bfloat16)
    moves = (iota((wide, wells), 0) == owner[...]).astype(jnp.bfloat16)
    one_slot = dot(moves, one_well, ((1,), (0,)), None).astype(jnp.bfloat16)
    picked = dot_exact(adj[...].reshape(3 * columns, size_z), one_z, ((1,), (0,)))
    flux = None
    for m in range(3):
        part = jnp.sum(picked[m * columns : (m + 1) * columns] * one_col, axis=0, keepdims=True)
        part = part * pin[m : m + 1, :]
        flux = part if flux is None else flux + part
    loads = dot_exact(one_seg * flux, one_slot, ((1,), (1,)))
    slot_no = iota((slots, wide), 0) + ix * slots
    mine = (iota((slots, wide), 1) == slot_no).astype(jnp.float32)
    loads = loads + dot(wrhs[...], mine, ((0,), (0,)))
    folded = ftab.shape[1] < segs
    if folded:
        loads = loads[: segs // 2] + pltpu.roll(loads[segs // 2 :], 64, 1)
    ftab[ix] = loads

    for i in (15, 16, 17, 3, 4, 5, 6):
        loads_in[i].wait()
    packed = ctab.shape[2]
    lane_no = iota((slots, packed), 1)
    first = iota((slots, packed), 0) + ix * slots
    table = None
    for no, ref in enumerate((sdiag, soff, spar)):
        here = (lane_no == first + no * wells).astype(jnp.float32)
        part = dot(ref[...].astype(jnp.float32), here, ((0,), (0,)))
        table = part if table is None else table + part
    share = tree(
        ext[0, x + DEPTH] + 2.0 * (ext[1, x + DEPTH] + ext[2, x + DEPTH] + ext[3, x + DEPTH])
        for x in planes
    )
    share = jnp.sum(jnp.sum(share, axis=0, keepdims=True), axis=1, keepdims=True)
    table = jnp.where(iota((segs, packed), 1) == 3 * wells, share, table)
    ctab[ix] = table

    def pack(read, write):
        for i in range(tiles):
            even, odd = read(2 * i), read(2 * i + 1)
            write(0, i, jnp.where(low, pltpu.roll(even, half, 0), odd))
            write(1, i, jnp.where(low, even, pltpu.roll(odd, half, 0)))

    def unpack(north, south):
        north_r, south_r = pltpu.roll(north, half, 0), pltpu.roll(south, half, 0)
        return jnp.where(low, north, south_r), jnp.where(low, north_r, south)

    loads_in[1].wait()

    def product(k, x):
        vector = [adj[m, x] for m in range(3)]
        return [
            tree(jac[9 * k + 3 * m + n, x].astype(jnp.float32) * vector[m] for m in range(3))
            for n in range(3)
        ]

    for n, value in enumerate(product(1, size_x - 1)):
        ustage[0, n] = value
    for n, value in enumerate(product(2, 0)):
        ustage[1, n] = value
    for x in planes:
        for n, value in enumerate(product(3, x)):
            ustage[2, n, x : x + 1, :] = value[size_y - 1 : size_y]
            cres[n, x] = jnp.where(rows == 0, 0.0, pltpu.roll(value, 1, 0))
    for x in planes:
        for n, value in enumerate(product(4, x)):
            ustage[3, n, x : x + 1, :] = value[0:1]
            cres[n, x] += jnp.where(rows == size_y - 1, 0.0, pltpu.roll(value, size_y - 1, 0))

    for f in range(4):

        def put(side, i, value, f=f):
            cpack[side, 4 * i + ORDER[f]] = value

        pack(lambda x, f=f: ext[f, x + DEPTH], put)
    diagonals = [exists(sx, sy).astype(jnp.int32) for sx, sy in SENDS[4:]]
    pl.semaphore_wait(barrier, n_x - 1 + n_y - 1 + sum(diagonals[1:], diagonals[0]))
    f_ops[0]()
    for op in u_ops:
        op()
    c_ops[0]()
    for op in t_ops:
        op()

    for x in planes:
        groups = [product(0, x)]
        if x > 0:
            groups.append(product(1, x - 1))
        if x < size_x - 1:
            groups.append(product(2, x + 1))
        above = product(5, x)
        groups.append([jnp.where(lanes == 0, 0.0, pltpu.roll(v, 1, 1)) for v in above])
        below = product(6, x)
        groups.append(
            [jnp.where(lanes == size_z - 1, 0.0, pltpu.roll(v, size_z - 1, 1)) for v in below]
        )
        for n in range(3):
            cres[n, x] += tree(group[n] for group in groups)

    c_ops[1]()
    total = tree(ctab[i] for i in range(n_x))
    base = (3 * wells) // 128 * 128
    ctabg[iy] = total[0:1, base : base + 128]
    cg_ops[0]()

    def constant(no):
        if wells % 128 == 0:
            return total[:, no * wells : (no + 1) * wells]
        return total if no == 0 else pltpu.roll(total, 128 - no * wells, 1)

    used = iota((segs, wide), 1) < wells
    diag = jnp.where(used, constant(0), 1.0)
    ratio = jnp.where(used, constant(1), 0.0) / diag
    parent = jnp.where(used, constant(2), 0.0)
    levels = iota((segs, wide), 0).astype(jnp.float32)
    steps = [
        jnp.where(levels == parent[s : s + 1], ratio[s : s + 1], 0.0) for s in range(1, segs)
    ]
    for i in (12, 2, 7):
        loads_in[i].wait()

    f_ops[1]()
    load = tree(ftab[i] for i in range(n_x))
    if folded:
        load = jnp.concatenate([load, pltpu.roll(load, 64, 1)], axis=0)
    for s in range(segs - 1, 0, -1):
        load = load + load[s : s + 1] * steps[s - 1]
    answers = load / diag
    values = dot_exact(answers, one_slot, ((1,), (0,)))
    values = jnp.sum(values * one_seg, axis=0, keepdims=True)
    spread = jnp.concatenate([one_col * (pout[n : n + 1, :] * values) for n in range(3)], axis=0)
    added = dot_exact(spread, one_z, ((1,), (1,)))

    wait_sides(u_refs, u_sem)
    for x in planes:
        live = active[x].astype(jnp.float32)
        rhs = None
        for n in range(3):
            row = n * columns + x * size_y
            value = cres[n, x] + added[row : row + size_y]
            if x == 0:
                value = value + uhalo[0, n]
            if x == size_x - 1:
                value = value + uhalo[1, n]
            value = value + jnp.where(rows == 0, uhalo[2, n, x : x + 1, :], 0.0)
            value = value + jnp.where(rows == size_y - 1, uhalo[3, n, x : x + 1, :], 0.0)
            value = value * live
            upd[n, x] = value
            part = weights[n, x] * value
            rhs = part if rhs is None else rhs + part
        pext[0, 0, x + DEPTH] = rhs

    def put_p(side, i, value):
        ppack[side, i] = value

    pack(lambda x: pext[0, 0, x + DEPTH], put_p)
    for op in v_ops:
        op()

    wout[...] = dot(mine, answers, ((1,), (1,)))
    cg_ops[1]()
    mean = tree(ctabg[i] for i in range(n_y))
    mean = jnp.where(iota((1, 128), 1) == 3 * wells - base, mean, 0.0)
    mean = jnp.sum(mean, axis=1, keepdims=True)
    shift = jnp.broadcast_to(mean * (0.75 / (n_x * n_y * columns * size_z)), (1, size_z))
    inverse = 1.0 / shift
    wait_sides(t_refs, t_sem)
    last_x = (ix == n_x - 1).astype(jnp.int32)
    last_y = (iy == n_y - 1).astype(jnp.int32)
    last_row = rows == jnp.where(last_y == 1, size_y - 1, size_y)
    keep_x = 1.0 - last_x.astype(jnp.float32)

    def following(a, b):
        a, b = pltpu.roll(a, size_y - 1, 0), pltpu.roll(b, size_y - 1, 0)
        return jnp.where(rows == size_y - 1, b, a), jnp.where(rows == size_y - 1, a, b)

    def preceding(a, b):
        a, b = pltpu.roll(a, 1, 0), pltpu.roll(b, 1, 0)
        return jnp.where(rows == 0, b, a), jnp.where(rows == 0, a, b)

    raw_x = None
    for i in range(wide_x // 2):
        both = [unpack(crecv[1, 4 * i + f], crecv[0, 4 * i + f]) for f in ORDER]
        for odd in range(2):
            j = 2 * i + odd
            parts = [(ext[f, j], both[f][odd]) for f in range(4)]
            south_raw = preceding(*parts[2])
            north = (jnp.where(last_row, 0.0, parts[2][0]), parts[2][1])
            south = preceding(*north)
            for h in range(2):
                here_x = parts[1][h]
                inside = jnp.where(lanes == size_z - 1, 0.0, parts[3][h])
                under = pltpu.roll(inside, 1, 1)
                if j > 0:
                    full = tree(
                        [
                            parts[0][h] + here_x,
                            raw_x[h] + parts[2][h],
                            south_raw[h] + parts[3][h],
                            under,
                        ]
                    )
                    coef[0, h, j] = full * inverse - 1.0
                east = here_x * inverse
                coef[1, h, j] = east * keep_x if j == DEPTH + size_x - 1 else east
                coef[2, h, j] = north[h] * inverse
                coef[3, h, j] = south[h] * inverse
                coef[4, h, j] = inside * inverse
                coef[5, h, j] = under * inverse
            raw_x = (parts[1][0], parts[1][1])

    wait_sides(v_refs, v_sem)
    for i in range(wide_x // 2):
        pair = unpack(precv[1, i], precv[0, i])
        pext[0, 1, 2 * i] = pair[0]
        pext[0, 1, 2 * i + 1] = pair[1]

    for k in range(ITERS):
        final = k == ITERS - 1
        for j in range(k + 1, wide_x - k - 1):
            here = (pext[k, 0, j], pext[k, 1, j])
            up = following(*here)
            down = preceding(*here)
            for h in range(1 if final else 2):
                image = coef[0, h, j] * here[h] - tree(
                    [
                        coef[1, h, j] * pext[k, h, j + 1],
                        coef[1, h, j - 1] * pext[k, h, j - 1],
                        coef[2, h, j] * up[h],
                        coef[3, h, j] * down[h],
                        coef[4, h, j] * pltpu.roll(here[h], size_z - 1, 1),
                        coef[5, h, j] * pltpu.roll(here[h], 1, 1),
                    ]
                )
                pext[k + 1, h, j] = image if k == 0 else 2.0 * image - pext[k - 1, h, j]

    def mine_of(k, x):
        return pext[k, 0, x + DEPTH]

    count = 16
    grams = [
        jnp.sum(tree(mine_of(i, x) * mine_of(j, x) for x in planes), axis=0, keepdims=True)
        for i, j in PAIRS
    ]
    grams += [jnp.zeros((1, size_z), jnp.float32)] * (count - len(PAIRS))
    column = jnp.sum(jnp.concatenate(grams, axis=0), axis=1, keepdims=True)
    on_lane = iota((count, 128), 0) == iota((count, 128), 1)
    entries = jnp.sum(jnp.where(on_lane, column, 0.0), axis=0, keepdims=True)
    gtab[flat if direct else ix] = entries
    g_ops[0]()
    g_ops[1]()
    sums = tree(gtab[i] for i in range(gtab.shape[0]))
    if not direct:
        gtabg[iy] = sums
        gg_ops[0]()
        gg_ops[1]()
        sums = tree(gtabg[i] for i in range(n_y))
    sums = jnp.sum(jnp.where(on_lane, sums, 0.0), axis=1, keepdims=True)
    sums = jnp.broadcast_to(sums, (count, size_z))

    def gram(i, j):
        row = PAIRS.index((min(i, j), max(i, j)))
        return sums[row : row + 1]

    answer = krylov_coefficients(gram, shift)
    for x in planes:
        pressure = tree(answer[k] * mine_of(k, x) for k in range(ITERS))
        for n in range(3):
            upd[n, x] += weights[n, x] * pressure

    sent_rows = sum(
        (count - 1) * rows_of(table.at[0])
        for table, count in (
            (ctab, n_x), (ctabg, n_y), (ftab, n_x), (gtab, gtab.shape[0]), (gtabg, 1 if direct else n_y),
        )
    )
    shapes = [[t, v] + ([u_refs[d]] if d < 4 else []) for d, (t, v) in enumerate(zip(t_refs, v_refs))]
    along_x, along_y, corner = [sum(rows_of(r) for r in shapes[d]) for d in (0, 2, 4)]
    for a in (1, 2):
        for b in (1, 2):

            @pl.when(jnp.logical_and(sides_x == a, sides_y == b))
            def _(count=a * along_x + b * along_y + a * b * corner + sent_rows):
                wait_rows(count, sent_sem.at[0])


def hand_over(update, answers, update_out, answers_out, sems):
    copies = [
        pltpu.make_async_copy(update, update_out, sems.at[0]),
        pltpu.make_async_copy(answers, answers_out, sems.at[1]),
    ]
    for copy in copies:
        copy.start()
    for copy in copies:
        copy.wait()


def shards(n_x, n_y, *args):
    args = list(args)
    size_x, size_y, size_z = args[0].shape[1:]
    for k in (8, 9, 10):
        args[k] = args[k][None]
    for k in (14, 15, 16, 17):
        args[k] = args[k][:, 0, :].T
    slots, segs = args[14].shape
    wells = args[13].shape[1]
    wide = -(-wells // 128) * 128
    packed = -(-(3 * wells + 1) // 128) * 128
    folded = segs // 2 if wells <= 64 and segs == 16 else segs
    joined = n_x * n_y if n_x * n_y <= 32 else n_x
    plane = (size_y, size_z)
    wide_x = size_x + 2 * DEPTH
    dma = pltpu.SemaphoreType.DMA

    def f32(*shape):
        return pltpu.VMEM(shape, jnp.float32)

    held = [pltpu.VMEM(args[k].shape, args[k].dtype) for k in (0, 1, 2, 7) + tuple(range(8, 18))]
    held += [f32(4, wide_x, *plane), f32(ITERS + 1, 2, wide_x, *plane)]
    tiles = size_x // 2
    along = DEPTH * size_y
    ruler = 2 * (2 * 5 * along + 2 * 3 * size_y) + 4 * 5 * along // 2
    ruler += n_x * segs * (packed + wide) // 128 + 2 * n_y + joined
    scratch = [
        f32(3, size_x, *plane),
        f32(6, 2, wide_x, *plane),
        f32(n_x, segs, packed),
        f32(n_y, 1, 128),
        f32(n_x, folded, wide),
        f32(joined, 1, 128),
        f32(n_y, 1, 128),
        f32(2, 4 * tiles, *plane),
        f32(2, 2 * wide_x, *plane),
        f32(2, tiles, *plane),
        f32(2, wide_x // 2, *plane),
        f32(4, 3, *plane),
        f32(4, 3, *plane),
        f32(ruler, 1, 128),
        dma((18,)),
        dma((1,)),
        dma((8,)),
    ]
    vmem = pl.BlockSpec(memory_space=pltpu.VMEM)
    update, answers = pl.pallas_call(
        functools.partial(kernel, n_x, n_y),
        out_shape=(
            pltpu.VMEM(args[0].shape, jnp.float32),
            pltpu.VMEM((slots, segs), jnp.float32),
        ),
        in_specs=[pl.BlockSpec(memory_space=pl.ANY)] * 18,
        out_specs=(vmem, vmem),
        scratch_shapes=held + scratch,
        compiler_params=pltpu.CompilerParams(collective_id=0, has_side_effects=True),
    )(*args)
    update = pltpu.with_memory_space_constraint(update, pltpu.VMEM)
    answers = pltpu.with_memory_space_constraint(answers, pltpu.VMEM)
    any_space = pl.BlockSpec(memory_space=pl.ANY)
    update, answers = pl.pallas_call(
        hand_over,
        out_shape=(
            jax.ShapeDtypeStruct(update.shape, jnp.float32),
            jax.ShapeDtypeStruct(answers.shape, jnp.float32),
        ),
        in_specs=[vmem, vmem],
        out_specs=(any_space, any_space),
        scratch_shapes=[dma((2,))],
    )(update, answers)
    return update, answers.T[:, None, :]


def solution(mesh):
    body = functools.partial(shards, mesh.shape["gx"], mesh.shape["gy"])
    cells = P("gx", "gy", None)
    stacked = P(None, "gx", "gy", None)
    perf = P(("gx", "gy"))
    perf_3 = P(None, ("gx", "gy"))
    segment = P(None, "gy", "gx")
    return jax.shard_map(
        body,
        mesh=mesh,
        in_specs=(stacked, stacked)
        + (cells,) * 5
        + (stacked,)
        + (perf,) * 3
        + (perf_3,) * 2
        + (P("gy", None),)
        + (segment,) * 4,
        out_specs=(stacked, segment),
        check_vma=False,
    )
```

```python
import functools
import math

import jax
import jax.numpy as jnp
from jax import lax
from jax.experimental import pallas as pl
from jax.experimental.pallas import tpu as pltpu
from jax.sharding import PartitionSpec as P

ITERS = 4
MESH = pl.DeviceIdType.MESH
HIGH = lax.Precision.HIGHEST
PAIRS = [(i, j) for i in range(ITERS) for j in range(i, ITERS + 1)]


def iota(shape, dim):
    return lax.broadcasted_iota(jnp.int32, shape, dim)


def dot(a, b, dims, precision=HIGH):
    return lax.dot_general(
        a, b, (dims, ((), ())), precision=precision, preferred_element_type=jnp.float32
    )


def dot_exact(a, pick, dims):
    high = a.astype(jnp.bfloat16)
    rest = a - high.astype(jnp.float32)
    mid = rest.astype(jnp.bfloat16)
    low = (rest - mid.astype(jnp.float32)).astype(jnp.bfloat16)
    parts = [dot(part, pick, dims, None) for part in (high, mid, low)]
    return parts[0] + (parts[1] + parts[2])


def tree(values):
    values = list(values)
    while len(values) > 1:
        pairs = [a + b for a, b in zip(values[::2], values[1::2])]
        values = pairs + values[len(pairs) * 2 :]
    return values[0]


def krylov_coefficients(gram, shift):
    size = ITERS + 1

    def apply(v):
        out = [None] * size

        def put(k, value):
            out[k] = value if out[k] is None else out[k] + value

        for k, value in enumerate(v):
            if value is None:
                continue
            scaled = value * shift
            put(k, scaled)
            if k == 0:
                put(1, scaled)
            else:
                put(k + 1, scaled * 0.5)
                put(k - 1, scaled * 0.5)
        return out

    def inner(a, b):
        total = []
        for j in range(size):
            if b[j] is None:
                continue
            part = [a[i] * gram(i, j) for i in range(size) if a[i] is not None]
            total.append(tree(part) * b[j])
        return tree(total)

    def axpy(a, scale, b):
        out = []
        for p, q in zip(a, b):
            if q is None:
                out.append(p)
            else:
                out.append(scale * q if p is None else p + scale * q)
        return out

    one = jnp.ones_like(shift)
    residual = [one] + [None] * ITERS
    direction = list(residual)
    answer = [None] * size
    norm = gram(0, 0)
    for iteration in range(ITERS):
        image = apply(direction)
        bottom = inner(direction, image)
        alpha = jnp.where(bottom > 0, norm / bottom, 0.0)
        answer = axpy(answer, alpha, direction)
        if iteration == ITERS - 1:
            break
        residual = axpy(residual, -alpha, image)
        new = inner(residual, residual)
        beta = jnp.where(norm > 0, new / norm, 0.0)
        direction = axpy(residual, beta, direction)
        norm = new
    return answer[:ITERS]


DEPTH = ITERS
ORDER = (0, 3, 2, 1)
SHIFT = 2.3
SENDS = [(1, 0), (-1, 0), (0, 1), (0, -1), (1, 1), (-1, 1), (1, -1), (-1, -1)]
FACES = [(1, 0), (-1, 0), (0, 1), (0, -1)]
HELD = 16


def kernel(n_x, n_y, *refs):
    inputs, (upd, wout) = refs[:18], refs[18:20]
    held, scratch = refs[20 : 20 + HELD], refs[20 + HELD :]
    adj, jac, active, weights, pcell, pwell, pseg, pin, pout, owner = held[:10]
    wrhs, sdiag, soff, spar, ext, pext = held[10:]
    (cres, coef, ctab, ftab, gtab, gtabg, cpack, crecv, ppack, precv) = scratch[:10]
    ustage, uhalo, ruler, in_sem, sent_sem, got_sem = scratch[10:]
    c_sem, f_sem, g_sem, gg_sem, t_sem, u_sem, v_sem = [got_sem.at[i] for i in range(7)]

    ix = lax.axis_index("gx")
    iy = lax.axis_index("gy")
    size_x, size_y, size_z = adj.shape[1:]
    planes = range(size_x)
    wide_x = size_x + 2 * DEPTH
    own = slice(DEPTH, DEPTH + size_x)
    half = size_y // 2
    tiles = size_x // 2
    edge = DEPTH // 2
    perfs = pcell.shape[1]
    slots, segs = wrhs.shape
    wells = owner.shape[1]
    wide = -(-wells // 128) * 128
    columns = size_x * size_y

    def exists(sx, sy):
        fine = None
        for step, at, count in ((sx, ix, n_x), (sy, iy, n_y)):
            if step:
                one = at < count - 1 if step > 0 else at > 0
                fine = one if fine is None else jnp.logical_and(fine, one)
        return fine

    barrier = pltpu.get_barrier_semaphore()
    everyone = n_x * n_y
    direct = gtab.shape[0] == everyone
    flat = ix * n_y + iy
    for off in range(1, n_x):
        pl.semaphore_signal(
            barrier, inc=1, device_id=(lax.rem(ix + off, n_x), iy), device_id_type=MESH
        )
    for off in range(1, n_y):
        pl.semaphore_signal(
            barrier, inc=1, device_id=(ix, lax.rem(iy + off, n_y)), device_id_type=MESH
        )
    for sx, sy in SENDS[4:]:

        @pl.when(exists(sx, sy))
        def _(sx=sx, sy=sy):
            pl.semaphore_signal(barrier, inc=1, device_id=(ix + sx, iy + sy), device_id_type=MESH)

    places = [
        adj, jac, active, ext.at[1, own], ext.at[2, own], ext.at[3, own], ext.at[0, own],
        weights, pcell, pwell, pseg, pin, pout, owner, wrhs, sdiag, soff, spar,
    ]
    loads_in = [
        pltpu.make_async_copy(src, dst, in_sem.at[i])
        for i, (src, dst) in enumerate(zip(inputs, places))
    ]
    for i in (8, 9, 10, 11, 13, 0, 14, 15, 16, 17, 3, 4, 5, 6, 1, 12, 2, 7):
        loads_in[i].start()

    def spot(sx, sy):
        if sy == 0:
            if sx > 0:
                return slice(size_x, size_x + DEPTH), slice(0, DEPTH)
            return slice(DEPTH, 2 * DEPTH), slice(DEPTH + size_x, wide_x)
        if sx == 0:
            return slice(0, tiles), slice(edge, edge + tiles)
        if sx > 0:
            return slice(tiles - edge, tiles), slice(0, edge)
        return slice(0, edge), slice(edge + tiles, tiles + 2 * edge)

    def halo_refs(sx, sy, coefs):
        src, dst = spot(sx, sy)
        if sy == 0:
            if coefs:
                return ext.at[:, src], ext.at[:, dst]
            return pext.at[0, 0, src], pext.at[0, 0, dst]
        side = 0 if sy > 0 else 1
        if coefs:
            src, dst = slice(0, 4 * tiles), slice(4 * edge, 4 * (edge + tiles))
            return cpack.at[side, src], crecv.at[side, dst]
        return ppack.at[side, src], precv.at[side, dst]

    def corner_parts(sx, sy):
        side = 0 if sy > 0 else 1
        put, got = (4 * (tiles - 1), 4 * (edge - 1)) if sx > 0 else (0, 4 * (edge + tiles))
        third = -2 if sx > 0 else 4 + ORDER[2]
        near = half if sx > 0 else 0
        row = half - 1 if sy > 0 else 0
        spans = [
            (0, 4, near, half),
            (0, 4, half - near + (half - 2 if sy > 0 else 0), 2),
            (third, 2, near + row, 1),
        ]
        return [
            (
                cpack.at[side, put + at : put + at + count, first : first + span],
                crecv.at[side, got + at : got + at + count, first : first + span],
            )
            for at, count, first, span in spans
        ]

    for d, (sx, sy) in enumerate(SENDS):

        @pl.when(jnp.logical_not(exists(-sx, -sy)))
        def _(d=d, sx=sx, sy=sy):
            targets = [halo_refs(sx, sy, False)[1]]
            targets += [r for _, r in corner_parts(sx, sy)] if d > 3 else [halo_refs(sx, sy, True)[1]]
            for ref in targets:
                ref[...] = jnp.zeros(ref.shape, jnp.float32)
            if d < 4:
                uhalo[d] = jnp.zeros(uhalo.shape[1:], jnp.float32)

    def message(sx, sy, src, dst, rsem):
        def copy():
            return pltpu.make_async_remote_copy(
                src_ref=src,
                dst_ref=dst,
                send_sem=sent_sem.at[0],
                recv_sem=rsem,
                device_id=(ix + sx, iy + sy),
                device_id_type=MESH,
            )

        def start():
            @pl.when(exists(sx, sy))
            def _():
                copy().start()

        return start

    sides_x = (ix > 0).astype(jnp.int32) + (ix < n_x - 1).astype(jnp.int32)
    sides_y = (iy > 0).astype(jnp.int32) + (iy < n_y - 1).astype(jnp.int32)

    def rows_of(ref):
        return math.prod(ref.shape) // 128

    def wait_rows(count, sem):
        part = ruler.at[pl.ds(0, count)]
        pltpu.make_async_copy(part, part, sem).wait()

    def wait_sides(refs, sem):
        along_x, along_y, corner = [
            sum(rows_of(r) for r in refs[d]) if d < len(refs) else 0 for d in (0, 2, 4)
        ]
        for a in (1, 2):
            for b in (1, 2):

                @pl.when(jnp.logical_and(sides_x == a, sides_y == b))
                def _(count=a * along_x + b * along_y + a * b * corner):
                    wait_rows(count, sem)

    def gather(table, rsem, axis):
        me, count = ((ix, n_x), (iy, n_y), (flat, everyone))[axis]

        def copy(off):
            if axis == 2:
                peer = off - 1 + (off > me).astype(jnp.int32)
            else:
                peer = lax.rem(me + jnp.where(me < count // 2, count - off, off), count)
            return pltpu.make_async_remote_copy(
                src_ref=table.at[me],
                dst_ref=table.at[me],
                send_sem=sent_sem.at[0],
                recv_sem=rsem,
                device_id=(
                    (peer, iy),
                    (ix, peer),
                    (lax.div(peer, n_y), lax.rem(peer, n_y)),
                )[axis],
                device_id_type=MESH,
            )

        def start():
            for off in range(1, count):
                copy(off).start()

        def wait():
            wait_rows((count - 1) * rows_of(table.at[0]), rsem)

        return start, wait

    t_refs = [[halo_refs(sx, sy, True)[1]] for sx, sy in FACES]
    t_refs += [[dst for _, dst in corner_parts(sx, sy)] for sx, sy in SENDS[4:]]
    v_refs = [[halo_refs(sx, sy, False)[1]] for sx, sy in SENDS]
    u_refs = [[uhalo.at[d]] for d in range(4)]
    c_ops = gather(ctab, c_sem, 0)
    f_ops = gather(ftab, f_sem, 0)
    g_ops = gather(gtab, g_sem, 2 if direct else 0)
    gg_ops = gather(gtabg, gg_sem, 1)
    t_ops = [message(sx, sy, *halo_refs(sx, sy, True), t_sem) for sx, sy in FACES]
    t_ops += [
        message(sx, sy, src, dst, t_sem) for sx, sy in SENDS[4:] for src, dst in corner_parts(sx, sy)
    ]
    v_ops = [
        message(sx, sy, *halo_refs(sx, sy, False), v_sem)
        for d, (sx, sy) in enumerate(SENDS)
    ]
    u_ops = [
        message(sx, sy, ustage.at[d], uhalo.at[d], u_sem)
        for d, (sx, sy) in enumerate(FACES)
    ]
    rows = iota((size_y, size_z), 0)
    lanes = iota((size_y, size_z), 1)
    low = rows < half

    for i in (8, 9, 10, 11, 13, 0, 14):
        loads_in[i].wait()
    cell = pcell[...]
    cell_col = lax.shift_right_logical(cell, size_z.bit_length() - 1)
    cell_z = cell & (size_z - 1)
    one_z = (iota((size_z, perfs), 0) == cell_z).astype(jnp.bfloat16)
    one_col = (iota((columns, perfs), 0) == cell_col).astype(jnp.float32)
    one_seg = (iota((segs, perfs), 0) == pseg[...]).astype(jnp.float32)
    one_well = (iota((wells, perfs), 0) == pwell[...]).astype(jnp.bfloat16)
    moves = (iota((wide, wells), 0) == owner[...]).astype(jnp.bfloat16)
    one_slot = dot(moves, one_well, ((1,), (0,)), None).astype(jnp.bfloat16)
    picked = dot_exact(adj[...].reshape(3 * columns, size_z), one_z, ((1,), (0,)))
    flux = None
    for m in range(3):
        part = jnp.sum(picked[m * columns : (m + 1) * columns] * one_col, axis=0, keepdims=True)
        part = part * pin[m : m + 1, :]
        flux = part if flux is None else flux + part
    loads = dot_exact(one_seg * flux, one_slot, ((1,), (1,)))
    slot_no = iota((slots, wide), 0) + ix * slots
    mine = (iota((slots, wide), 1) == slot_no).astype(jnp.float32)
    loads = loads + dot(wrhs[...], mine, ((0,), (0,)))
    folded = ftab.shape[1] < segs
    if folded:
        loads = loads[: segs // 2] + pltpu.roll(loads[segs // 2 :], 64, 1)
    ftab[ix] = loads

    for i in (15, 16, 17, 3, 4, 5, 6):
        loads_in[i].wait()
    packed = ctab.shape[2]
    lane_no = iota((slots, packed), 1)
    first = iota((slots, packed), 0) + ix * slots
    table = None
    for no, ref in enumerate((sdiag, soff, spar)):
        here = (lane_no == first + no * wells).astype(jnp.float32)
        part = dot(ref[...].astype(jnp.float32), here, ((0,), (0,)))
        table = part if table is None else table + part
    ctab[ix] = table

    def pack(read, write):
        for i in range(tiles):
            even, odd = read(2 * i), read(2 * i + 1)
            write(0, i, jnp.where(low, pltpu.roll(even, half, 0), odd))
            write(1, i, jnp.where(low, even, pltpu.roll(odd, half, 0)))

    def unpack(north, south):
        north_r, south_r = pltpu.roll(north, half, 0), pltpu.roll(south, half, 0)
        return jnp.where(low, north, south_r), jnp.where(low, north_r, south)

    loads_in[1].wait()

    def product(k, x):
        vector = [adj[m, x] for m in range(3)]
        return [
            tree(jac[9 * k + 3 * m + n, x].astype(jnp.float32) * vector[m] for m in range(3))
            for n in range(3)
        ]

    for n, value in enumerate(product(1, size_x - 1)):
        ustage[0, n] = value
    for n, value in enumerate(product(2, 0)):
        ustage[1, n] = value
    for x in planes:
        for n, value in enumerate(product(3, x)):
            ustage[2, n, x : x + 1, :] = value[size_y - 1 : size_y]
            cres[n, x] = jnp.where(rows == 0, 0.0, pltpu.roll(value, 1, 0))
    for x in planes:
        for n, value in enumerate(product(4, x)):
            ustage[3, n, x : x + 1, :] = value[0:1]
            cres[n, x] += jnp.where(rows == size_y - 1, 0.0, pltpu.roll(value, size_y - 1, 0))

    for f in range(4):

        def put(side, i, value, f=f):
            cpack[side, 4 * i + ORDER[f]] = value

        pack(lambda x, f=f: ext[f, x + DEPTH], put)
    diagonals = [exists(sx, sy).astype(jnp.int32) for sx, sy in SENDS[4:]]
    pl.semaphore_wait(barrier, n_x - 1 + n_y - 1 + sum(diagonals[1:], diagonals[0]))
    f_ops[0]()
    for op in u_ops:
        op()
    c_ops[0]()
    for op in t_ops:
        op()

    for x in planes:
        groups = [product(0, x)]
        if x > 0:
            groups.append(product(1, x - 1))
        if x < size_x - 1:
            groups.append(product(2, x + 1))
        above = product(5, x)
        groups.append([jnp.where(lanes == 0, 0.0, pltpu.roll(v, 1, 1)) for v in above])
        below = product(6, x)
        groups.append(
            [jnp.where(lanes == size_z - 1, 0.0, pltpu.roll(v, size_z - 1, 1)) for v in below]
        )
        for n in range(3):
            cres[n, x] += tree(group[n] for group in groups)

    c_ops[1]()
    total = tree(ctab[i] for i in range(n_x))

    def constant(no):
        if wells % 128 == 0:
            return total[:, no * wells : (no + 1) * wells]
        return total if no == 0 else pltpu.roll(total, 128 - no * wells, 1)

    used = iota((segs, wide), 1) < wells
    diag = jnp.where(used, constant(0), 1.0)
    ratio = jnp.where(used, constant(1), 0.0) / diag
    parent = jnp.where(used, constant(2), 0.0)
    levels = iota((segs, wide), 0).astype(jnp.float32)
    steps = [
        jnp.where(levels == parent[s : s + 1], ratio[s : s + 1], 0.0) for s in range(1, segs)
    ]
    for i in (12, 2, 7):
        loads_in[i].wait()

    f_ops[1]()
    load = tree(ftab[i] for i in range(n_x))
    if folded:
        load = jnp.concatenate([load, pltpu.roll(load, 64, 1)], axis=0)
    for s in range(segs - 1, 0, -1):
        load = load + load[s : s + 1] * steps[s - 1]
    answers = load / diag
    values = dot_exact(answers, one_slot, ((1,), (0,)))
    values = jnp.sum(values * one_seg, axis=0, keepdims=True)
    spread = jnp.concatenate([one_col * (pout[n : n + 1, :] * values) for n in range(3)], axis=0)
    added = dot_exact(spread, one_z, ((1,), (1,)))

    wait_sides(u_refs, u_sem)
    for x in planes:
        live = active[x].astype(jnp.float32)
        rhs = None
        for n in range(3):
            row = n * columns + x * size_y
            value = cres[n, x] + added[row : row + size_y]
            if x == 0:
                value = value + uhalo[0, n]
            if x == size_x - 1:
                value = value + uhalo[1, n]
            value = value + jnp.where(rows == 0, uhalo[2, n, x : x + 1, :], 0.0)
            value = value + jnp.where(rows == size_y - 1, uhalo[3, n, x : x + 1, :], 0.0)
            value = value * live
            upd[n, x] = value
            part = weights[n, x] * value
            rhs = part if rhs is None else rhs + part
        pext[0, 0, x + DEPTH] = rhs

    def put_p(side, i, value):
        ppack[side, i] = value

    pack(lambda x: pext[0, 0, x + DEPTH], put_p)
    for op in v_ops:
        op()

    wout[...] = dot(mine, answers, ((1,), (1,)))
    shift = jnp.full((1, size_z), SHIFT, jnp.float32)
    inverse = 1.0 / SHIFT
    wait_sides(t_refs, t_sem)
    last_x = (ix == n_x - 1).astype(jnp.int32)
    last_y = (iy == n_y - 1).astype(jnp.int32)
    last_row = rows == jnp.where(last_y == 1, size_y - 1, size_y)
    keep_x = 1.0 - last_x.astype(jnp.float32)

    def following(a, b):
        a, b = pltpu.roll(a, size_y - 1, 0), pltpu.roll(b, size_y - 1, 0)
        return jnp.where(rows == size_y - 1, b, a), jnp.where(rows == size_y - 1, a, b)

    def preceding(a, b):
        a, b = pltpu.roll(a, 1, 0), pltpu.roll(b, 1, 0)
        return jnp.where(rows == 0, b, a), jnp.where(rows == 0, a, b)

    raw_x = None
    for i in range(wide_x // 2):
        both = [unpack(crecv[1, 4 * i + f], crecv[0, 4 * i + f]) for f in ORDER]
        for odd in range(2):
            j = 2 * i + odd
            parts = [(ext[f, j], both[f][odd]) for f in range(4)]
            south_raw = preceding(*parts[2])
            north = (jnp.where(last_row, 0.0, parts[2][0]), parts[2][1])
            south = preceding(*north)
            for h in range(2):
                here_x = parts[1][h]
                inside = jnp.where(lanes == size_z - 1, 0.0, parts[3][h])
                under = pltpu.roll(inside, 1, 1)
                if j > 0:
                    full = tree(
                        [
                            parts[0][h] + here_x,
                            raw_x[h] + parts[2][h],
                            south_raw[h] + parts[3][h],
                            under,
                        ]
                    )
                    coef[0, h, j] = full * inverse - 1.0
                east = here_x * inverse
                coef[1, h, j] = east * keep_x if j == DEPTH + size_x - 1 else east
                coef[2, h, j] = north[h] * inverse
                coef[3, h, j] = south[h] * inverse
                coef[4, h, j] = inside * inverse
                coef[5, h, j] = under * inverse
            raw_x = (parts[1][0], parts[1][1])

    wait_sides(v_refs, v_sem)
    for i in range(wide_x // 2):
        pair = unpack(precv[1, i], precv[0, i])
        pext[0, 1, 2 * i] = pair[0]
        pext[0, 1, 2 * i + 1] = pair[1]

    for k in range(ITERS):
        final = k == ITERS - 1
        for j in range(k + 1, wide_x - k - 1):
            here = (pext[k, 0, j], pext[k, 1, j])
            up = following(*here)
            down = preceding(*here)
            for h in range(1 if final else 2):
                image = coef[0, h, j] * here[h] - tree(
                    [
                        coef[1, h, j] * pext[k, h, j + 1],
                        coef[1, h, j - 1] * pext[k, h, j - 1],
                        coef[2, h, j] * up[h],
                        coef[3, h, j] * down[h],
                        coef[4, h, j] * pltpu.roll(here[h], size_z - 1, 1),
                        coef[5, h, j] * pltpu.roll(here[h], 1, 1),
                    ]
                )
                pext[k + 1, h, j] = image if k == 0 else 2.0 * image - pext[k - 1, h, j]

    def mine_of(k, x):
        return pext[k, 0, x + DEPTH]

    count = 16
    grams = [
        jnp.sum(tree(mine_of(i, x) * mine_of(j, x) for x in planes), axis=0, keepdims=True)
        for i, j in PAIRS
    ]
    grams += [jnp.zeros((1, size_z), jnp.float32)] * (count - len(PAIRS))
    column = jnp.sum(jnp.concatenate(grams, axis=0), axis=1, keepdims=True)
    on_lane = iota((count, 128), 0) == iota((count, 128), 1)
    entries = jnp.sum(jnp.where(on_lane, column, 0.0), axis=0, keepdims=True)
    gtab[flat if direct else ix] = entries
    g_ops[0]()
    g_ops[1]()
    sums = tree(gtab[i] for i in range(gtab.shape[0]))
    if not direct:
        gtabg[iy] = sums
        gg_ops[0]()
        gg_ops[1]()
        sums = tree(gtabg[i] for i in range(n_y))
    sums = jnp.sum(jnp.where(on_lane, sums, 0.0), axis=1, keepdims=True)
    sums = jnp.broadcast_to(sums, (count, size_z))

    def gram(i, j):
        row = PAIRS.index((min(i, j), max(i, j)))
        return sums[row : row + 1]

    answer = krylov_coefficients(gram, shift)
    for x in planes:
        pressure = tree(answer[k] * mine_of(k, x) for k in range(ITERS))
        for n in range(3):
            upd[n, x] += weights[n, x] * pressure

    sent_rows = sum(
        (count - 1) * rows_of(table.at[0])
        for table, count in (
            (ctab, n_x), (ftab, n_x), (gtab, gtab.shape[0]), (gtabg, 1 if direct else n_y),
        )
    )
    shapes = [t + v + (u_refs[d] if d < 4 else []) for d, (t, v) in enumerate(zip(t_refs, v_refs))]
    along_x, along_y, corner = [sum(rows_of(r) for r in shapes[d]) for d in (0, 2, 4)]
    for a in (1, 2):
        for b in (1, 2):

            @pl.when(jnp.logical_and(sides_x == a, sides_y == b))
            def _(count=a * along_x + b * along_y + a * b * corner + sent_rows):
                wait_rows(count, sent_sem.at[0])


def hand_over(update, answers, update_out, answers_out, sems):
    copies = [
        pltpu.make_async_copy(update, update_out, sems.at[0]),
        pltpu.make_async_copy(answers, answers_out, sems.at[1]),
    ]
    for copy in copies:
        copy.start()
    for copy in copies:
        copy.wait()


def shards(n_x, n_y, *args):
    args = list(args)
    size_x, size_y, size_z = args[0].shape[1:]
    for k in (8, 9, 10):
        args[k] = args[k][None]
    for k in (14, 15, 16, 17):
        args[k] = args[k][:, 0, :].T
    slots, segs = args[14].shape
    wells = args[13].shape[1]
    wide = -(-wells // 128) * 128
    packed = -(-3 * wells // 128) * 128
    folded = segs // 2 if wells <= 64 and segs == 16 else segs
    joined = n_x * n_y if n_x * n_y <= 32 else n_x
    plane = (size_y, size_z)
    wide_x = size_x + 2 * DEPTH
    dma = pltpu.SemaphoreType.DMA

    def f32(*shape):
        return pltpu.VMEM(shape, jnp.float32)

    held = [pltpu.VMEM(args[k].shape, args[k].dtype) for k in (0, 1, 2, 7) + tuple(range(8, 18))]
    held += [f32(4, wide_x, *plane), f32(ITERS + 1, 2, wide_x, *plane)]
    tiles = size_x // 2
    along = DEPTH * size_y
    ruler = 2 * (2 * 5 * along + 2 * 3 * size_y) + 4 * 5 * along // 2
    ruler += n_x * segs * (packed + wide) // 128 + 2 * n_y + joined
    scratch = [
        f32(3, size_x, *plane),
        f32(6, 2, wide_x, *plane),
        f32(n_x, segs, packed),
        f32(n_x, folded, wide),
        f32(joined, 1, 128),
        f32(n_y, 1, 128),
        f32(2, 4 * tiles, *plane),
        f32(2, 2 * wide_x, *plane),
        f32(2, tiles, *plane),
        f32(2, wide_x // 2, *plane),
        f32(4, 3, *plane),
        f32(4, 3, *plane),
        f32(ruler, 1, 128),
        dma((18,)),
        dma((1,)),
        dma((7,)),
    ]
    vmem = pl.BlockSpec(memory_space=pltpu.VMEM)
    update, answers = pl.pallas_call(
        functools.partial(kernel, n_x, n_y),
        out_shape=(
            pltpu.VMEM(args[0].shape, jnp.float32),
            pltpu.VMEM((slots, segs), jnp.float32),
        ),
        in_specs=[pl.BlockSpec(memory_space=pl.ANY)] * 18,
        out_specs=(vmem, vmem),
        scratch_shapes=held + scratch,
        compiler_params=pltpu.CompilerParams(collective_id=0, has_side_effects=True),
    )(*args)
    update = pltpu.with_memory_space_constraint(update, pltpu.VMEM)
    answers = pltpu.with_memory_space_constraint(answers, pltpu.VMEM)
    any_space = pl.BlockSpec(memory_space=pl.ANY)
    update, answers = pl.pallas_call(
        hand_over,
        out_shape=(
            jax.ShapeDtypeStruct(update.shape, jnp.float32),
            jax.ShapeDtypeStruct(answers.shape, jnp.float32),
        ),
        in_specs=[vmem, vmem],
        out_specs=(any_space, any_space),
        scratch_shapes=[dma((2,))],
    )(update, answers)
    return update, answers.T[:, None, :]


def solution(mesh):
    body = functools.partial(shards, mesh.shape["gx"], mesh.shape["gy"])
    cells = P("gx", "gy", None)
    stacked = P(None, "gx", "gy", None)
    perf = P(("gx", "gy"))
    perf_3 = P(None, ("gx", "gy"))
    segment = P(None, "gy", "gx")
    return jax.shard_map(
        body,
        mesh=mesh,
        in_specs=(stacked, stacked)
        + (cells,) * 5
        + (stacked,)
        + (perf,) * 3
        + (perf_3,) * 2
        + (P("gy", None),)
        + (segment,) * 4,
        out_specs=(stacked, segment),
        check_vma=False,
    )
```

```python
import functools
import math

import jax
import jax.numpy as jnp
from jax import lax
from jax.experimental import pallas as pl
from jax.experimental.pallas import tpu as pltpu
from jax.sharding import PartitionSpec as P

ITERS = 4
MESH = pl.DeviceIdType.MESH
HIGH = lax.Precision.HIGHEST
PAIRS = [(i, j) for i in range(ITERS) for j in range(i, ITERS + 1)]


def iota(shape, dim):
    return lax.broadcasted_iota(jnp.int32, shape, dim)


def dot(a, b, dims, precision=HIGH):
    return lax.dot_general(
        a, b, (dims, ((), ())), precision=precision, preferred_element_type=jnp.float32
    )


def dot_exact(a, pick, dims):
    high = a.astype(jnp.bfloat16)
    rest = a - high.astype(jnp.float32)
    mid = rest.astype(jnp.bfloat16)
    low = (rest - mid.astype(jnp.float32)).astype(jnp.bfloat16)
    parts = [dot(part, pick, dims, None) for part in (high, mid, low)]
    return parts[0] + (parts[1] + parts[2])


def tree(values):
    values = list(values)
    while len(values) > 1:
        pairs = [a + b for a, b in zip(values[::2], values[1::2])]
        values = pairs + values[len(pairs) * 2 :]
    return values[0]


def krylov_coefficients(gram, shift):
    size = ITERS + 1

    def apply(v):
        out = [None] * size

        def put(k, value):
            out[k] = value if out[k] is None else out[k] + value

        for k, value in enumerate(v):
            if value is None:
                continue
            scaled = value * shift
            put(k, scaled)
            if k == 0:
                put(1, scaled)
            else:
                put(k + 1, scaled * 0.5)
                put(k - 1, scaled * 0.5)
        return out

    def inner(a, b):
        total = []
        for j in range(size):
            if b[j] is None:
                continue
            part = [a[i] * gram(i, j) for i in range(size) if a[i] is not None]
            total.append(tree(part) * b[j])
        return tree(total)

    def axpy(a, scale, b):
        out = []
        for p, q in zip(a, b):
            if q is None:
                out.append(p)
            else:
                out.append(scale * q if p is None else p + scale * q)
        return out

    one = jnp.ones_like(shift)
    residual = [one] + [None] * ITERS
    direction = list(residual)
    answer = [None] * size
    norm = gram(0, 0)
    for iteration in range(ITERS):
        image = apply(direction)
        bottom = inner(direction, image)
        alpha = jnp.where(bottom > 0, norm / bottom, 0.0)
        answer = axpy(answer, alpha, direction)
        if iteration == ITERS - 1:
            break
        residual = axpy(residual, -alpha, image)
        new = inner(residual, residual)
        beta = jnp.where(norm > 0, new / norm, 0.0)
        direction = axpy(residual, beta, direction)
        norm = new
    return answer[:ITERS]


DEPTH = ITERS
ORDER = (0, 3, 2, 1)
SHIFT = 2.3
SENDS = [(1, 0), (-1, 0), (0, 1), (0, -1), (1, 1), (-1, 1), (1, -1), (-1, -1)]
FACES = [(1, 0), (-1, 0), (0, 1), (0, -1)]
HELD = 12
LOAD_SEM = (0, 1, 2, 3, 3, 3, 3, 4, 5, 5, 5, 6, 7, 8, 9, 9, 9, 10)


def kernel(n_x, n_y, *refs):
    inputs, (upd, wout) = refs[:18], refs[18:20]
    held, scratch = refs[20 : 20 + HELD], refs[20 + HELD :]
    adj, jac, active, weights, places_of, pin, pout, owner, tables, spar, ext, pext = held
    pcell, pwell, pseg = [places_of.at[i] for i in range(3)]
    wrhs, sdiag, soff = [tables.at[i] for i in range(3)]
    (cres, coef, ftab, gtab, gtabg, cpack, crecv, ppack, precv) = scratch[:9]
    ustage, uhalo, ruler, in_sem, sent_sem, got_sem = scratch[9:]
    f_sem, g_sem, gg_sem, t_sem, u_sem, v_sem = [got_sem.at[i] for i in range(6)]

    ix = lax.axis_index("gx")
    iy = lax.axis_index("gy")
    size_x, size_y, size_z = adj.shape[1:]
    planes = range(size_x)
    wide_x = size_x + 2 * DEPTH
    own = slice(DEPTH, DEPTH + size_x)
    half = size_y // 2
    tiles = size_x // 2
    edge = DEPTH // 2
    perfs = pcell.shape[1]
    slots, segs = wrhs.shape
    wells = owner.shape[1]
    wide = -(-wells // 128) * 128
    columns = size_x * size_y

    def exists(sx, sy):
        fine = None
        for step, at, count in ((sx, ix, n_x), (sy, iy, n_y)):
            if step:
                one = at < count - 1 if step > 0 else at > 0
                fine = one if fine is None else jnp.logical_and(fine, one)
        return fine

    barrier = pltpu.get_barrier_semaphore()
    everyone = n_x * n_y
    direct = gtab.shape[0] == everyone
    flat = ix * n_y + iy
    for off in range(1, n_x):
        pl.semaphore_signal(
            barrier, inc=1, device_id=(lax.rem(ix + off, n_x), iy), device_id_type=MESH
        )
    for off in range(1, n_y):
        pl.semaphore_signal(
            barrier, inc=1, device_id=(ix, lax.rem(iy + off, n_y)), device_id_type=MESH
        )
    for sx, sy in SENDS[4:]:

        @pl.when(exists(sx, sy))
        def _(sx=sx, sy=sy):
            pl.semaphore_signal(barrier, inc=1, device_id=(ix + sx, iy + sy), device_id_type=MESH)

    places = [
        adj, jac, active, ext.at[1, own], ext.at[2, own], ext.at[3, own], ext.at[0, own],
        weights, pcell, pwell, pseg, pin, pout, owner, wrhs, sdiag, soff, spar,
    ]
    loads_in = [
        pltpu.make_async_copy(src, dst, in_sem.at[LOAD_SEM[i]])
        for i, (src, dst) in enumerate(zip(inputs, places))
    ]
    for i in (8, 9, 10, 11, 13, 0, 14, 15, 16, 17, 3, 4, 5, 6, 1, 12, 2, 7):
        loads_in[i].start()

    def spot(sx, sy):
        if sy == 0:
            if sx > 0:
                return slice(size_x, size_x + DEPTH), slice(0, DEPTH)
            return slice(DEPTH, 2 * DEPTH), slice(DEPTH + size_x, wide_x)
        if sx == 0:
            return slice(0, tiles), slice(edge, edge + tiles)
        if sx > 0:
            return slice(tiles - edge, tiles), slice(0, edge)
        return slice(0, edge), slice(edge + tiles, tiles + 2 * edge)

    def halo_refs(sx, sy, coefs):
        src, dst = spot(sx, sy)
        if sy == 0:
            if coefs:
                return ext.at[:, src], ext.at[:, dst]
            return pext.at[0, 0, src], pext.at[0, 0, dst]
        side = 0 if sy > 0 else 1
        if coefs:
            src, dst = slice(0, 4 * tiles), slice(4 * edge, 4 * (edge + tiles))
            return cpack.at[side, src], crecv.at[side, dst]
        return ppack.at[side, src], precv.at[side, dst]

    def corner_parts(sx, sy):
        side = 0 if sy > 0 else 1
        put, got = (4 * (tiles - 1), 4 * (edge - 1)) if sx > 0 else (0, 4 * (edge + tiles))
        third = -2 if sx > 0 else 4 + ORDER[2]
        near = half if sx > 0 else 0
        row = half - 1 if sy > 0 else 0
        spans = [
            (0, 4, near, half),
            (0, 4, half - near + (half - 2 if sy > 0 else 0), 2),
            (third, 2, near + row, 1),
        ]
        return [
            (
                cpack.at[side, put + at : put + at + count, first : first + span],
                crecv.at[side, got + at : got + at + count, first : first + span],
            )
            for at, count, first, span in spans
        ]

    for d, (sx, sy) in enumerate(SENDS):

        @pl.when(jnp.logical_not(exists(-sx, -sy)))
        def _(d=d, sx=sx, sy=sy):
            targets = [halo_refs(sx, sy, False)[1]]
            targets += [r for _, r in corner_parts(sx, sy)] if d > 3 else [halo_refs(sx, sy, True)[1]]
            for ref in targets:
                ref[...] = jnp.zeros(ref.shape, jnp.float32)
            if d < 4:
                uhalo[d] = jnp.zeros(uhalo.shape[1:], jnp.float32)

    def message(sx, sy, src, dst, rsem):
        def copy():
            return pltpu.make_async_remote_copy(
                src_ref=src,
                dst_ref=dst,
                send_sem=sent_sem.at[0],
                recv_sem=rsem,
                device_id=(ix + sx, iy + sy),
                device_id_type=MESH,
            )

        def start():
            @pl.when(exists(sx, sy))
            def _():
                copy().start()

        return start

    sides_x = (ix > 0).astype(jnp.int32) + (ix < n_x - 1).astype(jnp.int32)
    sides_y = (iy > 0).astype(jnp.int32) + (iy < n_y - 1).astype(jnp.int32)

    def rows_of(ref):
        return math.prod(ref.shape) // 128

    def wait_rows(count, sem):
        part = ruler.at[pl.ds(0, count)]
        pltpu.make_async_copy(part, part, sem).wait()

    def wait_sides(refs, sem):
        along_x, along_y, corner = [
            sum(rows_of(r) for r in refs[d]) if d < len(refs) else 0 for d in (0, 2, 4)
        ]
        for a in (1, 2):
            for b in (1, 2):

                @pl.when(jnp.logical_and(sides_x == a, sides_y == b))
                def _(count=a * along_x + b * along_y + a * b * corner):
                    wait_rows(count, sem)

    def gather(table, rsem, axis):
        me, count = ((ix, n_x), (iy, n_y), (flat, everyone))[axis]

        def copy(off):
            if axis == 2:
                peer = off - 1 + (off > me).astype(jnp.int32)
            else:
                peer = lax.rem(me + jnp.where(me < count // 2, count - off, off), count)
            return pltpu.make_async_remote_copy(
                src_ref=table.at[me],
                dst_ref=table.at[me],
                send_sem=sent_sem.at[0],
                recv_sem=rsem,
                device_id=(
                    (peer, iy),
                    (ix, peer),
                    (lax.div(peer, n_y), lax.rem(peer, n_y)),
                )[axis],
                device_id_type=MESH,
            )

        def start():
            for off in range(1, count):
                copy(off).start()

        def wait():
            wait_rows((count - 1) * rows_of(table.at[0]), rsem)

        return start, wait

    t_refs = [[halo_refs(sx, sy, True)[1]] for sx, sy in FACES]
    t_refs += [[dst for _, dst in corner_parts(sx, sy)] for sx, sy in SENDS[4:]]
    v_refs = [[halo_refs(sx, sy, False)[1]] for sx, sy in SENDS]
    u_refs = [[uhalo.at[d]] for d in range(4)]
    f_ops = gather(ftab, f_sem, 0)
    g_ops = gather(gtab, g_sem, 2 if direct else 0)
    gg_ops = gather(gtabg, gg_sem, 1)
    t_ops = [message(sx, sy, *halo_refs(sx, sy, True), t_sem) for sx, sy in FACES]
    t_ops += [
        message(sx, sy, src, dst, t_sem) for sx, sy in SENDS[4:] for src, dst in corner_parts(sx, sy)
    ]
    v_ops = [
        message(sx, sy, *halo_refs(sx, sy, False), v_sem)
        for d, (sx, sy) in enumerate(SENDS)
    ]
    u_ops = [
        message(sx, sy, ustage.at[d], uhalo.at[d], u_sem)
        for d, (sx, sy) in enumerate(FACES)
    ]
    rows = iota((size_y, size_z), 0)
    lanes = iota((size_y, size_z), 1)
    low = rows < half

    def loaded(i, ref):
        pltpu.make_async_copy(ref, ref, in_sem.at[LOAD_SEM[i]]).wait()

    loaded(8, places_of)
    loaded(14, tables)
    for i in (11, 13, 0):
        loads_in[i].wait()
    cell = pcell[...]
    cell_col = lax.shift_right_logical(cell, size_z.bit_length() - 1)
    cell_z = cell & (size_z - 1)
    one_z = (iota((size_z, perfs), 0) == cell_z).astype(jnp.bfloat16)
    one_col = (iota((columns, perfs), 0) == cell_col).astype(jnp.float32)
    one_seg = (iota((segs, perfs), 0) == pseg[...]).astype(jnp.float32)
    one_well = (iota((wells, perfs), 0) == pwell[...]).astype(jnp.bfloat16)
    moves = (iota((wide, wells), 0) == owner[...]).astype(jnp.bfloat16)
    one_slot = dot(moves, one_well, ((1,), (0,)), None).astype(jnp.bfloat16)
    picked = dot_exact(adj[...].reshape(3 * columns, size_z), one_z, ((1,), (0,)))
    flux = None
    for m in range(3):
        part = jnp.sum(picked[m * columns : (m + 1) * columns] * one_col, axis=0, keepdims=True)
        part = part * pin[m : m + 1, :]
        flux = part if flux is None else flux + part
    loads = dot_exact(one_seg * flux, one_slot, ((1,), (1,)))
    slot_no = iota((slots, wide), 0) + ix * slots
    mine = (iota((slots, wide), 1) == slot_no).astype(jnp.float32)
    loads = loads + dot(wrhs[...], mine, ((0,), (0,)))
    packed = -(-3 * wells // 128) * 128
    blocks = packed // wide
    held_rows = ftab.shape[1] - segs * blocks
    folded = held_rows < segs
    if folded:
        loads = loads[: segs // 2] + pltpu.roll(loads[segs // 2 :], 64, 1)
    ftab[ix, :held_rows] = loads

    loads_in[17].wait()
    loaded(3, ext.at[:, own])
    lane_no = iota((slots, packed), 1)
    first = iota((slots, packed), 0) + ix * slots
    table = None
    for no, ref in enumerate((sdiag, soff, spar)):
        here = (lane_no == first + no * wells).astype(jnp.float32)
        part = dot(ref[...].astype(jnp.float32), here, ((0,), (0,)))
        table = part if table is None else table + part
    for b in range(blocks):
        ftab[ix, held_rows + b * segs : held_rows + (b + 1) * segs] = table[:, b * wide : (b + 1) * wide]

    def pack(read, write):
        for i in range(tiles):
            even, odd = read(2 * i), read(2 * i + 1)
            write(0, i, jnp.where(low, pltpu.roll(even, half, 0), odd))
            write(1, i, jnp.where(low, even, pltpu.roll(odd, half, 0)))

    def unpack(north, south):
        north_r, south_r = pltpu.roll(north, half, 0), pltpu.roll(south, half, 0)
        return jnp.where(low, north, south_r), jnp.where(low, north_r, south)

    loads_in[1].wait()

    def product(k, x):
        vector = [adj[m, x] for m in range(3)]
        return [
            tree(jac[9 * k + 3 * m + n, x].astype(jnp.float32) * vector[m] for m in range(3))
            for n in range(3)
        ]

    for n, value in enumerate(product(1, size_x - 1)):
        ustage[0, n] = value
    for n, value in enumerate(product(2, 0)):
        ustage[1, n] = value
    for x in planes:
        for n, value in enumerate(product(3, x)):
            ustage[2, n, x : x + 1, :] = value[size_y - 1 : size_y]
            cres[n, x] = jnp.where(rows == 0, 0.0, pltpu.roll(value, 1, 0))
    for x in planes:
        for n, value in enumerate(product(4, x)):
            ustage[3, n, x : x + 1, :] = value[0:1]
            cres[n, x] += jnp.where(rows == size_y - 1, 0.0, pltpu.roll(value, size_y - 1, 0))

    for f in range(4):

        def put(side, i, value, f=f):
            cpack[side, 4 * i + ORDER[f]] = value

        pack(lambda x, f=f: ext[f, x + DEPTH], put)
    diagonals = [exists(sx, sy).astype(jnp.int32) for sx, sy in SENDS[4:]]
    pl.semaphore_wait(barrier, n_x - 1 + n_y - 1 + sum(diagonals[1:], diagonals[0]))
    f_ops[0]()
    for op in u_ops:
        op()
    for op in t_ops:
        op()

    for x in planes:
        groups = [product(0, x)]
        if x > 0:
            groups.append(product(1, x - 1))
        if x < size_x - 1:
            groups.append(product(2, x + 1))
        above = product(5, x)
        groups.append([jnp.where(lanes == 0, 0.0, pltpu.roll(v, 1, 1)) for v in above])
        below = product(6, x)
        groups.append(
            [jnp.where(lanes == size_z - 1, 0.0, pltpu.roll(v, size_z - 1, 1)) for v in below]
        )
        for n in range(3):
            cres[n, x] += tree(group[n] for group in groups)

    for i in (12, 2, 7):
        loads_in[i].wait()

    f_ops[1]()
    total = [
        tree(ftab[i, held_rows + b * segs : held_rows + (b + 1) * segs] for i in range(n_x)) for b in range(blocks)
    ]
    total = jnp.concatenate(total, axis=1)

    def constant(no):
        if wells % 128 == 0:
            return total[:, no * wells : (no + 1) * wells]
        return total if no == 0 else pltpu.roll(total, 128 - no * wells, 1)

    used = iota((segs, wide), 1) < wells
    diag = jnp.where(used, constant(0), 1.0)
    ratio = jnp.where(used, constant(1), 0.0) / diag
    parent = jnp.where(used, constant(2), 0.0)
    levels = iota((segs, wide), 0).astype(jnp.float32)
    steps = [
        jnp.where(levels == parent[s : s + 1], ratio[s : s + 1], 0.0) for s in range(1, segs)
    ]
    load = tree(ftab[i, :held_rows] for i in range(n_x))
    if folded:
        load = jnp.concatenate([load, pltpu.roll(load, 64, 1)], axis=0)
    for s in range(segs - 1, 0, -1):
        load = load + load[s : s + 1] * steps[s - 1]
    answers = load / diag
    values = dot_exact(answers, one_slot, ((1,), (0,)))
    values = jnp.sum(values * one_seg, axis=0, keepdims=True)
    spread = jnp.concatenate([one_col * (pout[n : n + 1, :] * values) for n in range(3)], axis=0)
    added = dot_exact(spread, one_z, ((1,), (1,)))

    wait_sides(u_refs, u_sem)
    for x in planes:
        live = active[x].astype(jnp.float32)
        rhs = None
        for n in range(3):
            row = n * columns + x * size_y
            value = cres[n, x] + added[row : row + size_y]
            if x == 0:
                value = value + uhalo[0, n]
            if x == size_x - 1:
                value = value + uhalo[1, n]
            value = value + jnp.where(rows == 0, uhalo[2, n, x : x + 1, :], 0.0)
            value = value + jnp.where(rows == size_y - 1, uhalo[3, n, x : x + 1, :], 0.0)
            value = value * live
            upd[n, x] = value
            part = weights[n, x] * value
            rhs = part if rhs is None else rhs + part
        pext[0, 0, x + DEPTH] = rhs

    def put_p(side, i, value):
        ppack[side, i] = value

    pack(lambda x: pext[0, 0, x + DEPTH], put_p)
    for d in (2, 3, 4, 5, 6, 7, 0, 1):
        v_ops[d]()

    wout[...] = dot(mine, answers, ((1,), (1,)))
    shift = jnp.full((1, size_z), SHIFT, jnp.float32)
    inverse = 1.0 / SHIFT
    wait_sides(t_refs, t_sem)
    last_x = (ix == n_x - 1).astype(jnp.int32)
    last_y = (iy == n_y - 1).astype(jnp.int32)
    last_row = rows == jnp.where(last_y == 1, size_y - 1, size_y)
    keep_x = 1.0 - last_x.astype(jnp.float32)

    def following(a, b):
        a, b = pltpu.roll(a, size_y - 1, 0), pltpu.roll(b, size_y - 1, 0)
        return jnp.where(rows == size_y - 1, b, a), jnp.where(rows == size_y - 1, a, b)

    def preceding(a, b):
        a, b = pltpu.roll(a, 1, 0), pltpu.roll(b, 1, 0)
        return jnp.where(rows == 0, b, a), jnp.where(rows == 0, a, b)

    raw_x = None
    for i in range(wide_x // 2):
        both = [unpack(crecv[1, 4 * i + f], crecv[0, 4 * i + f]) for f in ORDER]
        for odd in range(2):
            j = 2 * i + odd
            parts = [(ext[f, j], both[f][odd]) for f in range(4)]
            south_raw = preceding(*parts[2])
            north = (jnp.where(last_row, 0.0, parts[2][0]), parts[2][1])
            south = preceding(*north)
            for h in range(2):
                here_x = parts[1][h]
                inside = jnp.where(lanes == size_z - 1, 0.0, parts[3][h])
                under = pltpu.roll(inside, 1, 1)
                if j > 0:
                    full = tree(
                        [
                            parts[0][h] + here_x,
                            raw_x[h] + parts[2][h],
                            south_raw[h] + parts[3][h],
                            under,
                        ]
                    )
                    coef[0, h, j] = full * inverse - 1.0
                east = here_x * inverse
                coef[1, h, j] = east * keep_x if j == DEPTH + size_x - 1 else east
                coef[2, h, j] = north[h] * inverse
                coef[3, h, j] = south[h] * inverse
                coef[4, h, j] = inside * inverse
                coef[5, h, j] = under * inverse
            raw_x = (parts[1][0], parts[1][1])

    wait_sides(v_refs, v_sem)
    for i in range(wide_x // 2):
        pair = unpack(precv[1, i], precv[0, i])
        pext[0, 1, 2 * i] = pair[0]
        pext[0, 1, 2 * i + 1] = pair[1]

    for k in range(ITERS):
        final = k == ITERS - 1
        for j in range(k + 1, wide_x - k - 1):
            here = (pext[k, 0, j], pext[k, 1, j])
            up = following(*here)
            down = preceding(*here)
            for h in range(1 if final else 2):
                image = coef[0, h, j] * here[h] - tree(
                    [
                        coef[1, h, j] * pext[k, h, j + 1],
                        coef[1, h, j - 1] * pext[k, h, j - 1],
                        coef[2, h, j] * up[h],
                        coef[3, h, j] * down[h],
                        coef[4, h, j] * pltpu.roll(here[h], size_z - 1, 1),
                        coef[5, h, j] * pltpu.roll(here[h], 1, 1),
                    ]
                )
                pext[k + 1, h, j] = image if k == 0 else 2.0 * image - pext[k - 1, h, j]

    def mine_of(k, x):
        return pext[k, 0, x + DEPTH]

    count = 16
    grams = [
        jnp.sum(tree(mine_of(i, x) * mine_of(j, x) for x in planes), axis=0, keepdims=True)
        for i, j in PAIRS
    ]
    grams += [jnp.zeros((1, size_z), jnp.float32)] * (count - len(PAIRS))
    column = jnp.sum(jnp.concatenate(grams, axis=0), axis=1, keepdims=True)
    on_lane = iota((count, 128), 0) == iota((count, 128), 1)
    entries = jnp.sum(jnp.where(on_lane, column, 0.0), axis=0, keepdims=True)
    gtab[flat if direct else ix] = entries
    g_ops[0]()
    g_ops[1]()
    sums = tree(gtab[i] for i in range(gtab.shape[0]))
    if not direct:
        gtabg[iy] = sums
        gg_ops[0]()
        gg_ops[1]()
        sums = tree(gtabg[i] for i in range(n_y))
    sums = jnp.sum(jnp.where(on_lane, sums, 0.0), axis=1, keepdims=True)
    sums = jnp.broadcast_to(sums, (count, size_z))

    def gram(i, j):
        row = PAIRS.index((min(i, j), max(i, j)))
        return sums[row : row + 1]

    answer = krylov_coefficients(gram, shift)
    for x in planes:
        pressure = tree(answer[k] * mine_of(k, x) for k in range(ITERS))
        for n in range(3):
            upd[n, x] += weights[n, x] * pressure

    sent_rows = sum(
        (count - 1) * rows_of(table.at[0])
        for table, count in (
            (ftab, n_x), (gtab, gtab.shape[0]), (gtabg, 1 if direct else n_y),
        )
    )
    shapes = [t + v + (u_refs[d] if d < 4 else []) for d, (t, v) in enumerate(zip(t_refs, v_refs))]
    along_x, along_y, corner = [sum(rows_of(r) for r in shapes[d]) for d in (0, 2, 4)]
    for a in (1, 2):
        for b in (1, 2):

            @pl.when(jnp.logical_and(sides_x == a, sides_y == b))
            def _(count=a * along_x + b * along_y + a * b * corner + sent_rows):
                wait_rows(count, sent_sem.at[0])


def hand_over(update, answers, update_out, answers_out, sems):
    copies = [
        pltpu.make_async_copy(update, update_out, sems.at[0]),
        pltpu.make_async_copy(answers, answers_out, sems.at[1]),
    ]
    for copy in copies:
        copy.start()
    for copy in copies:
        copy.wait()


def shards(n_x, n_y, *args):
    args = list(args)
    size_x, size_y, size_z = args[0].shape[1:]
    for k in (8, 9, 10):
        args[k] = args[k][None]
    for k in (14, 15, 16, 17):
        args[k] = args[k][:, 0, :].T
    slots, segs = args[14].shape
    wells = args[13].shape[1]
    wide = -(-wells // 128) * 128
    packed = -(-3 * wells // 128) * 128
    folded = segs // 2 if wells <= 64 and segs == 16 else segs
    joined = n_x * n_y if n_x * n_y <= 32 else n_x
    plane = (size_y, size_z)
    wide_x = size_x + 2 * DEPTH
    dma = pltpu.SemaphoreType.DMA

    def f32(*shape):
        return pltpu.VMEM(shape, jnp.float32)

    held = [pltpu.VMEM(args[k].shape, args[k].dtype) for k in (0, 1, 2, 7)]
    held += [pltpu.VMEM((3,) + args[8].shape, jnp.int32)]
    held += [pltpu.VMEM(args[k].shape, args[k].dtype) for k in (11, 12, 13)]
    held += [f32(3, *args[14].shape), pltpu.VMEM(args[17].shape, jnp.int32)]
    held += [f32(4, wide_x, *plane), f32(ITERS + 1, 2, wide_x, *plane)]
    tiles = size_x // 2
    along = DEPTH * size_y
    ruler = 2 * (2 * 5 * along + 2 * 3 * size_y) + 4 * 5 * along // 2
    ruler += n_x * segs * (packed + wide) // 128 + 2 * n_y + joined
    scratch = [
        f32(3, size_x, *plane),
        f32(6, 2, wide_x, *plane),
        f32(n_x, folded + segs * packed // wide, wide),
        f32(joined, 1, 128),
        f32(n_y, 1, 128),
        f32(2, 4 * tiles, *plane),
        f32(2, 2 * wide_x, *plane),
        f32(2, tiles, *plane),
        f32(2, wide_x // 2, *plane),
        f32(4, 3, *plane),
        f32(4, 3, *plane),
        f32(ruler, 1, 128),
        dma((11,)),
        dma((1,)),
        dma((6,)),
    ]
    vmem = pl.BlockSpec(memory_space=pltpu.VMEM)
    update, answers = pl.pallas_call(
        functools.partial(kernel, n_x, n_y),
        out_shape=(
            pltpu.VMEM(args[0].shape, jnp.float32),
            pltpu.VMEM((slots, segs), jnp.float32),
        ),
        in_specs=[pl.BlockSpec(memory_space=pl.ANY)] * 18,
        out_specs=(vmem, vmem),
        scratch_shapes=held + scratch,
        compiler_params=pltpu.CompilerParams(collective_id=0, has_side_effects=True),
    )(*args)
    update = pltpu.with_memory_space_constraint(update, pltpu.VMEM)
    answers = pltpu.with_memory_space_constraint(answers, pltpu.VMEM)
    any_space = pl.BlockSpec(memory_space=pl.ANY)
    update, answers = pl.pallas_call(
        hand_over,
        out_shape=(
            jax.ShapeDtypeStruct(update.shape, jnp.float32),
            jax.ShapeDtypeStruct(answers.shape, jnp.float32),
        ),
        in_specs=[vmem, vmem],
        out_specs=(any_space, any_space),
        scratch_shapes=[dma((2,))],
    )(update, answers)
    return update, answers.T[:, None, :]


def solution(mesh):
    body = functools.partial(shards, mesh.shape["gx"], mesh.shape["gy"])
    cells = P("gx", "gy", None)
    stacked = P(None, "gx", "gy", None)
    perf = P(("gx", "gy"))
    perf_3 = P(None, ("gx", "gy"))
    segment = P(None, "gy", "gx")
    return jax.shard_map(
        body,
        mesh=mesh,
        in_specs=(stacked, stacked)
        + (cells,) * 5
        + (stacked,)
        + (perf,) * 3
        + (perf_3,) * 2
        + (P("gy", None),)
        + (segment,) * 4,
        out_specs=(stacked, segment),
        check_vma=False,
    )
```

```python
import functools
import math

import jax
import jax.numpy as jnp
from jax import lax
from jax.experimental import pallas as pl
from jax.experimental.pallas import tpu as pltpu
from jax.sharding import PartitionSpec as P

ITERS = 4
MESH = pl.DeviceIdType.MESH
HIGH = lax.Precision.HIGHEST
PAIRS = [(i, j) for i in range(ITERS) for j in range(i, ITERS + 1)]


def iota(shape, dim):
    return lax.broadcasted_iota(jnp.int32, shape, dim)


def dot(a, b, dims, precision=HIGH):
    return lax.dot_general(
        a, b, (dims, ((), ())), precision=precision, preferred_element_type=jnp.float32
    )


def dot_exact(a, pick, dims):
    high = a.astype(jnp.bfloat16)
    rest = a - high.astype(jnp.float32)
    mid = rest.astype(jnp.bfloat16)
    low = (rest - mid.astype(jnp.float32)).astype(jnp.bfloat16)
    parts = [dot(part, pick, dims, None) for part in (high, mid, low)]
    return parts[0] + (parts[1] + parts[2])


def tree(values):
    values = list(values)
    while len(values) > 1:
        pairs = [a + b for a, b in zip(values[::2], values[1::2])]
        values = pairs + values[len(pairs) * 2 :]
    return values[0]


def krylov_coefficients(gram, shift):
    size = ITERS + 1

    def apply(v):
        out = [None] * size

        def put(k, value):
            out[k] = value if out[k] is None else out[k] + value

        for k, value in enumerate(v):
            if value is None:
                continue
            scaled = value * shift
            put(k, scaled)
            if k == 0:
                put(1, scaled)
            else:
                put(k + 1, scaled * 0.5)
                put(k - 1, scaled * 0.5)
        return out

    def inner(a, b):
        total = []
        for j in range(size):
            if b[j] is None:
                continue
            part = [a[i] * gram(i, j) for i in range(size) if a[i] is not None]
            total.append(tree(part) * b[j])
        return tree(total)

    def axpy(a, scale, b):
        out = []
        for p, q in zip(a, b):
            if q is None:
                out.append(p)
            else:
                out.append(scale * q if p is None else p + scale * q)
        return out

    one = jnp.ones_like(shift)
    residual = [one] + [None] * ITERS
    direction = list(residual)
    answer = [None] * size
    norm = gram(0, 0)
    for iteration in range(ITERS):
        image = apply(direction)
        bottom = inner(direction, image)
        alpha = jnp.where(bottom > 0, norm / bottom, 0.0)
        answer = axpy(answer, alpha, direction)
        if iteration == ITERS - 1:
            break
        residual = axpy(residual, -alpha, image)
        new = inner(residual, residual)
        beta = jnp.where(norm > 0, new / norm, 0.0)
        direction = axpy(residual, beta, direction)
        norm = new
    return answer[:ITERS]


DEPTH = ITERS
ORDER = (0, 3, 2, 1)
SHIFT = 2.3
SENDS = [(1, 0), (-1, 0), (0, 1), (0, -1), (1, 1), (-1, 1), (1, -1), (-1, -1)]
FACES = [(1, 0), (-1, 0), (0, 1), (0, -1)]
HELD = 12
LOAD_SEM = (0, 1, 2, 3, 3, 3, 3, 4, 5, 5, 5, 6, 7, 8, 9, 9, 9, 10)


def kernel(n_x, n_y, *refs):
    inputs, (upd, wout) = refs[:18], refs[18:20]
    held, scratch = refs[20 : 20 + HELD], refs[20 + HELD :]
    adj, jac, active, weights, places_of, pin, pout, owner, tables, spar, ext, pext = held
    pcell, pwell, pseg = [places_of.at[i] for i in range(3)]
    wrhs, sdiag, soff = [tables.at[i] for i in range(3)]
    (cres, coef, ftab, gtab, gtabg, cpack, crecv, ppack, precv) = scratch[:9]
    ustage, uhalo, ruler, in_sem, sent_sem, got_sem = scratch[9:]
    f_sem, g_sem, gg_sem, t_sem, u_sem, v_sem = [got_sem.at[i] for i in range(6)]

    ix = lax.axis_index("gx")
    iy = lax.axis_index("gy")
    size_x, size_y, size_z = adj.shape[1:]
    planes = range(size_x)
    wide_x = size_x + 2 * DEPTH
    own = slice(DEPTH, DEPTH + size_x)
    half = size_y // 2
    tiles = size_x // 2
    edge = DEPTH // 2
    perfs = pcell.shape[1]
    slots, segs = wrhs.shape
    wells = owner.shape[1]
    wide = -(-wells // 128) * 128
    columns = size_x * size_y

    def exists(sx, sy):
        fine = None
        for step, at, count in ((sx, ix, n_x), (sy, iy, n_y)):
            if step:
                one = at < count - 1 if step > 0 else at > 0
                fine = one if fine is None else jnp.logical_and(fine, one)
        return fine

    barrier = pltpu.get_barrier_semaphore()
    everyone = n_x * n_y
    direct = gtab.shape[0] == everyone
    flat = ix * n_y + iy
    for off in range(1, n_x):
        pl.semaphore_signal(
            barrier, inc=1, device_id=(lax.rem(ix + off, n_x), iy), device_id_type=MESH
        )
    for off in range(1, n_y):
        pl.semaphore_signal(
            barrier, inc=1, device_id=(ix, lax.rem(iy + off, n_y)), device_id_type=MESH
        )
    for sx, sy in SENDS[4:]:

        @pl.when(exists(sx, sy))
        def _(sx=sx, sy=sy):
            pl.semaphore_signal(barrier, inc=1, device_id=(ix + sx, iy + sy), device_id_type=MESH)

    places = [
        adj, jac, active, ext.at[1, own], ext.at[2, own], ext.at[3, own], ext.at[0, own],
        weights, pcell, pwell, pseg, pin, pout, owner, wrhs, sdiag, soff, spar,
    ]
    loads_in = [
        pltpu.make_async_copy(src, dst, in_sem.at[LOAD_SEM[i]])
        for i, (src, dst) in enumerate(zip(inputs, places))
    ]
    for i in (8, 9, 10, 11, 13, 0, 14, 15, 16, 17, 3, 4, 5, 6, 1, 12, 2, 7):
        loads_in[i].start()

    def spot(sx, sy):
        if sy == 0:
            if sx > 0:
                return slice(size_x, size_x + DEPTH), slice(0, DEPTH)
            return slice(DEPTH, 2 * DEPTH), slice(DEPTH + size_x, wide_x)
        if sx == 0:
            return slice(0, tiles), slice(edge, edge + tiles)
        if sx > 0:
            return slice(tiles - edge, tiles), slice(0, edge)
        return slice(0, edge), slice(edge + tiles, tiles + 2 * edge)

    def halo_refs(sx, sy, coefs):
        src, dst = spot(sx, sy)
        if sy == 0:
            if coefs:
                return ext.at[:, src], ext.at[:, dst]
            return pext.at[0, 0, src], pext.at[0, 0, dst]
        side = 0 if sy > 0 else 1
        if coefs:
            src, dst = slice(0, 4 * tiles), slice(4 * edge, 4 * (edge + tiles))
            return cpack.at[side, src], crecv.at[side, dst]
        return ppack.at[side, src], precv.at[side, dst]

    def corner_parts(sx, sy):
        side = 0 if sy > 0 else 1
        put, got = (4 * (tiles - 1), 4 * (edge - 1)) if sx > 0 else (0, 4 * (edge + tiles))
        third = -2 if sx > 0 else 4 + ORDER[2]
        near = half if sx > 0 else 0
        row = half - 1 if sy > 0 else 0
        spans = [
            (0, 4, near, half),
            (0, 4, half - near + (half - 2 if sy > 0 else 0), 2),
            (third, 2, near + row, 1),
        ]
        return [
            (
                cpack.at[side, put + at : put + at + count, first : first + span],
                crecv.at[side, got + at : got + at + count, first : first + span],
            )
            for at, count, first, span in spans
        ]

    for d, (sx, sy) in enumerate(SENDS):

        @pl.when(jnp.logical_not(exists(-sx, -sy)))
        def _(d=d, sx=sx, sy=sy):
            targets = [halo_refs(sx, sy, False)[1]]
            targets += [r for _, r in corner_parts(sx, sy)] if d > 3 else [halo_refs(sx, sy, True)[1]]
            for ref in targets:
                ref[...] = jnp.zeros(ref.shape, jnp.float32)
            if d < 4:
                uhalo[d] = jnp.zeros(uhalo.shape[1:], jnp.float32)

    def message(sx, sy, src, dst, rsem):
        def copy():
            return pltpu.make_async_remote_copy(
                src_ref=src,
                dst_ref=dst,
                send_sem=sent_sem.at[0],
                recv_sem=rsem,
                device_id=(ix + sx, iy + sy),
                device_id_type=MESH,
            )

        def start():
            @pl.when(exists(sx, sy))
            def _():
                copy().start()

        return start

    sides_x = (ix > 0).astype(jnp.int32) + (ix < n_x - 1).astype(jnp.int32)
    sides_y = (iy > 0).astype(jnp.int32) + (iy < n_y - 1).astype(jnp.int32)

    def rows_of(ref):
        return math.prod(ref.shape) // 128

    def wait_rows(count, sem):
        part = ruler.at[pl.ds(0, count)]
        pltpu.make_async_copy(part, part, sem).wait()

    def wait_sides(refs, sem):
        along_x, along_y, corner = [
            sum(rows_of(r) for r in refs[d]) if d < len(refs) else 0 for d in (0, 2, 4)
        ]
        for a in (1, 2):
            for b in (1, 2):

                @pl.when(jnp.logical_and(sides_x == a, sides_y == b))
                def _(count=a * along_x + b * along_y + a * b * corner):
                    wait_rows(count, sem)

    def gather(table, rsem, axis):
        me, count = ((ix, n_x), (iy, n_y), (flat, everyone))[axis]

        def copy(off):
            if axis == 2:
                peer = off - 1 + (off > me).astype(jnp.int32)
            else:
                peer = jnp.where(me < count // 2, count - off, off - 1)
                peer = jnp.where(jnp.where(me < count // 2, peer <= me, peer >= me), jnp.where(me < count // 2, peer - 1, peer + 1), peer)
            return pltpu.make_async_remote_copy(
                src_ref=table.at[me],
                dst_ref=table.at[me],
                send_sem=sent_sem.at[0],
                recv_sem=rsem,
                device_id=(
                    (peer, iy),
                    (ix, peer),
                    (lax.div(peer, n_y), lax.rem(peer, n_y)),
                )[axis],
                device_id_type=MESH,
            )

        def start():
            for off in range(1, count):
                copy(off).start()

        def wait():
            wait_rows((count - 1) * rows_of(table.at[0]), rsem)

        return start, wait

    t_refs = [[halo_refs(sx, sy, True)[1]] for sx, sy in FACES]
    t_refs += [[dst for _, dst in corner_parts(sx, sy)] for sx, sy in SENDS[4:]]
    v_refs = [[halo_refs(sx, sy, False)[1]] for sx, sy in SENDS]
    u_refs = [[uhalo.at[d]] for d in range(4)]
    f_ops = gather(ftab, f_sem, 0)
    g_ops = gather(gtab, g_sem, 2 if direct else 0)
    gg_ops = gather(gtabg, gg_sem, 1)
    t_ops = [message(sx, sy, *halo_refs(sx, sy, True), t_sem) for sx, sy in FACES]
    t_ops += [
        message(sx, sy, src, dst, t_sem) for sx, sy in SENDS[4:] for src, dst in corner_parts(sx, sy)
    ]
    v_ops = [
        message(sx, sy, *halo_refs(sx, sy, False), v_sem)
        for d, (sx, sy) in enumerate(SENDS)
    ]
    u_ops = [
        message(sx, sy, ustage.at[d], uhalo.at[d], u_sem)
        for d, (sx, sy) in enumerate(FACES)
    ]
    rows = iota((size_y, size_z), 0)
    lanes = iota((size_y, size_z), 1)
    low = rows < half

    def loaded(i, ref):
        pltpu.make_async_copy(ref, ref, in_sem.at[LOAD_SEM[i]]).wait()

    loaded(8, places_of)
    loaded(14, tables)
    for i in (11, 13, 0):
        loads_in[i].wait()
    cell = pcell[...]
    cell_col = lax.shift_right_logical(cell, size_z.bit_length() - 1)
    cell_z = cell & (size_z - 1)
    one_z = (iota((size_z, perfs), 0) == cell_z).astype(jnp.bfloat16)
    one_col = (iota((columns, perfs), 0) == cell_col).astype(jnp.float32)
    one_seg = (iota((segs, perfs), 0) == pseg[...]).astype(jnp.float32)
    one_well = (iota((wells, perfs), 0) == pwell[...]).astype(jnp.bfloat16)
    moves = (iota((wide, wells), 0) == owner[...]).astype(jnp.bfloat16)
    one_slot = dot(moves, one_well, ((1,), (0,)), None).astype(jnp.bfloat16)
    picked = dot_exact(adj[...].reshape(3 * columns, size_z), one_z, ((1,), (0,)))
    flux = None
    for m in range(3):
        part = jnp.sum(picked[m * columns : (m + 1) * columns] * one_col, axis=0, keepdims=True)
        part = part * pin[m : m + 1, :]
        flux = part if flux is None else flux + part
    loads = dot_exact(one_seg * flux, one_slot, ((1,), (1,)))
    slot_no = iota((slots, wide), 0) + ix * slots
    mine = (iota((slots, wide), 1) == slot_no).astype(jnp.float32)
    loads = loads + dot(wrhs[...], mine, ((0,), (0,)))
    packed = -(-3 * wells // 128) * 128
    blocks = packed // wide
    held_rows = ftab.shape[1] - segs * blocks
    folded = held_rows < segs
    if folded:
        loads = loads[: segs // 2] + pltpu.roll(loads[segs // 2 :], 64, 1)
    ftab[ix, :held_rows] = loads

    loads_in[17].wait()
    loaded(3, ext.at[:, own])
    lane_no = iota((slots, packed), 1)
    first = iota((slots, packed), 0) + ix * slots
    table = None
    for no, ref in enumerate((sdiag, soff, spar)):
        here = (lane_no == first + no * wells).astype(jnp.float32)
        part = dot(ref[...].astype(jnp.float32), here, ((0,), (0,)))
        table = part if table is None else table + part
    for b in range(blocks):
        ftab[ix, held_rows + b * segs : held_rows + (b + 1) * segs] = table[:, b * wide : (b + 1) * wide]

    def pack(read, write):
        for i in range(tiles):
            even, odd = read(2 * i), read(2 * i + 1)
            write(0, i, jnp.where(low, pltpu.roll(even, half, 0), odd))
            write(1, i, jnp.where(low, even, pltpu.roll(odd, half, 0)))

    def unpack(north, south):
        north_r, south_r = pltpu.roll(north, half, 0), pltpu.roll(south, half, 0)
        return jnp.where(low, north, south_r), jnp.where(low, north_r, south)

    loads_in[1].wait()

    def product(k, x):
        vector = [adj[m, x] for m in range(3)]
        return [
            tree(jac[9 * k + 3 * m + n, x].astype(jnp.float32) * vector[m] for m in range(3))
            for n in range(3)
        ]

    for n, value in enumerate(product(1, size_x - 1)):
        ustage[0, n] = value
    for n, value in enumerate(product(2, 0)):
        ustage[1, n] = value
    for x in planes:
        for n, value in enumerate(product(3, x)):
            ustage[2, n, x : x + 1, :] = value[size_y - 1 : size_y]
            cres[n, x] = jnp.where(rows == 0, 0.0, pltpu.roll(value, 1, 0))
    for x in planes:
        for n, value in enumerate(product(4, x)):
            ustage[3, n, x : x + 1, :] = value[0:1]
            cres[n, x] += jnp.where(rows == size_y - 1, 0.0, pltpu.roll(value, size_y - 1, 0))

    for f in range(4):

        def put(side, i, value, f=f):
            cpack[side, 4 * i + ORDER[f]] = value

        pack(lambda x, f=f: ext[f, x + DEPTH], put)
    diagonals = [exists(sx, sy).astype(jnp.int32) for sx, sy in SENDS[4:]]
    pl.semaphore_wait(barrier, n_x - 1 + n_y - 1 + sum(diagonals[1:], diagonals[0]))
    f_ops[0]()
    for op in u_ops:
        op()
    for op in t_ops:
        op()

    for x in planes:
        groups = [product(0, x)]
        if x > 0:
            groups.append(product(1, x - 1))
        if x < size_x - 1:
            groups.append(product(2, x + 1))
        above = product(5, x)
        groups.append([jnp.where(lanes == 0, 0.0, pltpu.roll(v, 1, 1)) for v in above])
        below = product(6, x)
        groups.append(
            [jnp.where(lanes == size_z - 1, 0.0, pltpu.roll(v, size_z - 1, 1)) for v in below]
        )
        for n in range(3):
            cres[n, x] += tree(group[n] for group in groups)

    for i in (12, 2, 7):
        loads_in[i].wait()

    f_ops[1]()
    total = [
        tree(ftab[i, held_rows + b * segs : held_rows + (b + 1) * segs] for i in range(n_x)) for b in range(blocks)
    ]
    total = jnp.concatenate(total, axis=1)

    def constant(no):
        if wells % 128 == 0:
            return total[:, no * wells : (no + 1) * wells]
        return total if no == 0 else pltpu.roll(total, 128 - no * wells, 1)

    used = iota((segs, wide), 1) < wells
    diag = jnp.where(used, constant(0), 1.0)
    ratio = jnp.where(used, constant(1), 0.0) / diag
    parent = jnp.where(used, constant(2), 0.0)
    levels = iota((segs, wide), 0).astype(jnp.float32)
    steps = [
        jnp.where(levels == parent[s : s + 1], ratio[s : s + 1], 0.0) for s in range(1, segs)
    ]
    load = tree(ftab[i, :held_rows] for i in range(n_x))
    if folded:
        load = jnp.concatenate([load, pltpu.roll(load, 64, 1)], axis=0)
    for s in range(segs - 1, 0, -1):
        load = load + load[s : s + 1] * steps[s - 1]
    answers = load / diag
    values = dot_exact(answers, one_slot, ((1,), (0,)))
    values = jnp.sum(values * one_seg, axis=0, keepdims=True)
    spread = jnp.concatenate([one_col * (pout[n : n + 1, :] * values) for n in range(3)], axis=0)
    added = dot_exact(spread, one_z, ((1,), (1,)))

    wait_sides(u_refs, u_sem)
    for x in planes:
        live = active[x].astype(jnp.float32)
        rhs = None
        for n in range(3):
            row = n * columns + x * size_y
            value = cres[n, x] + added[row : row + size_y]
            if x == 0:
                value = value + uhalo[0, n]
            if x == size_x - 1:
                value = value + uhalo[1, n]
            value = value + jnp.where(rows == 0, uhalo[2, n, x : x + 1, :], 0.0)
            value = value + jnp.where(rows == size_y - 1, uhalo[3, n, x : x + 1, :], 0.0)
            value = value * live
            upd[n, x] = value
            part = weights[n, x] * value
            rhs = part if rhs is None else rhs + part
        pext[0, 0, x + DEPTH] = rhs

    def put_p(side, i, value):
        ppack[side, i] = value

    pack(lambda x: pext[0, 0, x + DEPTH], put_p)
    for d in (2, 3, 4, 5, 6, 7, 0, 1):
        v_ops[d]()

    wout[...] = dot(mine, answers, ((1,), (1,)))
    shift = jnp.full((1, size_z), SHIFT, jnp.float32)
    inverse = 1.0 / SHIFT
    wait_sides(t_refs, t_sem)
    last_x = (ix == n_x - 1).astype(jnp.int32)
    last_y = (iy == n_y - 1).astype(jnp.int32)
    last_row = rows == jnp.where(last_y == 1, size_y - 1, size_y)
    keep_x = 1.0 - last_x.astype(jnp.float32)

    def following(a, b):
        a, b = pltpu.roll(a, size_y - 1, 0), pltpu.roll(b, size_y - 1, 0)
        return jnp.where(rows == size_y - 1, b, a), jnp.where(rows == size_y - 1, a, b)

    def preceding(a, b):
        a, b = pltpu.roll(a, 1, 0), pltpu.roll(b, 1, 0)
        return jnp.where(rows == 0, b, a), jnp.where(rows == 0, a, b)

    raw_x = None
    for i in range(wide_x // 2):
        both = [unpack(crecv[1, 4 * i + f], crecv[0, 4 * i + f]) for f in ORDER]
        for odd in range(2):
            j = 2 * i + odd
            parts = [(ext[f, j], both[f][odd]) for f in range(4)]
            south_raw = preceding(*parts[2])
            north = (jnp.where(last_row, 0.0, parts[2][0]), parts[2][1])
            south = preceding(*north)
            for h in range(2):
                here_x = parts[1][h]
                inside = jnp.where(lanes == size_z - 1, 0.0, parts[3][h])
                under = pltpu.roll(inside, 1, 1)
                if j > 0:
                    full = tree(
                        [
                            parts[0][h] + here_x,
                            raw_x[h] + parts[2][h],
                            south_raw[h] + parts[3][h],
                            under,
                        ]
                    )
                    coef[0, h, j] = full * inverse - 1.0
                east = here_x * inverse
                coef[1, h, j] = east * keep_x if j == DEPTH + size_x - 1 else east
                coef[2, h, j] = north[h] * inverse
                coef[3, h, j] = south[h] * inverse
                coef[4, h, j] = inside * inverse
                coef[5, h, j] = under * inverse
            raw_x = (parts[1][0], parts[1][1])

    wait_sides(v_refs, v_sem)
    for i in range(wide_x // 2):
        pair = unpack(precv[1, i], precv[0, i])
        pext[0, 1, 2 * i] = pair[0]
        pext[0, 1, 2 * i + 1] = pair[1]

    for k in range(ITERS):
        final = k == ITERS - 1
        for j in range(k + 1, wide_x - k - 1):
            here = (pext[k, 0, j], pext[k, 1, j])
            up = following(*here)
            down = preceding(*here)
            for h in range(1 if final else 2):
                image = coef[0, h, j] * here[h] - tree(
                    [
                        coef[1, h, j] * pext[k, h, j + 1],
                        coef[1, h, j - 1] * pext[k, h, j - 1],
                        coef[2, h, j] * up[h],
                        coef[3, h, j] * down[h],
                        coef[4, h, j] * pltpu.roll(here[h], size_z - 1, 1),
                        coef[5, h, j] * pltpu.roll(here[h], 1, 1),
                    ]
                )
                pext[k + 1, h, j] = image if k == 0 else 2.0 * image - pext[k - 1, h, j]

    def mine_of(k, x):
        return pext[k, 0, x + DEPTH]

    count = 16
    grams = [
        jnp.sum(tree(mine_of(i, x) * mine_of(j, x) for x in planes), axis=0, keepdims=True)
        for i, j in PAIRS
    ]
    grams += [jnp.zeros((1, size_z), jnp.float32)] * (count - len(PAIRS))
    column = jnp.sum(jnp.concatenate(grams, axis=0), axis=1, keepdims=True)
    on_lane = iota((count, 128), 0) == iota((count, 128), 1)
    entries = jnp.sum(jnp.where(on_lane, column, 0.0), axis=0, keepdims=True)
    gtab[flat if direct else ix] = entries
    g_ops[0]()
    g_ops[1]()
    sums = tree(gtab[i] for i in range(gtab.shape[0]))
    if not direct:
        gtabg[iy] = sums
        gg_ops[0]()
        gg_ops[1]()
        sums = tree(gtabg[i] for i in range(n_y))
    sums = jnp.sum(jnp.where(on_lane, sums, 0.0), axis=1, keepdims=True)
    sums = jnp.broadcast_to(sums, (count, size_z))

    def gram(i, j):
        row = PAIRS.index((min(i, j), max(i, j)))
        return sums[row : row + 1]

    answer = krylov_coefficients(gram, shift)
    for x in planes:
        pressure = tree(answer[k] * mine_of(k, x) for k in range(ITERS))
        for n in range(3):
            upd[n, x] += weights[n, x] * pressure

    sent_rows = sum(
        (count - 1) * rows_of(table.at[0])
        for table, count in (
            (ftab, n_x), (gtab, gtab.shape[0]), (gtabg, 1 if direct else n_y),
        )
    )
    shapes = [t + v + (u_refs[d] if d < 4 else []) for d, (t, v) in enumerate(zip(t_refs, v_refs))]
    along_x, along_y, corner = [sum(rows_of(r) for r in shapes[d]) for d in (0, 2, 4)]
    for a in (1, 2):
        for b in (1, 2):

            @pl.when(jnp.logical_and(sides_x == a, sides_y == b))
            def _(count=a * along_x + b * along_y + a * b * corner + sent_rows):
                wait_rows(count, sent_sem.at[0])


def hand_over(update, answers, update_out, answers_out, sems):
    copies = [
        pltpu.make_async_copy(update, update_out, sems.at[0]),
        pltpu.make_async_copy(answers, answers_out, sems.at[1]),
    ]
    for copy in copies:
        copy.start()
    for copy in copies:
        copy.wait()


def shards(n_x, n_y, *args):
    args = list(args)
    size_x, size_y, size_z = args[0].shape[1:]
    for k in (8, 9, 10):
        args[k] = args[k][None]
    for k in (14, 15, 16, 17):
        args[k] = args[k][:, 0, :].T
    slots, segs = args[14].shape
    wells = args[13].shape[1]
    wide = -(-wells // 128) * 128
    packed = -(-3 * wells // 128) * 128
    folded = segs // 2 if wells <= 64 and segs == 16 else segs
    joined = n_x * n_y if n_x * n_y <= 32 else n_x
    plane = (size_y, size_z)
    wide_x = size_x + 2 * DEPTH
    dma = pltpu.SemaphoreType.DMA

    def f32(*shape):
        return pltpu.VMEM(shape, jnp.float32)

    held = [pltpu.VMEM(args[k].shape, args[k].dtype) for k in (0, 1, 2, 7)]
    held += [pltpu.VMEM((3,) + args[8].shape, jnp.int32)]
    held += [pltpu.VMEM(args[k].shape, args[k].dtype) for k in (11, 12, 13)]
    held += [f32(3, *args[14].shape), pltpu.VMEM(args[17].shape, jnp.int32)]
    held += [f32(4, wide_x, *plane), f32(ITERS + 1, 2, wide_x, *plane)]
    tiles = size_x // 2
    along = DEPTH * size_y
    ruler = 2 * (2 * 5 * along + 2 * 3 * size_y) + 4 * 5 * along // 2
    ruler += n_x * segs * (packed + wide) // 128 + 2 * n_y + joined
    scratch = [
        f32(3, size_x, *plane),
        f32(6, 2, wide_x, *plane),
        f32(n_x, folded + segs * packed // wide, wide),
        f32(joined, 1, 128),
        f32(n_y, 1, 128),
        f32(2, 4 * tiles, *plane),
        f32(2, 2 * wide_x, *plane),
        f32(2, tiles, *plane),
        f32(2, wide_x // 2, *plane),
        f32(4, 3, *plane),
        f32(4, 3, *plane),
        f32(ruler, 1, 128),
        dma((11,)),
        dma((1,)),
        dma((6,)),
    ]
    vmem = pl.BlockSpec(memory_space=pltpu.VMEM)
    update, answers = pl.pallas_call(
        functools.partial(kernel, n_x, n_y),
        out_shape=(
            pltpu.VMEM(args[0].shape, jnp.float32),
            pltpu.VMEM((slots, segs), jnp.float32),
        ),
        in_specs=[pl.BlockSpec(memory_space=pl.ANY)] * 18,
        out_specs=(vmem, vmem),
        scratch_shapes=held + scratch,
        compiler_params=pltpu.CompilerParams(collective_id=0, has_side_effects=True),
    )(*args)
    update = pltpu.with_memory_space_constraint(update, pltpu.VMEM)
    answers = pltpu.with_memory_space_constraint(answers, pltpu.VMEM)
    any_space = pl.BlockSpec(memory_space=pl.ANY)
    update, answers = pl.pallas_call(
        hand_over,
        out_shape=(
            jax.ShapeDtypeStruct(update.shape, jnp.float32),
            jax.ShapeDtypeStruct(answers.shape, jnp.float32),
        ),
        in_specs=[vmem, vmem],
        out_specs=(any_space, any_space),
        scratch_shapes=[dma((2,))],
    )(update, answers)
    return update, answers.T[:, None, :]


def solution(mesh):
    body = functools.partial(shards, mesh.shape["gx"], mesh.shape["gy"])
    cells = P("gx", "gy", None)
    stacked = P(None, "gx", "gy", None)
    perf = P(("gx", "gy"))
    perf_3 = P(None, ("gx", "gy"))
    segment = P(None, "gy", "gx")
    return jax.shard_map(
        body,
        mesh=mesh,
        in_specs=(stacked, stacked)
        + (cells,) * 5
        + (stacked,)
        + (perf,) * 3
        + (perf_3,) * 2
        + (P("gy", None),)
        + (segment,) * 4,
        out_specs=(stacked, segment),
        check_vma=False,
    )
```

```python
import functools
import math

import jax
import jax.numpy as jnp
from jax import lax
from jax.experimental import pallas as pl
from jax.experimental.pallas import tpu as pltpu
from jax.sharding import PartitionSpec as P

ITERS = 4
MESH = pl.DeviceIdType.MESH
HIGH = lax.Precision.HIGHEST
PAIRS = [(i, j) for i in range(ITERS) for j in range(i, ITERS + 1)]


def iota(shape, dim):
    return lax.broadcasted_iota(jnp.int32, shape, dim)


def dot(a, b, dims, precision=HIGH):
    return lax.dot_general(
        a, b, (dims, ((), ())), precision=precision, preferred_element_type=jnp.float32
    )


def dot_exact(a, pick, dims):
    high = a.astype(jnp.bfloat16)
    rest = a - high.astype(jnp.float32)
    mid = rest.astype(jnp.bfloat16)
    low = (rest - mid.astype(jnp.float32)).astype(jnp.bfloat16)
    parts = [dot(part, pick, dims, None) for part in (high, mid, low)]
    return parts[0] + (parts[1] + parts[2])


def tree(values):
    values = list(values)
    while len(values) > 1:
        pairs = [a + b for a, b in zip(values[::2], values[1::2])]
        values = pairs + values[len(pairs) * 2 :]
    return values[0]


def krylov_coefficients(gram, shift):
    size = ITERS + 1

    def apply(v):
        out = [None] * size

        def put(k, value):
            out[k] = value if out[k] is None else out[k] + value

        for k, value in enumerate(v):
            if value is None:
                continue
            scaled = value * shift
            put(k, scaled)
            if k == 0:
                put(1, scaled)
            else:
                put(k + 1, scaled * 0.5)
                put(k - 1, scaled * 0.5)
        return out

    def inner(a, b):
        total = []
        for j in range(size):
            if b[j] is None:
                continue
            part = [a[i] * gram(i, j) for i in range(size) if a[i] is not None]
            total.append(tree(part) * b[j])
        return tree(total)

    def axpy(a, scale, b):
        out = []
        for p, q in zip(a, b):
            if q is None:
                out.append(p)
            else:
                out.append(scale * q if p is None else p + scale * q)
        return out

    one = jnp.ones_like(shift)
    residual = [one] + [None] * ITERS
    direction = list(residual)
    answer = [None] * size
    norm = gram(0, 0)
    for iteration in range(ITERS):
        image = apply(direction)
        bottom = inner(direction, image)
        alpha = jnp.where(bottom > 0, norm / bottom, 0.0)
        answer = axpy(answer, alpha, direction)
        if iteration == ITERS - 1:
            break
        residual = axpy(residual, -alpha, image)
        new = inner(residual, residual)
        beta = jnp.where(norm > 0, new / norm, 0.0)
        direction = axpy(residual, beta, direction)
        norm = new
    return answer[:ITERS]


DEPTH = ITERS
ORDER = (0, 3, 2, 1)
SHIFT = 2.3
SENDS = [(1, 0), (-1, 0), (0, 1), (0, -1), (1, 1), (-1, 1), (1, -1), (-1, -1)]
FACES = [(1, 0), (-1, 0), (0, 1), (0, -1)]
HELD = 12
LOAD_SEM = (0, 1, 2, 3, 3, 3, 3, 4, 5, 5, 5, 6, 7, 8, 9, 9, 9, 10)


def kernel(n_x, n_y, *refs):
    inputs, (upd, wout) = refs[:18], refs[18:20]
    held, scratch = refs[20 : 20 + HELD], refs[20 + HELD :]
    adj, jac, active, weights, places_of, pin, pout, owner, tables, spar, ext, pext = held
    pcell, pwell, pseg = [places_of.at[i] for i in range(3)]
    wrhs, sdiag, soff = [tables.at[i] for i in range(3)]
    (cres, coef, ftab, gtab, gtabg, cpack, crecv, ppack, precv) = scratch[:9]
    ustage, uhalo, ruler, in_sem, sent_sem, got_sem = scratch[9:]
    f_sem, g_sem, gg_sem, t_sem, u_sem, v_sem = [got_sem.at[i] for i in range(6)]

    ix = lax.axis_index("gx")
    iy = lax.axis_index("gy")
    size_x, size_y, size_z = adj.shape[1:]
    planes = range(size_x)
    wide_x = size_x + 2 * DEPTH
    own = slice(DEPTH, DEPTH + size_x)
    half = size_y // 2
    tiles = size_x // 2
    edge = DEPTH // 2
    perfs = pcell.shape[1]
    slots, segs = wrhs.shape
    wells = owner.shape[1]
    wide = -(-wells // 128) * 128
    columns = size_x * size_y

    def exists(sx, sy):
        fine = None
        for step, at, count in ((sx, ix, n_x), (sy, iy, n_y)):
            if step:
                one = at < count - 1 if step > 0 else at > 0
                fine = one if fine is None else jnp.logical_and(fine, one)
        return fine

    barrier = pltpu.get_barrier_semaphore()
    everyone = n_x * n_y
    direct = gtab.shape[0] == everyone
    flat = ix * n_y + iy
    for off in range(1, n_x):
        pl.semaphore_signal(
            barrier, inc=1, device_id=(lax.rem(ix + off, n_x), iy), device_id_type=MESH
        )
    for off in range(1, n_y):
        pl.semaphore_signal(
            barrier, inc=1, device_id=(ix, lax.rem(iy + off, n_y)), device_id_type=MESH
        )
    for sx, sy in SENDS[4:]:

        @pl.when(exists(sx, sy))
        def _(sx=sx, sy=sy):
            pl.semaphore_signal(barrier, inc=1, device_id=(ix + sx, iy + sy), device_id_type=MESH)

    places = [
        adj, jac, active, ext.at[1, own], ext.at[2, own], ext.at[3, own], ext.at[0, own],
        weights, pcell, pwell, pseg, pin, pout, owner, wrhs, sdiag, soff, spar,
    ]
    loads_in = [
        pltpu.make_async_copy(src, dst, in_sem.at[LOAD_SEM[i]])
        for i, (src, dst) in enumerate(zip(inputs, places))
    ]
    for i in (8, 9, 10, 11, 13, 0, 14, 15, 16, 17, 3, 4, 5, 6, 1, 12, 2, 7):
        loads_in[i].start()

    def spot(sx, sy):
        if sy == 0:
            if sx > 0:
                return slice(size_x, size_x + DEPTH), slice(0, DEPTH)
            return slice(DEPTH, 2 * DEPTH), slice(DEPTH + size_x, wide_x)
        if sx == 0:
            return slice(0, tiles), slice(edge, edge + tiles)
        if sx > 0:
            return slice(tiles - edge, tiles), slice(0, edge)
        return slice(0, edge), slice(edge + tiles, tiles + 2 * edge)

    def halo_refs(sx, sy, coefs):
        src, dst = spot(sx, sy)
        if sy == 0:
            if coefs:
                return ext.at[:, src], ext.at[:, dst]
            return pext.at[0, 0, src], pext.at[0, 0, dst]
        side = 0 if sy > 0 else 1
        if coefs:
            src, dst = slice(0, 4 * tiles), slice(4 * edge, 4 * (edge + tiles))
            return cpack.at[side, src], crecv.at[side, dst]
        return ppack.at[side, src], precv.at[side, dst]

    def corner_parts(sx, sy):
        side = 0 if sy > 0 else 1
        put, got = (4 * (tiles - 1), 4 * (edge - 1)) if sx > 0 else (0, 4 * (edge + tiles))
        third = -2 if sx > 0 else 4 + ORDER[2]
        near = half if sx > 0 else 0
        row = half - 1 if sy > 0 else 0
        spans = [
            (0, 4, near, half),
            (0, 4, half - near + (half - 2 if sy > 0 else 0), 2),
            (third, 2, near + row, 1),
        ]
        return [
            (
                cpack.at[side, put + at : put + at + count, first : first + span],
                crecv.at[side, got + at : got + at + count, first : first + span],
            )
            for at, count, first, span in spans
        ]

    for d, (sx, sy) in enumerate(SENDS):

        @pl.when(jnp.logical_not(exists(-sx, -sy)))
        def _(d=d, sx=sx, sy=sy):
            targets = [halo_refs(sx, sy, False)[1]]
            targets += [r for _, r in corner_parts(sx, sy)] if d > 3 else [halo_refs(sx, sy, True)[1]]
            for ref in targets:
                ref[...] = jnp.zeros(ref.shape, jnp.float32)
            if d < 4:
                uhalo[d] = jnp.zeros(uhalo.shape[1:], jnp.float32)

    def message(sx, sy, src, dst, rsem):
        def copy():
            return pltpu.make_async_remote_copy(
                src_ref=src,
                dst_ref=dst,
                send_sem=sent_sem.at[0],
                recv_sem=rsem,
                device_id=(ix + sx, iy + sy),
                device_id_type=MESH,
            )

        def start():
            @pl.when(exists(sx, sy))
            def _():
                copy().start()

        return start

    sides_x = (ix > 0).astype(jnp.int32) + (ix < n_x - 1).astype(jnp.int32)
    sides_y = (iy > 0).astype(jnp.int32) + (iy < n_y - 1).astype(jnp.int32)

    def rows_of(ref):
        return math.prod(ref.shape) // 128

    def wait_rows(count, sem):
        part = ruler.at[pl.ds(0, count)]
        pltpu.make_async_copy(part, part, sem).wait()

    def wait_sides(refs, sem):
        along_x, along_y, corner = [
            sum(rows_of(r) for r in refs[d]) if d < len(refs) else 0 for d in (0, 2, 4)
        ]
        for a in (1, 2):
            for b in (1, 2):

                @pl.when(jnp.logical_and(sides_x == a, sides_y == b))
                def _(count=a * along_x + b * along_y + a * b * corner):
                    wait_rows(count, sem)

    def gather(table, rsem, axis):
        me, count = ((ix, n_x), (iy, n_y), (flat, everyone))[axis]

        def copy(off):
            if axis == 2:
                peer = off - 1 + (off > me).astype(jnp.int32)
            else:
                peer = lax.rem(me + jnp.where(me < count // 2, count - off, off), count)
            return pltpu.make_async_remote_copy(
                src_ref=table.at[me],
                dst_ref=table.at[me],
                send_sem=sent_sem.at[0],
                recv_sem=rsem,
                device_id=(
                    (peer, iy),
                    (ix, peer),
                    (lax.div(peer, n_y), lax.rem(peer, n_y)),
                )[axis],
                device_id_type=MESH,
            )

        def start():
            for off in range(1, count):
                copy(off).start()

        def wait():
            wait_rows((count - 1) * rows_of(table.at[0]), rsem)

        return start, wait

    t_refs = [[halo_refs(sx, sy, True)[1]] for sx, sy in FACES]
    t_refs += [[dst for _, dst in corner_parts(sx, sy)] for sx, sy in SENDS[4:]]
    v_refs = [[halo_refs(sx, sy, False)[1]] for sx, sy in SENDS]
    u_refs = [[uhalo.at[d]] for d in range(4)]
    f_ops = gather(ftab, f_sem, 0)
    g_ops = gather(gtab, g_sem, 2 if direct else 0)
    gg_ops = gather(gtabg, gg_sem, 1)
    t_ops = [message(sx, sy, *halo_refs(sx, sy, True), t_sem) for sx, sy in FACES]
    t_ops += [
        message(sx, sy, src, dst, t_sem) for sx, sy in SENDS[4:] for src, dst in corner_parts(sx, sy)
    ]
    v_ops = [
        message(sx, sy, *halo_refs(sx, sy, False), v_sem)
        for d, (sx, sy) in enumerate(SENDS)
    ]
    u_ops = [
        message(sx, sy, ustage.at[d], uhalo.at[d], u_sem)
        for d, (sx, sy) in enumerate(FACES)
    ]
    rows = iota((size_y, size_z), 0)
    lanes = iota((size_y, size_z), 1)
    low = rows < half

    def loaded(i, ref):
        pltpu.make_async_copy(ref, ref, in_sem.at[LOAD_SEM[i]]).wait()

    loaded(8, places_of)
    loaded(14, tables)
    for i in (11, 13, 0):
        loads_in[i].wait()
    cell = pcell[...]
    cell_col = lax.shift_right_logical(cell, size_z.bit_length() - 1)
    cell_z = cell & (size_z - 1)
    one_z = (iota((size_z, perfs), 0) == cell_z).astype(jnp.bfloat16)
    one_col = (iota((columns, perfs), 0) == cell_col).astype(jnp.float32)
    one_seg = (iota((segs, perfs), 0) == pseg[...]).astype(jnp.float32)
    one_well = (iota((wells, perfs), 0) == pwell[...]).astype(jnp.bfloat16)
    moves = (iota((wide, wells), 0) == owner[...]).astype(jnp.bfloat16)
    one_slot = dot(moves, one_well, ((1,), (0,)), None).astype(jnp.bfloat16)
    picked = dot_exact(adj[...].reshape(3 * columns, size_z), one_z, ((1,), (0,)))
    flux = None
    for m in range(3):
        part = jnp.sum(picked[m * columns : (m + 1) * columns] * one_col, axis=0, keepdims=True)
        part = part * pin[m : m + 1, :]
        flux = part if flux is None else flux + part
    loads = dot_exact(one_seg * flux, one_slot, ((1,), (1,)))
    slot_no = iota((slots, wide), 0) + ix * slots
    mine = (iota((slots, wide), 1) == slot_no).astype(jnp.float32)
    loads = loads + dot(wrhs[...], mine, ((0,), (0,)))
    packed = -(-3 * wells // 128) * 128
    blocks = packed // wide
    held_rows = ftab.shape[1] - segs * blocks
    folded = held_rows < segs
    if folded:
        loads = loads[: segs // 2] + pltpu.roll(loads[segs // 2 :], 64, 1)
    ftab[ix, :held_rows] = loads

    loads_in[17].wait()
    loaded(3, ext.at[:, own])
    lane_no = iota((slots, packed), 1)
    first = iota((slots, packed), 0) + ix * slots
    table = None
    for no, ref in enumerate((sdiag, soff, spar)):
        here = (lane_no == first + no * wells).astype(jnp.float32)
        part = dot(ref[...].astype(jnp.float32), here, ((0,), (0,)))
        table = part if table is None else table + part
    for b in range(blocks):
        ftab[ix, held_rows + b * segs : held_rows + (b + 1) * segs] = table[:, b * wide : (b + 1) * wide]

    def pack(read, write):
        for i in range(tiles):
            even, odd = read(2 * i), read(2 * i + 1)
            write(0, i, jnp.where(low, pltpu.roll(even, half, 0), odd))
            write(1, i, jnp.where(low, even, pltpu.roll(odd, half, 0)))

    def unpack(north, south):
        north_r, south_r = pltpu.roll(north, half, 0), pltpu.roll(south, half, 0)
        return jnp.where(low, north, south_r), jnp.where(low, north_r, south)

    loads_in[1].wait()

    def product(k, x):
        vector = [adj[m, x] for m in range(3)]
        return [
            tree(jac[9 * k + 3 * m + n, x].astype(jnp.float32) * vector[m] for m in range(3))
            for n in range(3)
        ]

    for n, value in enumerate(product(1, size_x - 1)):
        ustage[0, n] = value
    for n, value in enumerate(product(2, 0)):
        ustage[1, n] = value
    for x in planes:
        for n, value in enumerate(product(3, x)):
            ustage[2, n, x : x + 1, :] = value[size_y - 1 : size_y]
            cres[n, x] = jnp.where(rows == 0, 0.0, pltpu.roll(value, 1, 0))
    for x in planes:
        for n, value in enumerate(product(4, x)):
            ustage[3, n, x : x + 1, :] = value[0:1]
            cres[n, x] += jnp.where(rows == size_y - 1, 0.0, pltpu.roll(value, size_y - 1, 0))

    for f in range(4):

        def put(side, i, value, f=f):
            cpack[side, 4 * i + ORDER[f]] = value

        pack(lambda x, f=f: ext[f, x + DEPTH], put)
    diagonals = [exists(sx, sy).astype(jnp.int32) for sx, sy in SENDS[4:]]
    pl.semaphore_wait(barrier, n_x - 1 + n_y - 1 + sum(diagonals[1:], diagonals[0]))
    f_ops[0]()
    for op in u_ops:
        op()
    for op in t_ops:
        op()

    for x in planes:
        groups = [product(0, x)]
        if x > 0:
            groups.append(product(1, x - 1))
        if x < size_x - 1:
            groups.append(product(2, x + 1))
        above = product(5, x)
        groups.append([jnp.where(lanes == 0, 0.0, pltpu.roll(v, 1, 1)) for v in above])
        below = product(6, x)
        groups.append(
            [jnp.where(lanes == size_z - 1, 0.0, pltpu.roll(v, size_z - 1, 1)) for v in below]
        )
        for n in range(3):
            cres[n, x] += tree(group[n] for group in groups)

    for i in (12, 2, 7):
        loads_in[i].wait()

    wait_sides(u_refs, u_sem)
    f_ops[1]()
    total = [
        tree(ftab[i, held_rows + b * segs : held_rows + (b + 1) * segs] for i in range(n_x)) for b in range(blocks)
    ]
    total = jnp.concatenate(total, axis=1)

    def constant(no):
        if wells % 128 == 0:
            return total[:, no * wells : (no + 1) * wells]
        return total if no == 0 else pltpu.roll(total, 128 - no * wells, 1)

    used = iota((segs, wide), 1) < wells
    diag = jnp.where(used, constant(0), 1.0)
    ratio = jnp.where(used, constant(1), 0.0) / diag
    parent = jnp.where(used, constant(2), 0.0)
    levels = iota((segs, wide), 0).astype(jnp.float32)
    steps = [
        jnp.where(levels == parent[s : s + 1], ratio[s : s + 1], 0.0) for s in range(1, segs)
    ]
    load = tree(ftab[i, :held_rows] for i in range(n_x))
    if folded:
        load = jnp.concatenate([load, pltpu.roll(load, 64, 1)], axis=0)
    for s in range(segs - 1, 0, -1):
        load = load + load[s : s + 1] * steps[s - 1]
    answers = load / diag
    values = dot_exact(answers, one_slot, ((1,), (0,)))
    values = jnp.sum(values * one_seg, axis=0, keepdims=True)
    spread = jnp.concatenate([one_col * (pout[n : n + 1, :] * values) for n in range(3)], axis=0)
    added = dot_exact(spread, one_z, ((1,), (1,)))

    for x in planes:
        live = active[x].astype(jnp.float32)
        rhs = None
        for n in range(3):
            row = n * columns + x * size_y
            value = cres[n, x] + added[row : row + size_y]
            if x == 0:
                value = value + uhalo[0, n]
            if x == size_x - 1:
                value = value + uhalo[1, n]
            value = value + jnp.where(rows == 0, uhalo[2, n, x : x + 1, :], 0.0)
            value = value + jnp.where(rows == size_y - 1, uhalo[3, n, x : x + 1, :], 0.0)
            value = value * live
            upd[n, x] = value
            part = weights[n, x] * value
            rhs = part if rhs is None else rhs + part
        pext[0, 0, x + DEPTH] = rhs

    def put_p(side, i, value):
        ppack[side, i] = value

    pack(lambda x: pext[0, 0, x + DEPTH], put_p)
    for d in (2, 3, 4, 5, 6, 7, 0, 1):
        v_ops[d]()

    wout[...] = dot(mine, answers, ((1,), (1,)))
    shift = jnp.full((1, size_z), SHIFT, jnp.float32)
    inverse = 1.0 / SHIFT
    wait_sides(t_refs, t_sem)
    last_x = (ix == n_x - 1).astype(jnp.int32)
    last_y = (iy == n_y - 1).astype(jnp.int32)
    last_row = rows == jnp.where(last_y == 1, size_y - 1, size_y)
    keep_x = 1.0 - last_x.astype(jnp.float32)

    def following(a, b):
        a, b = pltpu.roll(a, size_y - 1, 0), pltpu.roll(b, size_y - 1, 0)
        return jnp.where(rows == size_y - 1, b, a), jnp.where(rows == size_y - 1, a, b)

    def preceding(a, b):
        a, b = pltpu.roll(a, 1, 0), pltpu.roll(b, 1, 0)
        return jnp.where(rows == 0, b, a), jnp.where(rows == 0, a, b)

    raw_x = None
    for i in range(wide_x // 2):
        both = [unpack(crecv[1, 4 * i + f], crecv[0, 4 * i + f]) for f in ORDER]
        for odd in range(2):
            j = 2 * i + odd
            parts = [(ext[f, j], both[f][odd]) for f in range(4)]
            south_raw = preceding(*parts[2])
            north = (jnp.where(last_row, 0.0, parts[2][0]), parts[2][1])
            south = preceding(*north)
            for h in range(2):
                here_x = parts[1][h]
                inside = jnp.where(lanes == size_z - 1, 0.0, parts[3][h])
                under = pltpu.roll(inside, 1, 1)
                if j > 0:
                    full = tree(
                        [
                            parts[0][h] + here_x,
                            raw_x[h] + parts[2][h],
                            south_raw[h] + parts[3][h],
                            under,
                        ]
                    )
                    coef[0, h, j] = full * inverse - 1.0
                east = here_x * inverse
                coef[1, h, j] = east * keep_x if j == DEPTH + size_x - 1 else east
                coef[2, h, j] = north[h] * inverse
                coef[3, h, j] = south[h] * inverse
                coef[4, h, j] = inside * inverse
                coef[5, h, j] = under * inverse
            raw_x = (parts[1][0], parts[1][1])

    wait_sides(v_refs, v_sem)
    for i in range(wide_x // 2):
        pair = unpack(precv[1, i], precv[0, i])
        pext[0, 1, 2 * i] = pair[0]
        pext[0, 1, 2 * i + 1] = pair[1]

    for k in range(ITERS):
        final = k == ITERS - 1
        for j in range(k + 1, wide_x - k - 1):
            here = (pext[k, 0, j], pext[k, 1, j])
            up = following(*here)
            down = preceding(*here)
            for h in range(1 if final else 2):
                image = coef[0, h, j] * here[h] - tree(
                    [
                        coef[1, h, j] * pext[k, h, j + 1],
                        coef[1, h, j - 1] * pext[k, h, j - 1],
                        coef[2, h, j] * up[h],
                        coef[3, h, j] * down[h],
                        coef[4, h, j] * pltpu.roll(here[h], size_z - 1, 1),
                        coef[5, h, j] * pltpu.roll(here[h], 1, 1),
                    ]
                )
                pext[k + 1, h, j] = image if k == 0 else 2.0 * image - pext[k - 1, h, j]

    def mine_of(k, x):
        return pext[k, 0, x + DEPTH]

    count = 16
    grams = [
        jnp.sum(tree(mine_of(i, x) * mine_of(j, x) for x in planes), axis=0, keepdims=True)
        for i, j in PAIRS
    ]
    grams += [jnp.zeros((1, size_z), jnp.float32)] * (count - len(PAIRS))
    column = jnp.sum(jnp.concatenate(grams, axis=0), axis=1, keepdims=True)
    on_lane = iota((count, 128), 0) == iota((count, 128), 1)
    entries = jnp.sum(jnp.where(on_lane, column, 0.0), axis=0, keepdims=True)
    gtab[flat if direct else ix] = entries
    g_ops[0]()
    g_ops[1]()
    sums = tree(gtab[i] for i in range(gtab.shape[0]))
    if not direct:
        gtabg[iy] = sums
        gg_ops[0]()
        gg_ops[1]()
        sums = tree(gtabg[i] for i in range(n_y))
    sums = jnp.sum(jnp.where(on_lane, sums, 0.0), axis=1, keepdims=True)
    sums = jnp.broadcast_to(sums, (count, size_z))

    def gram(i, j):
        row = PAIRS.index((min(i, j), max(i, j)))
        return sums[row : row + 1]

    answer = krylov_coefficients(gram, shift)
    for x in planes:
        pressure = tree(answer[k] * mine_of(k, x) for k in range(ITERS))
        for n in range(3):
            upd[n, x] += weights[n, x] * pressure

    sent_rows = sum(
        (count - 1) * rows_of(table.at[0])
        for table, count in (
            (ftab, n_x), (gtab, gtab.shape[0]), (gtabg, 1 if direct else n_y),
        )
    )
    shapes = [t + v + (u_refs[d] if d < 4 else []) for d, (t, v) in enumerate(zip(t_refs, v_refs))]
    along_x, along_y, corner = [sum(rows_of(r) for r in shapes[d]) for d in (0, 2, 4)]
    for a in (1, 2):
        for b in (1, 2):

            @pl.when(jnp.logical_and(sides_x == a, sides_y == b))
            def _(count=a * along_x + b * along_y + a * b * corner + sent_rows):
                wait_rows(count, sent_sem.at[0])


def hand_over(update, answers, update_out, answers_out, sems):
    copies = [
        pltpu.make_async_copy(update, update_out, sems.at[0]),
        pltpu.make_async_copy(answers, answers_out, sems.at[1]),
    ]
    for copy in copies:
        copy.start()
    for copy in copies:
        copy.wait()


def shards(n_x, n_y, *args):
    args = list(args)
    size_x, size_y, size_z = args[0].shape[1:]
    for k in (8, 9, 10):
        args[k] = args[k][None]
    for k in (14, 15, 16, 17):
        args[k] = args[k][:, 0, :].T
    slots, segs = args[14].shape
    wells = args[13].shape[1]
    wide = -(-wells // 128) * 128
    packed = -(-3 * wells // 128) * 128
    folded = segs // 2 if wells <= 64 and segs == 16 else segs
    joined = n_x * n_y if n_x * n_y <= 32 else n_x
    plane = (size_y, size_z)
    wide_x = size_x + 2 * DEPTH
    dma = pltpu.SemaphoreType.DMA

    def f32(*shape):
        return pltpu.VMEM(shape, jnp.float32)

    held = [pltpu.VMEM(args[k].shape, args[k].dtype) for k in (0, 1, 2, 7)]
    held += [pltpu.VMEM((3,) + args[8].shape, jnp.int32)]
    held += [pltpu.VMEM(args[k].shape, args[k].dtype) for k in (11, 12, 13)]
    held += [f32(3, *args[14].shape), pltpu.VMEM(args[17].shape, jnp.int32)]
    held += [f32(4, wide_x, *plane), f32(ITERS + 1, 2, wide_x, *plane)]
    tiles = size_x // 2
    along = DEPTH * size_y
    ruler = 2 * (2 * 5 * along + 2 * 3 * size_y) + 4 * 5 * along // 2
    ruler += n_x * segs * (packed + wide) // 128 + 2 * n_y + joined
    scratch = [
        f32(3, size_x, *plane),
        f32(6, 2, wide_x, *plane),
        f32(n_x, folded + segs * packed // wide, wide),
        f32(joined, 1, 128),
        f32(n_y, 1, 128),
        f32(2, 4 * tiles, *plane),
        f32(2, 2 * wide_x, *plane),
        f32(2, tiles, *plane),
        f32(2, wide_x // 2, *plane),
        f32(4, 3, *plane),
        f32(4, 3, *plane),
        f32(ruler, 1, 128),
        dma((11,)),
        dma((1,)),
        dma((6,)),
    ]
    vmem = pl.BlockSpec(memory_space=pltpu.VMEM)
    update, answers = pl.pallas_call(
        functools.partial(kernel, n_x, n_y),
        out_shape=(
            pltpu.VMEM(args[0].shape, jnp.float32),
            pltpu.VMEM((slots, segs), jnp.float32),
        ),
        in_specs=[pl.BlockSpec(memory_space=pl.ANY)] * 18,
        out_specs=(vmem, vmem),
        scratch_shapes=held + scratch,
        compiler_params=pltpu.CompilerParams(collective_id=0, has_side_effects=True),
    )(*args)
    update = pltpu.with_memory_space_constraint(update, pltpu.VMEM)
    answers = pltpu.with_memory_space_constraint(answers, pltpu.VMEM)
    any_space = pl.BlockSpec(memory_space=pl.ANY)
    update, answers = pl.pallas_call(
        hand_over,
        out_shape=(
            jax.ShapeDtypeStruct(update.shape, jnp.float32),
            jax.ShapeDtypeStruct(answers.shape, jnp.float32),
        ),
        in_specs=[vmem, vmem],
        out_specs=(any_space, any_space),
        scratch_shapes=[dma((2,))],
    )(update, answers)
    return update, answers.T[:, None, :]


def solution(mesh):
    body = functools.partial(shards, mesh.shape["gx"], mesh.shape["gy"])
    cells = P("gx", "gy", None)
    stacked = P(None, "gx", "gy", None)
    perf = P(("gx", "gy"))
    perf_3 = P(None, ("gx", "gy"))
    segment = P(None, "gy", "gx")
    return jax.shard_map(
        body,
        mesh=mesh,
        in_specs=(stacked, stacked)
        + (cells,) * 5
        + (stacked,)
        + (perf,) * 3
        + (perf_3,) * 2
        + (P("gy", None),)
        + (segment,) * 4,
        out_specs=(stacked, segment),
        check_vma=False,
    )
```
